32 devices in a mesh: section: 2 (over core), dp: 16 (over z, y, x).
Axes of the slice: x: 2, y: 2, z: 4, core: 2. Of those that a mesh axis runs over, the one named last changes fastest.
Arguments:
- tokens: bfloat16 [32, 512, 768], P('dp'), may hold values from -6 to 6
- segment_ids: int32 [32, 512], P('dp'), may hold values from 0 to 7, never falling along the last dimension, each value on 1 to 128 neighbouring positions
- cotangent: bfloat16 [32, 512, 128], P('dp'), may hold values from -48 to 48
- qkv_weight: float32 [2, 768, 2304], P('section', 'dp'), may hold values from -0.21875 to 0.21875
- out_weight: float32 [2, 768, 768], P('section', 'dp'), may hold values from -1.75 to 1.75
- up_weight: float32 [2, 768, 3072], P('section', 'dp'), may hold values from -0.21875 to 0.21875
- down_weight: float32 [2, 3072, 768], P('section', 'dp'), may hold values from -0.109375 to 0.109375
- ln_gains: float32 [2, 2, 768], P('section', None, 'dp'), may hold values from 0.5 to 1.5
- shifts: float32 [2, 6, 768], P('section', None, 'dp'), may hold values from -1.8 to 1.8
- up_bias: float32 [2, 3072], P('section', 'dp'), may hold values from -1.8 to 1.8
- head_weight: float32 [768, 128], P(('section', 'dp')), may hold values from -0.21875 to 0.21875
Outputs:
- qkv_grad: float32 [2, 768, 2304], P('section', 'dp')
- out_grad: float32 [2, 768, 768], P('section', 'dp')
- up_grad: float32 [2, 768, 3072], P('section', 'dp')
- down_grad: float32 [2, 3072, 768], P('section', 'dp')
- gain_grad: float32 [2, 2, 768], P('section', None, 'dp')
- shift_grad: float32 [2, 6, 768], P('section', None, 'dp')
- up_bias_grad: float32 [2, 3072], P('section', 'dp')
- head_grad: float32 [768, 128], P(('section', 'dp'))
- input_grads: float32 [2, 32, 512, 768], P('section', 'dp')
The draws below stay inside these ranges and needn't reach their ends.
Inputs may be any that keep to these rules, and one draw needn't show every extreme that they name: `segment_ids`: along each row the ids never fall; a passage holds 1 to 128 tokens.
All inputs are finite; a program needn't handle non-finite values.
Results may differ from the reference program's by a relative error of at most 0.02.
Values may be sent and summed in bfloat16 or wider, within the bound.
No kernel may reach another device: no remote copies, remote signals or barrier semaphores. Data moves between devices by JAX's collectives and lax.ppermute only.
A program may use at most 256 MiB of HBM per device.

```python
import math
import jax
import jax.numpy as jnp
import numpy as np
from jax import lax

D = 768
HEADS = 12
HDIM = 64
FF = 3072
PROJ = 128
SEQ = 512
NSEG = 8
MOST = 128
LAYERS = 2
ROWS = 32


def strengthened(array, stream_key, source, target, blocks, factor):
    owner, partner = [(jnp.arange(array.shape[axis_at]) // (array.shape[axis_at] // blocks)).reshape([-1 if axis == axis_at else 1 for axis in range(array.ndim)]) for axis_at in (source, target)]
    chosen = jax.random.permutation(stream_key, blocks)[partner]
    strong = (owner == chosen) | (owner == (partner + blocks // 2) % blocks)
    return jnp.where(strong, factor * array, array)


def shard_levels(rng, dims, split, smallest, largest):
    loudness, own = 1.0, jax.random.fold_in(rng, 6)
    for position, parts in split:
        draws = jnp.exp(jax.random.uniform(jax.random.fold_in(own, position), (parts,), jnp.float32, smallest / len(split), largest / len(split)))
        loudness = loudness * jnp.repeat(draws, dims[position] // parts).reshape([-1 if axis == position else 1 for axis in range(len(dims))])
    return loudness


def profile(count, total, reach, slope):
    portions = [(1 << 20) // math.isqrt(standing ** slope) + 1 for standing in range(2, count + 1)]
    spare, holding = total - reach - (count - 1), [1] * (count - 1)
    while spare > 0:
        movable = [i for i in range(count - 1) if holding[i] < reach]
        mass, left = sum([portions[i] for i in movable]), spare
        for i in movable:
            extra = min(reach - holding[i], max(1, left * portions[i] // mass), spare)
            holding[i] = holding[i] + extra
            spare = spare - extra
    return np.array([reach] + holding)


def uneven(key, number_of, total, reach, lean):
    if number_of == 2:
        one = jax.random.randint(key, (), max(1, total - reach), min(reach, total - 1) + 1)
        return jnp.stack([one, total - one])
    sizes = jnp.asarray(profile(number_of, total, reach, lean), jnp.int32)
    twos = (number_of - 1) // 2
    giver, taker = sizes[1:1 + 2 * twos:2], sizes[2:2 + 2 * twos:2]
    room = jnp.minimum(giver - 1, reach - taker)
    passed = jax.random.randint(jax.random.fold_in(key, 1), (twos,), 0, 1 << 20) % (room + 1)
    sizes = sizes.at[1:1 + 2 * twos:2].set(giver - passed).at[2:2 + 2 * twos:2].set(taker + passed)
    return sizes[jax.random.permutation(jax.random.fold_in(key, 2), number_of)]


def normal_values(stream_key, shape, deviation, bound, split=(), kind=jnp.bfloat16):
    level = shard_levels(stream_key, shape, split, -0.22, 0.18) if split else 1.0
    array = jax.random.normal(stream_key, shape, jnp.float32) * deviation * level
    return jnp.minimum(jnp.maximum(array, -bound), bound).astype(kind)


def heavy_noise(stream_key, extent, scale, limit, cuts, heavy, kind=jnp.bfloat16):
    result = scale * jax.random.normal(stream_key, extent, jnp.float32)
    if cuts:
        result = result * shard_levels(stream_key, extent, cuts, -0.22, 0.18)
    return jnp.clip(strengthened(result, jax.random.fold_in(stream_key, 3), *heavy), -limit, limit).astype(kind)


def setup_inputs(seed: int = 0) -> dict:
    streams_of = jax.random.split(jax.random.key(seed), 12)
    tokens = heavy_noise(streams_of[0], (ROWS, SEQ, D), 1.0, 6.0, ((0, 16),), (0, 2, 16, 2.0))
    segment_ids = jax.vmap(lambda own: jnp.searchsorted(jnp.cumsum(uneven(own, NSEG, SEQ, MOST, 2)), jnp.arange(SEQ), side="right"))(jax.random.split(streams_of[1], ROWS)).reshape((ROWS, SEQ)).astype(jnp.int32)
    cotangent = normal_values(streams_of[2], (ROWS, SEQ, PROJ), 8.0, 48.0, ((0, 16),))
    qkv_weight = normal_values(streams_of[3], (LAYERS, D, 3 * D), D ** -0.5, 0.21875, ((0, 2), (1, 16)), jnp.float32)
    out_weight = normal_values(streams_of[4], (LAYERS, D, D), (D // 64) ** -0.5, 1.75, ((0, 2), (1, 16)), jnp.float32)
    up_weight = normal_values(streams_of[5], (LAYERS, D, FF), D ** -0.5, 0.21875, ((0, 2), (1, 16)), jnp.float32)
    down_weight = normal_values(streams_of[6], (LAYERS, FF, D), FF ** -0.5, 0.109375, ((0, 2), (1, 16)), jnp.float32)
    ln_gains = jnp.clip(1.0 + 0.1 * jax.random.normal(streams_of[7], (LAYERS, 2, D), jnp.float32), 0.5, 1.5)
    shifts = normal_values(streams_of[8], (LAYERS, 6, D), 0.3, 1.8, ((0, 2), (2, 16)), jnp.float32)
    up_bias = normal_values(streams_of[9], (LAYERS, FF), 0.3, 1.8, ((0, 2), (1, 16)), jnp.float32)
    head_weight = normal_values(streams_of[10], (D, PROJ), D ** -0.5, 0.21875, ((0, 32),), jnp.float32)
    return dict(tokens=tokens, segment_ids=segment_ids, cotangent=cotangent, qkv_weight=qkv_weight, out_weight=out_weight, up_weight=up_weight, down_weight=down_weight, ln_gains=ln_gains, shifts=shifts, up_bias=up_bias, head_weight=head_weight)


@jax.custom_vjp
def low(v):
    return lax.optimization_barrier(v.astype(jnp.bfloat16)).astype(jnp.float32)

@jax.custom_vjp
def low_back(v):
    return v

def low_keep(v):
    return (low(v), None)

def low_pass(kept, grad):
    return (grad,)

def back_keep(v):
    return (v, None)

def back_low(kept, grad):
    return (low(grad),)
low.defvjp(low_keep, low_pass)
low_back.defvjp(back_keep, back_low)
norm_eps = 1e-06

def matmul(left, right):
    return jnp.dot(left, right, precision=lax.Precision.HIGHEST, preferred_element_type=jnp.float32)

def layer_norm(values, gain, shift):
    center = values - lax.optimization_barrier(jnp.mean(values, axis=-1, keepdims=True))
    spread = lax.optimization_barrier(jnp.mean(center * center, axis=-1, keepdims=True))
    return center * lax.rsqrt(spread + norm_eps) * gain + shift

def attend_row(inputs):
    query, keys, value, seg = inputs
    length = query.shape[0]
    query = query.reshape(length, HEADS, HDIM)
    keys = keys.reshape(length, HEADS, HDIM)
    value = value.reshape(length, HEADS, HDIM)
    scores = jnp.einsum('qhd,khd->hqk', query, keys, precision=lax.Precision.HIGHEST) * HDIM ** (-0.5)
    same = seg[:, None] == seg[None, :]
    scores = low_back(jnp.where(same[None], scores, -1000000000.0))
    probs = jax.nn.softmax(scores, axis=-1)
    mixed = jnp.einsum('hqk,khd->qhd', low(probs), value, precision=lax.Precision.HIGHEST)
    return mixed.reshape(length, HEADS * HDIM)

def encoder_layer(acts, seg, weights):
    w_qkv, w_out, w_up, w_down, gains, shift, up_shift = weights
    width = w_out.shape[0]
    bias = jnp.concatenate([shift[0], jnp.zeros((width,), jnp.float32), shift[1]])
    qkv = low(low_back(matmul(acts, w_qkv) + bias))
    query = qkv[..., :width]
    keys = qkv[..., width:2 * width]
    value = qkv[..., 2 * width:]
    mixed = lax.map(jax.checkpoint(attend_row), (query, keys, value, seg))
    mixed = low(low_back(mixed))
    branch = low_back(matmul(mixed, w_out) + shift[2])
    hidden = layer_norm(acts + branch, gains[0], shift[4])
    upper = low_back(matmul(low(hidden), w_up) + up_shift)
    active = low(jax.nn.gelu(upper, approximate=False))
    second = low_back(matmul(active, w_down) + shift[3])
    return layer_norm(hidden + second, gains[1], shift[5])

def network(params, acts, boundary, seg):
    head = params[-1]
    outcome = acts
    for level in range(LAYERS):
        weights = tuple((low(item[level]) for item in params[:-1]))
        outcome = encoder_layer(acts, seg, weights)
        if level < LAYERS - 1:
            acts = low(low_back(outcome)) + boundary
    proj = low_back(matmul(low(outcome), low(head)))
    return proj * lax.rsqrt(lax.optimization_barrier(jnp.sum(proj * proj, axis=-1, keepdims=True)) + norm_eps)

def reference(tokens, segment_ids, cotangent, qkv_weight, out_weight, up_weight, down_weight, ln_gains, shifts, up_bias, head_weight):
    params = (qkv_weight, out_weight, up_weight, down_weight, ln_gains, shifts, up_bias, head_weight)
    group = math.gcd(ROWS, max(1, 4096 // SEQ))
    count = ROWS // group
    acts_all = tokens.astype(jnp.float32).reshape(count, group, SEQ, D)
    segs_all = segment_ids.reshape(count, group, SEQ)
    cots_all = cotangent.astype(jnp.float32).reshape(count, group, SEQ, PROJ)

    def one_group(totals, items):
        acts, seg, cot = items
        boundary = jnp.zeros_like(acts)
        _, pull = jax.vjp(lambda p, a, b: network(p, a, b, seg), params, acts, boundary)
        grads, first_grad, second_grad = pull(cot)
        totals = jax.tree.map(lambda s, g: s + g, totals, grads)
        return (totals, (first_grad, second_grad))
    start = jax.tree.map(jnp.zeros_like, params)
    totals, (first, second) = lax.scan(one_group, start, (acts_all, segs_all, cots_all))
    input_grads = jnp.stack([first.reshape(ROWS, SEQ, D), second.reshape(ROWS, SEQ, D)])
    return (totals[0], totals[1], totals[2], totals[3], totals[4], totals[5], totals[6], totals[7], input_grads)
```

```python
import jax
import jax.numpy as jnp
from jax import lax
from jax.sharding import PartitionSpec as P

HEADS = 12
HDIM = 64
norm_eps = 1e-06
BF = jnp.bfloat16
F32 = jnp.float32
BOTH = ("section", "dp")
PAD = 16


def layer_norm(values, gain, shift):
    center = values - jnp.mean(values, axis=-1, keepdims=True)
    spread = jnp.mean(center * center, axis=-1, keepdims=True)
    return center * lax.rsqrt(spread + norm_eps) * gain + shift


def unit_norm(proj):
    return proj * lax.rsqrt(jnp.sum(proj * proj, axis=-1, keepdims=True) + norm_eps)


def gelu_exact(values):
    return jax.nn.gelu(values, approximate=False)


def flip(value, mask):
    count = lax.axis_size("dp")
    pairs = [(s * count + i, s * count + (i ^ mask)) for s in range(2) for i in range(count)]
    return lax.ppermute(value, BOTH, pairs)


def swap(value):
    count = lax.axis_size("dp")
    pairs = [(s * count + i, (1 - s) * count + i) for s in range(2) for i in range(count)]
    return lax.ppermute(value, BOTH, pairs)


def gather_chunk(block):
    count = lax.axis_size("dp")
    me = lax.axis_index("dp")
    own = block[None]
    bit = 4
    while bit < count:
        other = flip(own, bit)
        high = (me & bit) != 0
        own = jnp.where(high, jnp.concatenate([other, own]), jnp.concatenate([own, other]))
        bit *= 2
    half = own.shape[0] // 2
    from_x = flip(own, 1)
    from_y = flip(own, 2)
    diag = jnp.concatenate([flip(from_y[:half], 1), flip(from_x[half:], 2)])
    quad = me & 3
    whole = jnp.zeros((4,) + own.shape, own.dtype)
    for rel, part in enumerate((own, from_x, from_y, diag)):
        whole = lax.dynamic_update_index_in_dim(whole, part, quad ^ rel, 0)
    return whole


def scatter_chunk(total):
    count = lax.axis_size("dp")
    me = lax.axis_index("dp")
    quad = me & 3
    part = [lax.dynamic_index_in_dim(total, quad ^ rel, 0, keepdims=False) for rel in range(4)]
    half = total.shape[1] // 2
    by_x = flip(part[3][:half].astype(BF), 1)
    by_y = flip(part[3][half:].astype(BF), 2)
    to_y = jnp.concatenate([part[2][:half] + by_x, part[2][half:]])
    to_x = jnp.concatenate([part[1][:half], part[1][half:] + by_y])
    rest = part[0] + flip(to_x.astype(BF), 1) + flip(to_y.astype(BF), 2)
    bit = count // 2
    while bit >= 4:
        size = rest.shape[0] // 2
        high = (me & bit) != 0
        keep = jnp.where(high, rest[size:], rest[:size])
        send = jnp.where(high, rest[:size], rest[size:])
        rest = keep + flip(send.astype(BF), bit)
        bit //= 2
    return rest[0]


def in_order(whole, first, units):
    quad, outer, rows, width = whole.shape
    size = width // (quad * outer)
    piece = whole[:, :, first * size : (first + units) * size]
    return piece.transpose(1, 0, 2, 3).reshape(quad * outer, units, size, width)


def attend(query, keys, value, same):
    scores = jnp.einsum("qhd,khd->hqk", query, keys, preferred_element_type=F32) * HDIM ** (-0.5)
    probs = jax.nn.softmax(jnp.where(same[None], scores, -1000000000.0), axis=-1)
    mixed = jnp.einsum("hqk,khd->qhd", probs.astype(BF), value, preferred_element_type=F32)
    return mixed, probs


def layer_forward(acts, same, weights):
    wq, wk, wv, wo, w_up, w_down, gains, shift, up_shift = weights
    length, width = acts.shape

    def proj(w, b):
        return (jnp.dot(acts, w, preferred_element_type=F32) + b).astype(BF)

    query = proj(wq, shift[0]).reshape(length, HEADS, HDIM)
    keys = proj(wk, 0.0).reshape(length, HEADS, HDIM)
    value = proj(wv, shift[1]).reshape(length, HEADS, HDIM)
    mixed, probs = attend(query, keys, value, same)
    mixed = mixed.astype(BF).reshape(length, width)
    total = acts.astype(F32) + jnp.dot(mixed, wo, preferred_element_type=F32) + shift[2]
    hidden = layer_norm(total, gains[0], shift[4])
    upper = jnp.dot(hidden.astype(BF), w_up, preferred_element_type=F32) + up_shift
    active = gelu_exact(upper).astype(BF)
    summed = hidden + jnp.dot(active, w_down, preferred_element_type=F32) + shift[3]
    outcome = layer_norm(summed, gains[1], shift[5])
    return outcome, (query, keys, value, probs, mixed, total, hidden, upper, active, summed)


def ffn_backward(weights, d_out, kept):
    wq, wk, wv, wo, w_up, w_down, gains, shift, up_shift = weights
    query, keys, value, probs, mixed, total, hidden, upper, active, summed = kept
    _, pull = jax.vjp(layer_norm, summed, gains[1], shift[5])
    d_sum, d_gain_two, d_shift_five = pull(d_out)
    d_second = d_sum.astype(BF)
    g_down = jnp.einsum("sf,sd->fd", active, d_second, preferred_element_type=F32)
    g_cdown = jnp.sum(d_second.astype(F32), axis=0)
    d_active = jnp.einsum("sd,fd->sf", d_second, w_down, preferred_element_type=F32)
    _, gelu_pull = jax.vjp(gelu_exact, upper)
    d_upper = gelu_pull(d_active)[0].astype(BF)
    g_cup = jnp.sum(d_upper.astype(F32), axis=0)
    g_up = jnp.einsum("sd,sf->df", hidden.astype(BF), d_upper, preferred_element_type=F32)
    d_hidden = d_sum + jnp.einsum("sf,df->sd", d_upper, w_up, preferred_element_type=F32)
    return d_hidden, (g_up, g_down, d_gain_two, d_shift_five, g_cdown, g_cup)


def attention_backward(acts, weights, d_hidden, kept):
    wq, wk, wv, wo, w_up, w_down, gains, shift, up_shift = weights
    query, keys, value, probs, mixed, total, hidden, upper, active, summed = kept
    length, width = acts.shape
    _, pull = jax.vjp(layer_norm, total, gains[0], shift[4])
    d_total, d_gain_one, d_shift_four = pull(d_hidden)
    d_branch = d_total.astype(BF)
    g_out = jnp.einsum("si,sd->id", mixed, d_branch, preferred_element_type=F32)
    g_cout = jnp.sum(d_branch.astype(F32), axis=0)
    d_mixed = jnp.einsum("sd,id->si", d_branch, wo, preferred_element_type=F32)
    d_mixed = d_mixed.astype(BF).reshape(length, HEADS, HDIM)
    d_value = jnp.einsum("hqk,qhd->khd", probs.astype(BF), d_mixed, preferred_element_type=F32)
    d_probs = jnp.einsum("qhd,khd->hqk", d_mixed, value, preferred_element_type=F32)
    d_scores = (probs * (d_probs - jnp.sum(probs * d_probs, axis=-1, keepdims=True))).astype(BF)
    scale = HDIM ** (-0.5)
    d_query = jnp.einsum("hqk,khd->qhd", d_scores, keys, preferred_element_type=F32) * scale
    d_keys = jnp.einsum("hqk,qhd->khd", d_scores, query, preferred_element_type=F32) * scale
    low = [item.astype(BF).reshape(length, width) for item in (d_query, d_keys, d_value)]
    g_q, g_k, g_v = [jnp.einsum("sd,se->de", acts, item, preferred_element_type=F32) for item in low]
    g_bq = jnp.sum(low[0].astype(F32), axis=0)
    g_bv = jnp.sum(low[2].astype(F32), axis=0)
    d_acts = d_total
    for item, w in zip(low, (wq, wk, wv)):
        d_acts = d_acts + jnp.einsum("se,de->sd", item, w, preferred_element_type=F32)
    return d_acts, (g_q, g_k, g_v, g_out, d_gain_one, d_shift_four, g_cout, g_bq, g_bv)


def head_backward(outcome, cot, head):
    low_out = outcome.astype(BF)
    proj = jnp.dot(low_out, head, preferred_element_type=F32)
    _, pull = jax.vjp(unit_norm, proj)
    d_proj = pull(cot.astype(F32))[0].astype(BF)
    grad_head = jnp.einsum("sd,sp->dp", low_out, d_proj, preferred_element_type=F32)
    d_outcome = jnp.einsum("sp,dp->sd", d_proj, head, preferred_element_type=F32)
    return d_outcome, grad_head


def shards(tokens, segment_ids, cotangent, qkv_w, out_w, up_w, down_w, gains_w, shifts_w, up_b, head_w):
    count = lax.axis_size("dp")
    section = lax.axis_index("section")
    first = section == 0
    rows_dev, length, width = tokens.shape
    mine = rows_dev // 2
    size = width // count
    ff = up_w.shape[2]
    ups = ff // width

    def cols(array, n):
        return [array[:, j * width : (j + 1) * width] for j in range(n)]

    q_u, k_u, v_u = cols(qkv_w[0].astype(BF), 3)
    up_u = cols(up_w[0].astype(BF), ups)
    plane = (
        jnp.concatenate([q_u, k_u] + up_u),
        jnp.concatenate([v_u, out_w[0].astype(BF), down_w[0].astype(BF)]),
    )
    got = swap(jnp.where(first, plane[1], plane[0]))
    zero = jnp.where(first, plane[0], got)
    one = jnp.where(first, got, plane[1])
    small = jnp.concatenate([gains_w.reshape(-1), shifts_w.reshape(-1), up_b.reshape(-1)]).astype(BF)
    small_n = small.shape[0]
    small_rows = -(-small_n // width)
    head_n = head_w.shape[0] * head_w.shape[1]
    head_rows = -(-head_n // width)
    pad_rows = -(-(small_rows + head_rows) // PAD) * PAD

    def to_rows(flat, rows):
        return jnp.pad(flat, (0, rows * width - flat.shape[0])).reshape(rows, width)

    extra = jnp.concatenate(
        [
            to_rows(small, small_rows),
            to_rows(head_w.astype(BF).reshape(-1), head_rows),
            jnp.zeros((pad_rows - small_rows - head_rows, width), BF),
        ]
    )
    parts = [
        jnp.concatenate([zero[: 2 * size], extra]),
        zero[2 * size :],
        one[: 2 * size],
        one[2 * size :],
    ]
    planes = []
    for item in parts:
        whole = gather_chunk(item)
        other = swap(whole)
        planes.append((jnp.where(first, whole, other), jnp.where(first, other, whole)))

    smalls = []
    heads = []
    for item in planes[0]:
        tail = item[:, :, 2 * size :].transpose(1, 0, 2, 3).reshape(count, pad_rows, width)
        flat = tail[:, :small_rows].reshape(count, -1)[:, :small_n].astype(F32)
        n_g = gains_w.shape[1] * size
        n_s = shifts_w.shape[1] * size
        gains = flat[:, :n_g].reshape(count, -1, size).transpose(1, 0, 2).reshape(-1, width)
        shift = flat[:, n_g : n_g + n_s].reshape(count, -1, size).transpose(1, 0, 2).reshape(-1, width)
        cup = flat[:, n_g + n_s :].reshape(-1)
        smalls.append((gains, shift, cup))
        block = tail[:, small_rows : small_rows + head_rows].reshape(count, -1)[:, :head_n]
        heads.append(block.reshape(count * head_w.shape[0], head_w.shape[1]))
    head = jnp.concatenate(heads)

    def layer_weights(level):
        attn, ffn = planes[2 * level], planes[2 * level + 1]
        wq, wk = [in_order(attn[0], j, 1).reshape(width, width) for j in range(2)]
        wv, wo = [in_order(attn[1], j, 1).reshape(width, width) for j in range(2)]
        w_up = in_order(ffn[0], 0, ups).transpose(0, 2, 1, 3).reshape(width, ff)
        w_down = in_order(ffn[1], 0, ups).reshape(ff, width)
        return (wq, wk, wv, wo, w_up, w_down) + smalls[level]

    weights = [layer_weights(level) for level in range(2)]
    own = lax.dynamic_slice_in_dim(tokens, section * mine, mine, 0)
    seg = lax.dynamic_slice_in_dim(segment_ids, section * mine, mine, 0)
    cot = lax.dynamic_slice_in_dim(cotangent, section * mine, mine, 0)
    add = lambda old, new: new if old is None else jax.tree.map(jnp.add, old, new)
    acc = {}
    first_in, second_in = [], []
    for row in range(mine):
        same = seg[row][:, None] == seg[row][None, :]
        a0 = own[row]
        y0, kept0 = layer_forward(a0, same, weights[0])
        a1 = y0.astype(BF)
        y1, kept1 = layer_forward(a1, same, weights[1])
        d_y1, g_head = head_backward(y1, cot[row], head)
        d_h, ffn1 = ffn_backward(weights[1], d_y1, kept1)
        d_a1, att1 = attention_backward(a1, weights[1], d_h, kept1)
        d_h, ffn0 = ffn_backward(weights[0], d_a1.astype(BF).astype(F32), kept0)
        d_a0, att0 = attention_backward(a0, weights[0], d_h, kept0)
        acc = add(acc or None, dict(head=g_head, ffn1=ffn1, att1=att1, ffn0=ffn0, att0=att0))
        first_in.append(d_a0)
        second_in.append(d_a1)

    def to_units(grad, units):
        block = grad.reshape(count // 4, 4, size, units, width).transpose(1, 0, 3, 2, 4)
        return block.reshape(4, count // 4, units * size, width)

    def by_chip(grad):
        block = grad.reshape(count // 4, 4, -1, width)
        return block.transpose(1, 0, 2, 3)

    def reduce(zero_plane, one_plane):
        keep = jnp.where(first, zero_plane, one_plane)
        send = jnp.where(first, one_plane, zero_plane)
        return scatter_chunk(keep + swap(send.astype(BF)).astype(F32))

    def ffn_chunk(grads):
        g_up, g_down = grads[:2]
        return reduce(to_units(g_up, ups), by_chip(g_down))

    def attn_planes(grads):
        return (
            jnp.concatenate([to_units(item, 1) for item in grads[:2]], axis=2),
            jnp.concatenate([to_units(item, 1) for item in grads[2:4]], axis=2),
        )

    def small_block(att, ffn, head_part):
        g_q, g_k, g_v, g_out, d_gain_one, d_shift_four, g_cout, g_bq, g_bv = att
        g_up, g_down, d_gain_two, d_shift_five, g_cdown, g_cup = ffn
        gains = jnp.stack([d_gain_one, d_gain_two]).reshape(2, count, size).transpose(1, 0, 2)
        shift = jnp.stack([g_bq, g_bv, g_cout, g_cdown, d_shift_four, d_shift_five])
        shift = shift.reshape(6, count, size).transpose(1, 0, 2)
        flat = jnp.concatenate(
            [gains.reshape(count, -1), shift.reshape(count, -1), g_cup.reshape(count, -1)], axis=1
        )
        flat = jnp.pad(flat, ((0, 0), (0, small_rows * width - small_n)))
        piece = jnp.pad(head_part.reshape(count, -1), ((0, 0), (0, head_rows * width - head_n)))
        block = jnp.concatenate(
            [
                flat.reshape(count, small_rows, width),
                piece.reshape(count, head_rows, width),
                jnp.zeros((count, pad_rows - small_rows - head_rows, width), F32),
            ],
            axis=1,
        )
        return by_chip(block)

    done_ffn1 = ffn_chunk(acc["ffn1"])
    done_att1 = reduce(*attn_planes(acc["att1"]))
    done_ffn0 = ffn_chunk(acc["ffn0"])
    half_head = acc["head"].reshape(2, -1, head_w.shape[1])
    last = attn_planes(acc["att0"])
    last = (
        jnp.concatenate([last[0], small_block(acc["att0"], acc["ffn0"], half_head[0])], axis=2),
        jnp.concatenate([last[1], small_block(acc["att1"], acc["ffn1"], half_head[1])], axis=2),
    )
    done_att0 = reduce(*last)

    cut = 2 * size
    sums_zero = jnp.concatenate([done_att0[:cut], done_ffn0])
    sums_one = jnp.concatenate([done_att1, done_ffn1])
    other = swap(jnp.where(first, sums_one, sums_zero))
    low_plane = jnp.where(first, sums_zero, other)
    high_plane = jnp.where(first, other, sums_one)

    def unit(array, j):
        return array[j * size : (j + 1) * size]

    qkv_grad = jnp.concatenate([unit(low_plane, 0), unit(low_plane, 1), unit(high_plane, 0)], axis=1)
    out_grad = unit(high_plane, 1)
    up_grad = jnp.concatenate([unit(low_plane, 2 + j) for j in range(ups)], axis=1)
    down_grad = high_plane[cut:]
    tail = done_att0[cut:]
    flat = tail[:small_rows].reshape(-1)[:small_n]
    n_g = gains_w.shape[1] * size
    n_s = shifts_w.shape[1] * size
    gain_grad = flat[:n_g].reshape(gains_w.shape)
    shift_grad = flat[n_g : n_g + n_s].reshape(shifts_w.shape)
    cup_grad = flat[n_g + n_s :].reshape(up_b.shape)
    head_grad = tail[small_rows : small_rows + head_rows].reshape(-1)[:head_n].reshape(head_w.shape)

    d_first, d_second = jnp.stack(first_in), jnp.stack(second_in)
    got = swap(jnp.where(first, d_second, d_first))
    keep = jnp.where(first, d_first, d_second)
    input_grads = jnp.where(first, jnp.concatenate([keep, got]), jnp.concatenate([got, keep]))
    return (
        qkv_grad[None],
        out_grad[None],
        up_grad[None],
        down_grad[None],
        gain_grad,
        shift_grad,
        cup_grad,
        head_grad,
        input_grads[None],
    )


def solution(mesh):
    return jax.shard_map(
        shards,
        mesh=mesh,
        in_specs=(
            P("dp", None, None),
            P("dp", None),
            P("dp", None, None),
            P("section", "dp", None),
            P("section", "dp", None),
            P("section", "dp", None),
            P("section", "dp", None),
            P("section", None, "dp"),
            P("section", None, "dp"),
            P("section", "dp"),
            P(("section", "dp"), None),
        ),
        out_specs=(
            P("section", "dp", None),
            P("section", "dp", None),
            P("section", "dp", None),
            P("section", "dp", None),
            P("section", None, "dp"),
            P("section", None, "dp"),
            P("section", "dp"),
            P(("section", "dp"), None),
            P("section", "dp", None, None),
        ),
        check_vma=False,
    )
```

```python
import jax
import jax.numpy as jnp
from jax import lax
from jax.experimental import pallas as pl
from jax.experimental.pallas import tpu as pltpu
from jax.sharding import PartitionSpec as P

HEADS = 12
HDIM = 64
GROUP = 4
BLOCK = 128
PAD = 16
norm_eps = 1e-06
BF = jnp.bfloat16
F32 = jnp.float32
BOTH = ("section", "dp")
SCALE = HDIM ** (-0.5)

ERF_SCALE = 0.425
ERF_POLY = (
    0.11985147519825406,
    0.12072713574380309,
    0.10159474513684189,
    0.12334456743816431,
    -0.0435293372534038,
    0.19486821903107854,
    -0.15132025578595443,
    0.03446332841595847,
)


def dot(left, right, over_left=1, over_right=0):
    return lax.dot_general(
        left, right, (((over_left,), (over_right,)), ((), ())), preferred_element_type=F32
    )


def shape_of(shape, dtype):
    return jax.ShapeDtypeStruct(shape, dtype)


def whole_block(*shape):
    return pl.BlockSpec(shape, lambda g: (0,) * len(shape))


def gelu_pair(u):
    bell = jnp.exp(u * u * -0.5)
    t = 1.0 / (1.0 + (ERF_SCALE * 0.7071067811865476) * jnp.abs(u))
    poly = ERF_POLY[-1]
    for item in ERF_POLY[-2::-1]:
        poly = poly * t + item
    tail = bell * (poly * t)
    cdf = jnp.where(u < 0.0, tail, 1.0 - tail)
    return u * cdf, cdf + u * bell * 0.3989422804014327


def norm_stats(v):
    center = v - jnp.mean(v, axis=-1, keepdims=True)
    t = lax.rsqrt(jnp.mean(center * center, axis=-1, keepdims=True) + norm_eps)
    return center * t, t


def norm_back(dy, n, t, gain):
    dn = dy * gain
    mean = jnp.mean(dn, axis=-1, keepdims=True)
    along = jnp.mean(dn * n, axis=-1, keepdims=True)
    return t * (dn - mean - n * along)


def colsum(v):
    return jnp.sum(v, axis=0, keepdims=True)


def near(b, blocks):
    return max(0, b - 1) * BLOCK, min(blocks, b + 2) * BLOCK


def attn_fwd_kernel(
    a_ref, sq_ref, sk_ref, wq_ref, wk_ref, wv_ref, wo_ref, bias_ref, shift_ref,
    q_ref, k_ref, v_ref, o_ref, n_ref, t_ref, acc,
):
    step = pl.program_id(0)
    blocks = a_ref.shape[0] // BLOCK
    a = a_ref[...]
    q_ref[...] = (dot(a, wq_ref[0]) + bias_ref[0:1]).astype(BF)
    k_ref[...] = dot(a, wk_ref[0]).astype(BF)
    v_ref[...] = (dot(a, wv_ref[0]) + bias_ref[1:2]).astype(BF)
    lane = lax.broadcasted_iota(jnp.int32, (BLOCK, 2 * HDIM), 1)
    for b in range(blocks):
        lo, hi = near(b, blocks)
        rows = slice(b * BLOCK, (b + 1) * BLOCK)
        same = sq_ref[rows, 0:1] == sk_ref[0:1, lo:hi]
        for pair in range(GROUP // 2):
            lanes = slice(pair * 2 * HDIM, (pair + 1) * 2 * HDIM)
            query = q_ref[rows, lanes]
            keys = k_ref[lo:hi, lanes]
            value = v_ref[lo:hi, lanes]
            out = []
            for mine in (lane < HDIM, lane >= HDIM):
                scores = dot(jnp.where(mine, query, jnp.zeros_like(query)), keys, 1, 1) * SCALE
                scores = jnp.where(same, scores, -1000000000.0)
                grown = jnp.exp(scores - jnp.max(scores, axis=-1, keepdims=True))
                probs = grown * (1.0 / jnp.sum(grown, axis=-1, keepdims=True))
                out.append(dot(probs.astype(BF), value))
            o_ref[rows, lanes] = jnp.where(lane < HDIM, out[0], out[1]).astype(BF)
    part = dot(o_ref[...], wo_ref[0])

    @pl.when(step == 0)
    def _():
        acc[...] = a.astype(F32) + shift_ref[2:3] + part

    @pl.when(step != 0)
    def _():
        acc[...] += part

    @pl.when(step == pl.num_programs(0) - 1)
    def _():
        n, t = norm_stats(acc[...])
        n_ref[...] = n
        t_ref[...] = jnp.broadcast_to(t, t_ref.shape)


def attn_weight_blocks(width, cols):
    def column(j):
        return pl.BlockSpec((1, width, cols), lambda g: (j, 0, g))

    return [column(0), column(1), column(2), pl.BlockSpec((1, cols, width), lambda g: (3, g, 0))]


def attn_fwd(a, seg_col, seg_row, w4, shift):
    length, width = a.shape
    cols = GROUP * HDIM
    group = pl.BlockSpec((length, cols), lambda g: (0, g))
    return pl.pallas_call(
        attn_fwd_kernel,
        grid=(HEADS // GROUP,),
        in_specs=[whole_block(length, width), whole_block(length, 128), whole_block(8, length)]
        + attn_weight_blocks(width, cols)
        + [pl.BlockSpec((8, cols), lambda g: (0, g)), whole_block(8, width)],
        out_specs=[group] * 4 + [whole_block(length, width), whole_block(length, 128)],
        out_shape=[shape_of((length, width), BF)] * 4
        + [shape_of((length, width), F32), shape_of((length, 128), F32)],
        scratch_shapes=[pltpu.VMEM((length, width), F32)],
        name="attn_fwd",
    )(a, seg_col, seg_row, w4, w4, w4, w4, shift, shift)


def ffn_fwd_kernel(
    n1_ref, up_ref, cup_ref, down_ref, gain_ref, shift_ref,
    g_ref, gp_ref, n_ref, t_ref, y_ref, h1, acc,
):
    step = pl.program_id(0)
    half = n1_ref.shape[0] // 2

    @pl.when(step == 0)
    def _():
        hidden = n1_ref[...] * gain_ref[0:1] + shift_ref[4:5]
        h1[...] = hidden.astype(BF)
        acc[...] = hidden + shift_ref[3:4]

    for r in range(2):
        rows = slice(r * half, (r + 1) * half)
        g, slope = gelu_pair(dot(h1[rows], up_ref[0]) + cup_ref[0])
        g = g.astype(BF)
        g_ref[rows] = g
        gp_ref[rows] = slope.astype(BF)
        acc[rows] += dot(g, down_ref[...])

    @pl.when(step == pl.num_programs(0) - 1)
    def _():
        n, t = norm_stats(acc[...])
        n_ref[...] = n
        t_ref[...] = jnp.broadcast_to(t, t_ref.shape)
        y_ref[...] = (n * gain_ref[1:2] + shift_ref[5:6]).astype(BF)


def ffn_fwd(n1, up, cup, down, gain, shift):
    length, width = n1.shape
    units = up.shape[0]
    column = pl.BlockSpec((length, width), lambda g: (0, g))
    return pl.pallas_call(
        ffn_fwd_kernel,
        grid=(units,),
        in_specs=[
            whole_block(length, width),
            pl.BlockSpec((1, width, width), lambda g: (g, 0, 0)),
            pl.BlockSpec((1, 1, width), lambda g: (g, 0, 0)),
            pl.BlockSpec((width, width), lambda g: (g, 0)),
            whole_block(8, width),
            whole_block(8, width),
        ],
        out_specs=[column, column, whole_block(length, width), whole_block(length, 128), whole_block(length, width)],
        out_shape=[shape_of((length, units * width), BF)] * 2
        + [shape_of((length, width), F32), shape_of((length, 128), F32), shape_of((length, width), BF)],
        scratch_shapes=[pltpu.VMEM((length, width), BF), pltpu.VMEM((length, width), F32)],
        name="ffn_fwd",
    )(n1, up, cup.reshape(units, 1, width), down, gain, shift)


def by_section(section, action):
    for plane in range(2):
        pl.when(section == plane)(lambda plane=plane: action(plane))


def copy_all(copies, start):
    for item in copies:
        if start:
            item.start()
        else:
            item.wait()


def ffn_bwd_kernel(
    place_ref, dy_ref, n2_ref, t2_ref, g_ref, gp_ref, up_ref, down_ref, n1_ref, t1_ref, gain_ref, shift_ref,
    keep_ref, send_ref, dr1_ref, sums_ref, cup_ref, h1, df, acc, gup, gdown, sem,
):
    step = pl.program_id(0)
    last = pl.num_programs(0) - 1
    quads = keep_ref.shape[0]
    outer = keep_ref.shape[1]
    width = h1.shape[1]
    size = width // (quads * outer)

    @pl.when(step == 0)
    def _():
        n2 = n2_ref[...]
        dy = dy_ref[...].astype(F32)
        dr2 = norm_back(dy, n2, t2_ref[:, 0:1], gain_ref[1:2])
        low = dr2.astype(BF)
        df[...] = low
        acc[...] = dr2
        h1[...] = (n1_ref[...] * gain_ref[0:1] + shift_ref[4:5]).astype(BF)
        sums_ref[...] = jnp.zeros_like(sums_ref)
        sums_ref[1:2] = colsum(dy * n2)
        sums_ref[2:3] = colsum(dy)
        sums_ref[3:4] = colsum(low.astype(F32))

    d = df[...]
    down = dot(g_ref[...], d, 0, 0).astype(BF)
    gdown[step] = down.reshape(quads, width // quads, width)
    du = (dot(d, down_ref[...], 1, 1) * gp_ref[...].astype(F32)).astype(BF)
    cup_ref[0] = colsum(du.astype(F32))
    up = dot(h1[...], du, 0, 0).astype(BF)
    gup[step] = up.reshape(outer, quads, size, width)
    acc[...] += dot(du, up_ref[0], 1, 1)

    def copies(j, plane):
        up_to, down_to = (keep_ref, send_ref) if plane == 0 else (send_ref, keep_ref)
        out = []
        for q in range(quads):
            rel = q ^ place_ref[0]
            out.append(
                pltpu.make_async_copy(
                    gup.at[j, :, q], up_to.at[rel, :, j * size : (j + 1) * size, :], sem.at[j, 0, q]
                )
            )
            out.append(pltpu.make_async_copy(gdown.at[j, q], down_to.at[rel, j], sem.at[j, 1, q]))
        return out

    for j in range(gup.shape[0]):
        @pl.when(step == j)
        def _(j=j):
            by_section(place_ref[1], lambda plane: copy_all(copies(j, plane), True))

    @pl.when(step == last)
    def _():
        dh = acc[...]
        n1 = n1_ref[...]
        dr1_ref[...] = norm_back(dh, n1, t1_ref[:, 0:1], gain_ref[0:1])
        sums_ref[0:1] = colsum(dh * n1)
        sums_ref[4:5] = colsum(dh)

        def finish(plane):
            for j in range(gup.shape[0]):
                copy_all(copies(j, plane), False)

        by_section(place_ref[1], finish)


def ffn_bwd(place, outer, dy, n2, t2, g, gp, up, down, n1, t1, gain, shift):
    length, width = n1.shape
    units = up.shape[0]
    size = width // (4 * outer)
    column = pl.BlockSpec((length, width), lambda g: (0, g))
    chunk = shape_of((4, outer, units * size, width), BF)
    return pl.pallas_call(
        ffn_bwd_kernel,
        grid=(units,),
        in_specs=[
            pl.BlockSpec(memory_space=pltpu.SMEM),
            whole_block(length, width),
            whole_block(length, width),
            whole_block(length, 128),
            column,
            column,
            pl.BlockSpec((1, width, width), lambda g: (g, 0, 0)),
            pl.BlockSpec((width, width), lambda g: (g, 0)),
            whole_block(length, width),
            whole_block(length, 128),
            whole_block(8, width),
            whole_block(8, width),
        ],
        out_specs=[
            pl.BlockSpec(memory_space=pl.ANY),
            pl.BlockSpec(memory_space=pl.ANY),
            whole_block(length, width),
            whole_block(8, width),
            pl.BlockSpec((1, 1, width), lambda g: (g, 0, 0)),
        ],
        out_shape=[chunk, chunk, shape_of((length, width), F32), shape_of((8, width), F32), shape_of((units, 1, width), F32)],
        scratch_shapes=[
            pltpu.VMEM((length, width), BF),
            pltpu.VMEM((length, width), BF),
            pltpu.VMEM((length, width), F32),
            pltpu.VMEM((units, outer, 4, size, width), BF),
            pltpu.VMEM((units, 4, width // 4, width), BF),
            pltpu.SemaphoreType.DMA((units, 2, 4)),
        ],
        name="ffn_bwd",
    )(place, dy, n2, t2, g, gp, up, down, n1, t1, gain, shift)


def attn_bwd_kernel(
    place_ref, dr_ref, a_ref, sq_ref, sk_ref, q_ref, k_ref, v_ref, o_ref, wq_ref, wk_ref, wv_ref, wo_ref,
    keep_ref, send_ref, da_ref, sums_ref, sumo_ref, dat, do_sc, dq, dk, dv, grads, sem,
):
    step = pl.program_id(0)
    length, width = a_ref.shape
    blocks = length // BLOCK
    quads = keep_ref.shape[0]
    outer = keep_ref.shape[1]
    size = width // (quads * outer)
    cols = GROUP * HDIM

    @pl.when(step == 0)
    def _():
        low = dr_ref[...].astype(BF)
        dat[...] = low
        da_ref[...] = dr_ref[...]
        sumo_ref[...] = jnp.zeros_like(sumo_ref)
        sumo_ref[0:1] = colsum(low.astype(F32))

    d = dat[...]
    grad_o = dot(o_ref[...], d, 0, 0).astype(BF)
    do_sc[...] = dot(d, wo_ref[0], 1, 1).astype(BF)
    dk[...] = jnp.zeros_like(dk)
    dv[...] = jnp.zeros_like(dv)
    lane = lax.broadcasted_iota(jnp.int32, (BLOCK, 2 * HDIM), 1)
    for b in range(blocks):
        lo, hi = near(b, blocks)
        rows = slice(b * BLOCK, (b + 1) * BLOCK)
        same = sk_ref[lo:hi, 0:1] == sq_ref[0:1, rows]
        for pair in range(GROUP // 2):
            lanes = slice(pair * 2 * HDIM, (pair + 1) * 2 * HDIM)
            query = q_ref[rows, lanes]
            d_out = do_sc[rows, lanes]
            keys = k_ref[lo:hi, lanes]
            value = v_ref[lo:hi, lanes]
            dqs, dks, dvs = [], [], []
            for mine in (lane < HDIM, lane >= HDIM):
                q_head = jnp.where(mine, query, jnp.zeros_like(query))
                do_head = jnp.where(mine, d_out, jnp.zeros_like(d_out))
                scores = jnp.where(same, dot(keys, q_head, 1, 1) * SCALE, -1000000000.0)
                grown = jnp.exp(scores - jnp.max(scores, axis=0, keepdims=True))
                probs = grown * (1.0 / jnp.sum(grown, axis=0, keepdims=True))
                d_probs = dot(value, do_head, 1, 1)
                d_scores = probs * (d_probs - jnp.sum(probs * d_probs, axis=0, keepdims=True))
                d_scores = d_scores.astype(BF)
                dvs.append(dot(probs.astype(BF), do_head))
                dks.append(dot(d_scores, q_head))
                dqs.append(dot(d_scores, keys, 0, 0))
            dq[rows, lanes] = jnp.where(lane < HDIM, dqs[0], dqs[1]) * SCALE
            dv[lo:hi, lanes] += dvs[0] + dvs[1]
            dk[lo:hi, lanes] += dks[0] + dks[1]
    a = a_ref[...]
    out = da_ref[...]
    lows = (dq[...].astype(BF), (dk[...] * SCALE).astype(BF), dv[...].astype(BF))
    made = []
    for low, w_ref in zip(lows, (wq_ref, wk_ref, wv_ref)):
        made.append(dot(a, low, 0, 0).astype(BF))
        out = out + dot(low, w_ref[0], 1, 1)
    da_ref[...] = out
    sums_ref[...] = jnp.zeros_like(sums_ref)
    sums_ref[0:1] = colsum(lows[0].astype(F32))
    sums_ref[1:2] = colsum(lows[2].astype(F32))
    steps = HEADS // GROUP
    for j in range(steps):
        @pl.when(step == j)
        def _(j=j):
            here = slice(j * cols, (j + 1) * cols)
            for unit in range(3):
                grads[unit, :, here] = made[unit]
            grads[3, here, :] = grad_o

    @pl.when(step == steps - 1)
    def _():
        def copies(plane):
            out = []
            for unit in range(4):
                to = keep_ref if unit // 2 == plane else send_ref
                at = (unit % 2) * size
                for block in range(quads * outer):
                    rel = (block % quads) ^ place_ref[0]
                    out.append(
                        pltpu.make_async_copy(
                            grads.at[unit, block * size : (block + 1) * size, :],
                            to.at[rel, block // quads, at : at + size, :],
                            sem.at[unit, block],
                        )
                    )
            return out

        def move(plane):
            items = copies(plane)
            copy_all(items, True)
            copy_all(items, False)

        by_section(place_ref[1], move)


def attn_bwd(place, outer, dr, a, seg_col, seg_row, q, k, v, o, w4):
    length, width = a.shape
    size = width // (4 * outer)
    cols = GROUP * HDIM
    group = pl.BlockSpec((length, cols), lambda g: (0, g))
    chunk = shape_of((4, outer, 2 * size, width), BF)
    return pl.pallas_call(
        attn_bwd_kernel,
        grid=(HEADS // GROUP,),
        in_specs=[
            pl.BlockSpec(memory_space=pltpu.SMEM),
            whole_block(length, width),
            whole_block(length, width),
            whole_block(8, length),
            whole_block(length, 128),
        ]
        + [group] * 4
        + attn_weight_blocks(width, cols),
        out_specs=[
            pl.BlockSpec(memory_space=pl.ANY),
            pl.BlockSpec(memory_space=pl.ANY),
            whole_block(length, width),
            pl.BlockSpec((8, cols), lambda g: (0, g)),
            whole_block(8, width),
        ],
        out_shape=[chunk, chunk, shape_of((length, width), F32), shape_of((8, width), F32), shape_of((8, width), F32)],
        scratch_shapes=[pltpu.VMEM((length, width), BF), pltpu.VMEM((length, cols), BF)]
        + [pltpu.VMEM((length, cols), F32)] * 3
        + [pltpu.VMEM((4, width, width), BF), pltpu.SemaphoreType.DMA((4, 4 * outer))],
        name="attn_bwd",
    )(place, dr, a, seg_row, seg_col, q, k, v, o, w4, w4, w4, w4)


def flip(value, mask):
    count = lax.axis_size("dp")
    pairs = [(s * count + i, s * count + (i ^ mask)) for s in range(2) for i in range(count)]
    return lax.ppermute(value, BOTH, pairs)


def swap(value):
    count = lax.axis_size("dp")
    pairs = [(s * count + i, (1 - s) * count + i) for s in range(2) for i in range(count)]
    return lax.ppermute(value, BOTH, pairs)


def after(values, *done):
    leaves, tree = jax.tree.flatten(values)
    return jax.tree.unflatten(tree, lax.optimization_barrier((*leaves, *done))[: len(leaves)])


def double(own, bit):
    other = flip(own, bit)
    high = (lax.axis_index("dp") & bit) != 0
    return jnp.where(high, jnp.concatenate([other, own]), jnp.concatenate([own, other]))


def outer_first(block):
    own, bit = block[None], 4
    while bit < lax.axis_size("dp") // 2:
        own = double(own, bit)
        bit *= 2
    return own


def outer_last(own):
    return double(own, lax.axis_size("dp") // 2)


def near_quad(own):
    return flip(own, 1), flip(own, 2)


def far_quad(from_x, from_y):
    half = from_x.shape[0] // 2
    return flip(from_y[:half], 1), flip(from_x[half:], 2)


def spread(own, quads):
    (from_x, from_y), (diag_low, diag_high) = quads
    half = own.shape[0] // 2
    return ((own, 0, 0), (from_x, 0, 1), (from_y, 0, 2), (diag_low, 0, 3), (diag_high, half, 3))


def assemble_kernel(attn, units, size, layout, place_ref, *refs):
    pieces = len(layout)
    mine, other = refs[:pieces], refs[pieces : 2 * pieces]
    outs, sem = refs[2 * pieces : -1], refs[-1]

    def copies(plane):
        out = []
        count = 0
        for which, group in ((plane, mine), (1 - plane, other)):
            for (outer, start, rel), ref in zip(layout, group):
                q = rel ^ place_ref[0]
                span = slice(start, start + outer)
                if attn:
                    moves = [
                        (ref.at[:, u * size : (u + 1) * size, :], outs[0].at[2 * which + u, span, q])
                        for u in range(2)
                    ]
                elif which == 0:
                    moves = [
                        (ref.at[:, u * size : (u + 1) * size, :], outs[0].at[u, span, q]) for u in range(units)
                    ]
                else:
                    moves = [(ref, outs[1].at[span, q])]
                for source, target in moves:
                    out.append(pltpu.make_async_copy(source, target, sem.at[count]))
                    count += 1
        return out

    def move(plane):
        items = copies(plane)
        copy_all(items, True)
        copy_all(items, False)

    by_section(place_ref[1], move)


def assemble(attn, place, units, size, own_quads, other_quads):
    own, other = spread(*own_quads), spread(*other_quads)
    layout = tuple((piece.shape[0], start, rel) for piece, start, rel in own)
    outer, _, width = own[0][0].shape
    if size % PAD == 0:
        if attn:
            shapes = [(4, outer, 4, size, width)]
        else:
            shapes = [(units, outer, 4, size, width), (outer, 4, units * size, width)]
        anywhere = pl.BlockSpec(memory_space=pl.ANY)
        outs = pl.pallas_call(
            lambda *refs: assemble_kernel(attn, units, size, layout, *refs),
            in_specs=[pl.BlockSpec(memory_space=pltpu.SMEM)] + [anywhere] * (2 * len(layout)),
            out_specs=[pl.BlockSpec(memory_space=pltpu.VMEM)] * len(shapes),
            out_shape=[shape_of(shape, BF) for shape in shapes],
            scratch_shapes=[pltpu.SemaphoreType.DMA((2 * len(layout) * units,))],
            name="assemble",
        )(place, *[piece for piece, _, _ in own], *[piece for piece, _, _ in other])
    else:
        planes = []
        for pieces in (own, other):
            whole = jnp.zeros((outer, 4) + own[0][0].shape[1:], BF)
            for piece, start, rel in pieces:
                whole = lax.dynamic_update_slice(whole, piece[:, None], (start, place[0] ^ rel, 0, 0))
            planes.append(whole.reshape(4 * outer, -1, width))
        first = place[1] == 0
        low = jnp.where(first, planes[0], planes[1])
        high = jnp.where(first, planes[1], planes[0])

        def unit(array, j):
            return array[:, j * size : (j + 1) * size].reshape(width, width)

        if attn:
            outs = [jnp.stack([unit(low, 0), unit(low, 1), unit(high, 0), unit(high, 1)])]
        else:
            outs = [jnp.stack([unit(low, j) for j in range(units)]), high]
    if attn:
        return outs[0].reshape(4, width, width)
    return outs[0].reshape(units, width, width), outs[1].reshape(units * width, width)


def in_chips(chunk, place, units, count):
    if count == 16:
        return chunk
    quads, outer, rows, width = chunk.shape
    size = width // count
    natural = chunk.reshape(quads, outer, units, -1, width).transpose(2, 1, 0, 3, 4)
    block = natural.reshape(units, count // 4, 4, size, width).transpose(2, 1, 0, 3, 4)
    return relative(block.reshape(4, count // 4, units * size, width), place)


def down_in_chips(chunk, place, count):
    if count == 16:
        return chunk
    width = chunk.shape[3]
    natural = chunk.transpose(1, 0, 2, 3).reshape(count // 4, 4, -1, width)
    return relative(natural.transpose(1, 0, 2, 3), place)


def relative(block, place):
    return jnp.stack([lax.dynamic_index_in_dim(block, place[0] ^ rel, 0, False) for rel in range(4)])


def low(value):
    return value.astype(BF)


class Reduce:
    def __init__(self, keep, send):
        self.keep, self.got = keep, swap(send)

    def part(self, rel, span=slice(None)):
        return self.keep[rel, span].astype(F32) + self.got[rel, span].astype(F32)

    def start_far(self):
        half = self.keep.shape[1] // 2
        self.halves = (slice(0, half), slice(half, None))
        self.far = [low(self.part(3, span)) for span in self.halves]
        self.by = [flip(item, mask) for item, mask in zip(self.far, (1, 2))]
        return self.far

    def start_near(self):
        first, second = self.halves
        to_y = jnp.concatenate([low(self.part(2, first) + self.by[0]), low(self.part(2, second))])
        to_x = jnp.concatenate([low(self.part(1, first)), low(self.part(1, second) + self.by[1])])
        self.near = [to_x, to_y]
        self.quad = [flip(to_x, 1), flip(to_y, 2)]
        return self.near

    def start_outer(self):
        rest = self.part(0) + self.quad[0].astype(F32) + self.quad[1].astype(F32)
        self.bit = lax.axis_size("dp") // 2
        return self.halve(rest)

    def halve(self, rest):
        size = rest.shape[0] // 2
        high = (lax.axis_index("dp") & self.bit) != 0
        self.rest = jnp.where(high, rest[size:], rest[:size])
        sent = low(jnp.where(high, rest[:size], rest[size:]))
        self.there = flip(sent, self.bit)
        return [sent]

    def next_outer(self):
        self.bit //= 2
        return self.halve(self.rest + self.there.astype(F32))

    def finish(self):
        while self.bit > 4:
            self.next_outer()
        return (self.rest + self.there.astype(F32))[0]


def shards(tokens, segment_ids, cotangent, qkv_w, out_w, up_w, down_w, gains_w, shifts_w, up_b, head_w):
    count = lax.axis_size("dp")
    section = lax.axis_index("section")
    me = lax.axis_index("dp")
    first = section == 0
    place = jnp.stack([me & 3, section]).astype(jnp.int32)
    grad_place = place if count == 16 else jnp.stack([jnp.zeros_like(section), section]).astype(jnp.int32)
    rows_dev, length, width = tokens.shape
    mine = rows_dev // 2
    size = width // count
    ff = up_w.shape[2]
    units = ff // width

    def cols(array, n):
        return [array[:, j * width : (j + 1) * width] for j in range(n)]

    q_u, k_u, v_u = cols(low(qkv_w[0]), 3)
    plane = (
        jnp.concatenate([q_u, k_u] + cols(low(up_w[0]), units)),
        jnp.concatenate([v_u, low(out_w[0]), low(down_w[0])]),
    )
    got = swap(jnp.where(first, plane[1], plane[0]))
    zero = jnp.where(first, plane[0], got)
    one = jnp.where(first, got, plane[1])
    small = low(jnp.concatenate([gains_w.reshape(-1), shifts_w.reshape(-1), up_b.reshape(-1)]))
    small_n = small.shape[0]
    small_rows = -(-small_n // width)
    head_n = head_w.shape[0] * head_w.shape[1]
    head_rows = -(-head_n // width)
    pad_rows = -(-(small_rows + head_rows) // PAD) * PAD

    def to_rows(flat, rows):
        return jnp.pad(flat, (0, rows * width - flat.shape[0])).reshape(rows, width)

    extra = jnp.concatenate(
        [
            to_rows(small, small_rows),
            to_rows(low(head_w).reshape(-1), head_rows),
            jnp.zeros((pad_rows - small_rows - head_rows, width), BF),
        ]
    )
    cut = 2 * size

    a0_one = outer_first(jnp.concatenate([zero[:cut], extra]))
    f0_one = outer_first(after(zero[cut:], a0_one))
    a0_own = outer_last(a0_one)
    a1_one = outer_first(after(one[:cut], a0_own))
    f0_own = outer_last(f0_one)
    f1_one = outer_first(after(one[cut:], f0_own))
    a1_own = outer_last(a1_one)
    f1_own = outer_last(f1_one)

    def both(own, near, far):
        return (own, (near, far)), jax.tree.map(swap, (own, (near, far)))

    a0_near = near_quad(a0_own)
    a0_all = both(a0_own, a0_near, far_quad(*a0_near))
    w4_0 = assemble(True, place, 2, size, *a0_all)

    smalls, heads = [], []
    tails = [jax.tree.map(lambda item: item[:, cut:], item) for item in a0_all]
    tails_full = []
    for own, quads in tails:
        whole = jnp.zeros((4,) + own.shape, BF)
        for piece, start, rel in spread(own, quads):
            whole = lax.dynamic_update_slice(whole, piece[None], (place[0] ^ rel, start, 0, 0))
        tails_full.append(whole.transpose(1, 0, 2, 3).reshape(count, pad_rows, width))
    tails_full = (
        jnp.where(first, tails_full[0], tails_full[1]),
        jnp.where(first, tails_full[1], tails_full[0]),
    )
    n_g = gains_w.shape[1] * size
    n_s = shifts_w.shape[1] * size
    for tail in tails_full:
        flat = tail[:, :small_rows].reshape(count, -1)[:, :small_n].astype(F32)
        gains = flat[:, :n_g].reshape(count, -1, size).transpose(1, 0, 2).reshape(-1, width)
        shift = flat[:, n_g : n_g + n_s].reshape(count, -1, size).transpose(1, 0, 2).reshape(-1, width)
        cup = flat[:, n_g + n_s :].reshape(-1)
        eight = lambda item: jnp.pad(item, ((0, 8 - item.shape[0]), (0, 0)))
        smalls.append((eight(gains), eight(shift), cup))
        block = tail[:, small_rows : small_rows + head_rows].reshape(count, -1)[:, :head_n]
        heads.append(block.reshape(count * head_w.shape[0], head_w.shape[1]))
    head = jnp.concatenate(heads)
    (gain0, shift0, cup0), (gain1, shift1, cup1) = smalls

    own = lax.dynamic_slice_in_dim(tokens, section * mine, mine, 0)
    seg = lax.dynamic_slice_in_dim(segment_ids, section * mine, mine, 0)
    cot = lax.dynamic_slice_in_dim(cotangent, section * mine, mine, 0)
    rows = range(mine)
    seg_col = [jnp.broadcast_to(seg[r][:, None], (length, 128)) for r in rows]
    seg_row = [jnp.broadcast_to(seg[r][None], (8, length)) for r in rows]

    f0_near = near_quad(f0_own)
    a0 = after([own[r] for r in rows], f0_own, a1_one)
    kept_a0 = [attn_fwd(a0[r], seg_col[r], seg_row[r], w4_0, shift0) for r in rows]
    n1 = [kept[4] for kept in kept_a0]
    f0_near = after(f0_near, *n1)
    a1_own = after(a1_own, *n1)
    f1_one = after(f1_one, *n1)
    f0_all = both(f0_own, f0_near, far_quad(*f0_near))
    a1_near = near_quad(a1_own)
    f1_own = outer_last(f1_one)
    up0, down0 = assemble(False, place, units, size, *f0_all)
    n1 = after(n1, a1_own, f1_one)
    kept_f0 = [ffn_fwd(n1[r], up0, cup0, down0, gain0, shift0) for r in rows]
    a1 = [kept[4] for kept in kept_f0]
    a1_near = after(a1_near, *a1)
    f1_own = after(f1_own, *a1)
    a1_all = both(a1_own, a1_near, far_quad(*a1_near))
    f1_near = near_quad(f1_own)
    w4_1 = assemble(True, place, 2, size, *a1_all)
    a1 = after(a1, f1_own)
    kept_a1 = [attn_fwd(a1[r], seg_col[r], seg_row[r], w4_1, shift1) for r in rows]
    n1 = [kept[4] for kept in kept_a1]
    f1_near = after(f1_near, *n1)
    f1_all = both(f1_own, f1_near, far_quad(*f1_near))
    up1, down1 = assemble(False, place, units, size, *f1_all)
    kept_f1 = [ffn_fwd(n1[r], up1, cup1, down1, gain1, shift1) for r in rows]

    d_y1, g_head = [], 0.0
    for r in rows:
        y1 = kept_f1[r][4]
        proj = dot(y1, head)
        rho = lax.rsqrt(jnp.sum(proj * proj, axis=-1, keepdims=True) + norm_eps)
        c = cot[r].astype(F32)
        d_proj = low(rho * c - rho * rho * rho * proj * jnp.sum(proj * c, axis=-1, keepdims=True))
        g_head = g_head + dot(y1, d_proj, 0, 0)
        d_y1.append(dot(d_proj, head, 1, 1))

    def total(items):
        out = items[0]
        for item in items[1:]:
            out = jax.tree.map(lambda x, y: (x.astype(F32) + y.astype(F32)).astype(x.dtype), out, item)
        return out

    def ffn_back(d_out, kept_a, kept_f, up, down, gain, shift):
        outs = [
            ffn_bwd(grad_place, 4, d_out[r], *kept_f[r][2:4], *kept_f[r][:2], up, down, *kept_a[r][4:6], gain, shift)
            for r in rows
        ]
        keep, send, sums, cup = total([(o[0], o[1], o[3], o[4]) for o in outs])
        if count != 16:
            as_up = [in_chips(item, place, units, count) for item in (keep, send)]
            as_down = [down_in_chips(item, place, count) for item in (keep, send)]
            keep = jnp.where(first, as_up[0], as_down[0])
            send = jnp.where(first, as_down[1], as_up[1])
        return keep, send, [o[2] for o in outs], sums, cup

    def attn_back(d_out, a, kept, w4):
        outs = [attn_bwd(grad_place, 4, d_out[r], a[r], seg_col[r], seg_row[r], *kept[r][:4], w4) for r in rows]
        keep, send, sums, sumo = total([(o[0], o[1], o[3], o[4]) for o in outs])
        keep, send = [in_chips(item, place, 2, count) for item in (keep, send)]
        return keep, send, [o[2] for o in outs], sums, sumo

    keep, send, d_r, sums_f1, g_cup1 = ffn_back(d_y1, kept_a1, kept_f1, up1, down1, gain1, shift1)
    red_f1 = Reduce(keep, send)
    d_r = after(d_r, *red_f1.start_far())
    keep, send, d_a1, sums_a1, sumo_a1 = attn_back(d_r, a1, kept_a1, w4_1)
    red_f1.by = after(red_f1.by, *d_a1)
    d_y0 = after([low(item) for item in d_a1], *red_f1.start_near())
    red_a1 = Reduce(keep, send)
    d_y0 = after(d_y0, *red_a1.start_far())
    keep, send, d_r, sums_f0, g_cup0 = ffn_back(d_y0, kept_a0, kept_f0, up0, down0, gain0, shift0)
    red_f1.quad = after(red_f1.quad, *d_r)
    red_a1.by = after(red_a1.by, *d_r)
    d_r = after(d_r, *red_f1.start_outer(), *red_a1.start_near())
    red_f0 = Reduce(keep, send)
    d_r = after(d_r, *red_f0.start_far())
    keep, send, d_a0, sums_a0, sumo_a0 = attn_back(d_r, a0, kept_a0, w4_0)
    red_f1.there = after(red_f1.there, *d_a0)
    red_a1.quad = after(red_a1.quad, *d_a0)
    red_f0.by = after(red_f0.by, *d_a0)

    def small_block(sums_a, sumo, sums_f, g_cup, head_part):
        gains = jnp.stack([sums_f[0], sums_f[1]]).reshape(2, count, size).transpose(1, 0, 2)
        shift = jnp.stack([sums_a[0], sums_a[1], sumo[0], sums_f[3], sums_f[4], sums_f[2]])
        shift = shift.reshape(6, count, size).transpose(1, 0, 2)
        flat = jnp.concatenate(
            [gains.reshape(count, -1), shift.reshape(count, -1), g_cup.reshape(count, -1)], axis=1
        )
        flat = jnp.pad(flat, ((0, 0), (0, small_rows * width - small_n)))
        piece = jnp.pad(head_part.reshape(count, -1), ((0, 0), (0, head_rows * width - head_n)))
        block = jnp.concatenate(
            [
                flat.reshape(count, small_rows, width),
                piece.reshape(count, head_rows, width),
                jnp.zeros((count, pad_rows - small_rows - head_rows, width), F32),
            ],
            axis=1,
        )
        return relative(low(block).reshape(count // 4, 4, pad_rows, width).transpose(1, 0, 2, 3), place)

    half_head = g_head.reshape(2, -1, head_w.shape[1])
    tail0 = small_block(sums_a0, sumo_a0, sums_f0, g_cup0, half_head[0])
    tail1 = small_block(sums_a1, sumo_a1, sums_f1, g_cup1, half_head[1])
    keep = jnp.concatenate([keep, jnp.where(first, tail0, tail1)], axis=2)
    send = jnp.concatenate([send, jnp.where(first, tail1, tail0)], axis=2)
    red_a0 = Reduce(keep, send)
    red_f0.start_near()
    red_a0.start_far()
    red_f1.next_outer()
    red_a1.start_outer()
    red_a0.start_near()
    red_f0.start_outer()
    done_f1 = red_f1.finish()
    done_a1 = red_a1.finish()
    red_a0.start_outer()
    done_f0 = red_f0.finish()
    done_a0 = red_a0.finish()

    sums_zero = jnp.concatenate([done_a0[:cut], done_f0])
    sums_one = jnp.concatenate([done_a1, done_f1])
    other = swap(jnp.where(first, sums_one, sums_zero))
    low_plane = jnp.where(first, sums_zero, other)
    high_plane = jnp.where(first, other, sums_one)

    def unit(array, j):
        return array[j * size : (j + 1) * size]

    qkv_grad = jnp.concatenate([unit(low_plane, 0), unit(low_plane, 1), unit(high_plane, 0)], axis=1)
    out_grad = unit(high_plane, 1)
    up_grad = jnp.concatenate([unit(low_plane, 2 + j) for j in range(units)], axis=1)
    down_grad = high_plane[cut:]
    tail = done_a0[cut:]
    flat = tail[:small_rows].reshape(-1)[:small_n]
    gain_grad = flat[:n_g].reshape(gains_w.shape)
    shift_grad = flat[n_g : n_g + n_s].reshape(shifts_w.shape)
    cup_grad = flat[n_g + n_s :].reshape(up_b.shape)
    head_grad = tail[small_rows : small_rows + head_rows].reshape(-1)[:head_n].reshape(head_w.shape)

    d_first, d_second = jnp.stack(d_a0), jnp.stack(d_a1)
    got = swap(jnp.where(first, d_second, d_first))
    keep = jnp.where(first, d_first, d_second)
    input_grads = jnp.where(first, jnp.concatenate([keep, got]), jnp.concatenate([got, keep]))
    return (
        qkv_grad[None],
        out_grad[None],
        up_grad[None],
        down_grad[None],
        gain_grad,
        shift_grad,
        cup_grad,
        head_grad,
        input_grads[None],
    )


def solution(mesh):
    return jax.shard_map(
        shards,
        mesh=mesh,
        in_specs=(
            P("dp", None, None),
            P("dp", None),
            P("dp", None, None),
            P("section", "dp", None),
            P("section", "dp", None),
            P("section", "dp", None),
            P("section", "dp", None),
            P("section", None, "dp"),
            P("section", None, "dp"),
            P("section", "dp"),
            P(("section", "dp"), None),
        ),
        out_specs=(
            P("section", "dp", None),
            P("section", "dp", None),
            P("section", "dp", None),
            P("section", "dp", None),
            P("section", None, "dp"),
            P("section", None, "dp"),
            P("section", "dp"),
            P(("section", "dp"), None),
            P("section", "dp", None, None),
        ),
        check_vma=False,
    )
```

```python
import jax
import jax.numpy as jnp
from jax import lax
from jax.experimental import pallas as pl
from jax.experimental.pallas import tpu as pltpu
from jax.sharding import PartitionSpec as P

HEADS = 12
HDIM = 64
GROUP = 4
BLOCK = 128
PAD = 16
norm_eps = 1e-06
BF = jnp.bfloat16
F32 = jnp.float32
BOTH = ("section", "dp")
SCALE = HDIM ** (-0.5)

ERF_SCALE = 0.425
ERF_POLY = (
    0.11985147519825406,
    0.12072713574380309,
    0.10159474513684189,
    0.12334456743816431,
    -0.0435293372534038,
    0.19486821903107854,
    -0.15132025578595443,
    0.03446332841595847,
)


def dot(left, right, over_left=1, over_right=0):
    return lax.dot_general(
        left, right, (((over_left,), (over_right,)), ((), ())), preferred_element_type=F32
    )


def shape_of(shape, dtype):
    return jax.ShapeDtypeStruct(shape, dtype)


def whole_block(*shape):
    return pl.BlockSpec(shape, lambda g: (0,) * len(shape))


def gelu_pair(u):
    bell = jnp.exp(u * u * -0.5)
    t = 1.0 / (1.0 + (ERF_SCALE * 0.7071067811865476) * jnp.abs(u))
    poly = ERF_POLY[-1]
    for item in ERF_POLY[-2::-1]:
        poly = poly * t + item
    tail = bell * (poly * t)
    cdf = jnp.where(u < 0.0, tail, 1.0 - tail)
    return u * cdf, cdf + u * bell * 0.3989422804014327


def norm_stats(v):
    center = v - jnp.mean(v, axis=-1, keepdims=True)
    t = lax.rsqrt(jnp.mean(center * center, axis=-1, keepdims=True) + norm_eps)
    return center * t, t


def norm_back(dy, n, t, gain):
    dn = dy * gain
    mean = jnp.mean(dn, axis=-1, keepdims=True)
    along = jnp.mean(dn * n, axis=-1, keepdims=True)
    return t * (dn - mean - n * along)


def colsum(v):
    return jnp.sum(v, axis=0, keepdims=True)


def near(b, blocks):
    return max(0, b - 1) * BLOCK, min(blocks, b + 2) * BLOCK


def pick(flag, left, right):
    return jnp.where(flag, left, right)


def attn_weights(first, refs):
    own_0, own_1, own_rows, other_0, other_1, other_rows = refs
    query = pick(first, own_0[...], other_0[...])
    keys = pick(first, own_1[...], other_1[...])
    value = pick(first, other_0[...], own_0[...])
    out = pick(first, other_rows[...], own_rows[...])
    return query, keys, value, out


def block_of(b, pair):
    return slice(b * BLOCK, (b + 1) * BLOCK), slice(pair * 2 * HDIM, (pair + 1) * 2 * HDIM)


def two_heads(pair, lane):
    zero = jnp.zeros_like(pair)
    return jnp.concatenate([jnp.where(lane < HDIM, pair, zero), jnp.where(lane >= HDIM, pair, zero)])


def attn_fwd_kernel(
    place_ref, a_ref, sq_ref, sk_ref, w0, w1, w2, w3, w4, w5, bias_ref, shift_ref,
    q_ref, k_ref, v_ref, o_ref, n_ref, t_ref, acc,
):
    step = pl.program_id(0)
    blocks = a_ref.shape[0] // BLOCK
    a = a_ref[...]
    wq, wk, wv, wo = attn_weights(place_ref[1] == 0, (w0, w1, w2, w3, w4, w5))
    q_ref[...] = (dot(a, wq) + bias_ref[0:1]).astype(BF)
    k_ref[...] = dot(a, wk).astype(BF)
    v_ref[...] = (dot(a, wv) + bias_ref[1:2]).astype(BF)
    lane = lax.broadcasted_iota(jnp.int32, (BLOCK, 2 * HDIM), 1)
    tiles = [(b, pair) for b in range(blocks) for pair in range(GROUP // 2)]

    def scores_of(b, pair):
        lo, hi = near(b, blocks)
        rows, lanes = block_of(b, pair)
        same = sq_ref[rows, 0:1] == sk_ref[0:1, lo:hi]
        scores = dot(two_heads(q_ref[rows, lanes] * SCALE, lane), k_ref[lo:hi, lanes], 1, 1)
        return jnp.where(jnp.concatenate([same, same]), scores, -1000000000.0)

    ahead = scores_of(*tiles[0])
    for j, (b, pair) in enumerate(tiles):
        lo, hi = near(b, blocks)
        rows, lanes = block_of(b, pair)
        scores = ahead
        if j + 1 < len(tiles):
            ahead = scores_of(*tiles[j + 1])
        grown = jnp.exp(scores - jnp.max(scores, axis=-1, keepdims=True))
        scale = 1.0 / jnp.sum(grown, axis=-1, keepdims=True)
        out = dot((grown * scale).astype(BF), v_ref[lo:hi, lanes])
        o_ref[rows, lanes] = jnp.where(lane < HDIM, out[:BLOCK], out[BLOCK:]).astype(BF)
    part = dot(o_ref[...], wo)

    @pl.when(step == 0)
    def _():
        acc[...] = a.astype(F32) + shift_ref[2:3] + part

    @pl.when(step != 0)
    def _():
        acc[...] += part

    @pl.when(step == pl.num_programs(0) - 1)
    def _():
        n, t = norm_stats(acc[...])
        n_ref[...] = n
        t_ref[...] = jnp.broadcast_to(t, t_ref.shape)


SCALARS = pl.BlockSpec(memory_space=pltpu.SMEM)
NO_COST = pl.CostEstimate(flops=0, bytes_accessed=0, transcendentals=0)


def attn_weight_blocks(width, cols):
    def column(j):
        return pl.BlockSpec((width, cols), lambda g: (j, g))

    return [column(0), column(1), pl.BlockSpec((cols, width), lambda g: (width // cols + g, 0))] * 2


def attn_weight_args(planes):
    own, other = planes
    return (own, own, own, other, other, other)


def attn_fwd(place, a, seg_col, seg_row, planes, shift):
    length, width = a.shape
    cols = GROUP * HDIM
    group = pl.BlockSpec((length, cols), lambda g: (0, g))
    return pl.pallas_call(
        attn_fwd_kernel,
        grid=(HEADS // GROUP,),
        in_specs=[SCALARS, whole_block(length, width), whole_block(length, 128), whole_block(8, length)]
        + attn_weight_blocks(width, cols)
        + [pl.BlockSpec((8, cols), lambda g: (0, g)), whole_block(8, width)],
        out_specs=[group] * 4 + [whole_block(length, width), whole_block(length, 128)],
        out_shape=[shape_of((length, width), BF)] * 4
        + [shape_of((length, width), F32), shape_of((length, 128), F32)],
        scratch_shapes=[pltpu.VMEM((length, width), F32)],
        cost_estimate=NO_COST,
        name="attn_fwd",
    )(place, a, seg_col, seg_row, *attn_weight_args(planes), shift, shift)


def ffn_fwd_kernel(
    place_ref, n1_ref, own_ref, other_ref, cup_ref, gain_ref, shift_ref,
    g_ref, gp_ref, n_ref, t_ref, y_ref, h1, acc,
):
    step = pl.program_id(0)

    @pl.when(step == 0)
    def _():
        hidden = n1_ref[...] * gain_ref[0:1] + shift_ref[4:5]
        h1[...] = hidden.astype(BF)
        acc[...] = hidden + shift_ref[3:4]

    first = place_ref[1] == 0
    up = pick(first, own_ref[0], other_ref[0])
    down = pick(first, other_ref[0], own_ref[0])
    wide = 256
    parts = h1.shape[1] // wide

    def upper(j):
        cols = slice(j * wide, (j + 1) * wide)
        return dot(h1[...], up[:, cols]) + cup_ref[0, :, cols]

    ahead = upper(0)
    total = acc[...]
    for j in range(parts):
        cols = slice(j * wide, (j + 1) * wide)
        here = ahead
        if j + 1 < parts:
            ahead = upper(j + 1)
        g, slope = gelu_pair(here)
        g = g.astype(BF)
        g_ref[:, cols] = g
        gp_ref[:, cols] = slope.astype(BF)
        total = total + dot(g, down[cols])
    acc[...] = total

    @pl.when(step == pl.num_programs(0) - 1)
    def _():
        n, t = norm_stats(acc[...])
        n_ref[...] = n
        t_ref[...] = jnp.broadcast_to(t, t_ref.shape)
        y_ref[...] = (n * gain_ref[1:2] + shift_ref[5:6]).astype(BF)


def ffn_fwd(place, n1, planes, cup, gain, shift):
    length, width = n1.shape
    units = planes[0].shape[0]
    unit = pl.BlockSpec((1, width, width), lambda g: (g, 0, 0))
    column = pl.BlockSpec((length, width), lambda g: (0, g))
    return pl.pallas_call(
        ffn_fwd_kernel,
        grid=(units,),
        in_specs=[
            SCALARS,
            whole_block(length, width),
            unit,
            unit,
            pl.BlockSpec((1, 1, width), lambda g: (g, 0, 0)),
            whole_block(8, width),
            whole_block(8, width),
        ],
        out_specs=[column, column, whole_block(length, width), whole_block(length, 128), whole_block(length, width)],
        out_shape=[shape_of((length, units * width), BF)] * 2
        + [shape_of((length, width), F32), shape_of((length, 128), F32), shape_of((length, width), BF)],
        scratch_shapes=[pltpu.VMEM((length, width), BF), pltpu.VMEM((length, width), F32)],
        cost_estimate=NO_COST,
        name="ffn_fwd",
    )(place, n1, *planes, cup.reshape(units, 1, width), gain, shift)


def send_index(q, place_ref, core):
    rel = q ^ place_ref[0]
    x, y = rel & 1, rel >> 1
    return x * (1 + core) + y * (2 - core)


def outer_index(z, core):
    return z + core * ((z >> 1) + 2 * (z & 1) - z)


def by_section(section, action):
    for plane in range(2):
        pl.when(section == plane)(lambda plane=plane: action(plane))


def copy_all(copies, start):
    for item in copies:
        if start:
            item.start()
        else:
            item.wait()


def ffn_bwd_kernel(
    place_ref, dy_ref, n2_ref, t2_ref, g_ref, gp_ref, own_ref, other_ref, n1_ref, t1_ref, gain_ref, shift_ref,
    keep_ref, send_ref, dr1_ref, sums_ref, cup_ref, h1, df, acc, gup, gdown, sem,
):
    step = pl.program_id(0)
    last = pl.num_programs(0) - 1
    quads = keep_ref.shape[0]
    outer = keep_ref.shape[1]
    width = h1.shape[1]
    size = width // (quads * outer)

    @pl.when(step == 0)
    def _():
        n2 = n2_ref[...]
        dy = dy_ref[...].astype(F32)
        dr2 = norm_back(dy, n2, t2_ref[:, 0:1], gain_ref[1:2])
        low = dr2.astype(BF)
        df[...] = low
        acc[...] = dr2
        h1[...] = (n1_ref[...] * gain_ref[0:1] + shift_ref[4:5]).astype(BF)
        sums_ref[...] = jnp.zeros_like(sums_ref)
        sums_ref[1:2] = colsum(dy * n2)
        sums_ref[2:3] = colsum(dy)
        sums_ref[3:4] = colsum(low.astype(F32))

    d = df[...]
    first = place_ref[1] == 0
    w_up = pick(first, own_ref[0], other_ref[0])
    w_down = pick(first, other_ref[0], own_ref[0])
    down = dot(g_ref[...], d, 0, 0).astype(BF)
    gdown[step] = down.reshape(quads, width // quads, width)
    du = (dot(d, w_down, 1, 1) * gp_ref[...].astype(F32)).astype(BF)
    cup_ref[0] = colsum(du.astype(F32))
    up = dot(h1[...], du, 0, 0).astype(BF)
    gup[step] = up.reshape(outer, quads, size, width)
    acc[...] += dot(du, w_up, 1, 1)

    def copies(j, plane):
        up_to, down_to = (keep_ref, send_ref) if plane == 0 else (send_ref, keep_ref)
        out = []
        for q in range(quads):
            rel = send_index(q, place_ref, 0)
            for z in range(outer):
                to = up_to.at[rel, z, j * size : (j + 1) * size, :]
                out.append(pltpu.make_async_copy(gup.at[j, z, q], to, sem.at[j, z, q]))
            to = down_to.at[send_index(q, place_ref, 1), outer_index(j, 1)]
            out.append(pltpu.make_async_copy(gdown.at[j, q], to, sem.at[j, outer, q]))
        return out

    for j in range(gup.shape[0]):
        @pl.when(step == j)
        def _(j=j):
            by_section(place_ref[1], lambda plane: copy_all(copies(j, plane), True))

    @pl.when(step == last)
    def _():
        dh = acc[...]
        n1 = n1_ref[...]
        dr1_ref[...] = norm_back(dh, n1, t1_ref[:, 0:1], gain_ref[0:1])
        sums_ref[0:1] = colsum(dh * n1)
        sums_ref[4:5] = colsum(dh)

        def finish(plane):
            for j in range(gup.shape[0]):
                copy_all(copies(j, plane), False)

        by_section(place_ref[1], finish)


def ffn_bwd(place, outer, dy, n2, t2, g, gp, planes, n1, t1, gain, shift):
    length, width = n1.shape
    units = planes[0].shape[0]
    unit = pl.BlockSpec((1, width, width), lambda g: (g, 0, 0))
    size = width // (4 * outer)
    column = pl.BlockSpec((length, width), lambda g: (0, g))
    chunk = shape_of((4, outer, units * size, width), BF)
    return pl.pallas_call(
        ffn_bwd_kernel,
        grid=(units,),
        in_specs=[
            pl.BlockSpec(memory_space=pltpu.SMEM),
            whole_block(length, width),
            whole_block(length, width),
            whole_block(length, 128),
            column,
            column,
            unit,
            unit,
            whole_block(length, width),
            whole_block(length, 128),
            whole_block(8, width),
            whole_block(8, width),
        ],
        out_specs=[
            pl.BlockSpec(memory_space=pl.ANY),
            pl.BlockSpec(memory_space=pl.ANY),
            whole_block(length, width),
            whole_block(8, width),
            pl.BlockSpec((1, 1, width), lambda g: (g, 0, 0)),
        ],
        out_shape=[chunk, chunk, shape_of((length, width), F32), shape_of((8, width), F32), shape_of((units, 1, width), F32)],
        scratch_shapes=[
            pltpu.VMEM((length, width), BF),
            pltpu.VMEM((length, width), BF),
            pltpu.VMEM((length, width), F32),
            pltpu.VMEM((units, outer, 4, size, width), BF),
            pltpu.VMEM((units, 4, width // 4, width), BF),
            pltpu.SemaphoreType.DMA((units, outer + 1, 4)),
        ],
        cost_estimate=NO_COST,
        name="ffn_bwd",
    )(place, dy, n2, t2, g, gp, *planes, n1, t1, gain, shift)


def attn_bwd_kernel(
    place_ref, dr_ref, a_ref, sq_ref, sk_ref, q_ref, k_ref, v_ref, o_ref, w0, w1, w2, w3, w4, w5,
    keep_ref, send_ref, da_ref, sums_ref, sumo_ref, dat, do_sc, dq, dk, dv, grads, sem,
):
    step = pl.program_id(0)
    length, width = a_ref.shape
    blocks = length // BLOCK
    quads = keep_ref.shape[0]
    outer = keep_ref.shape[1]
    size = width // (quads * outer)
    cols = GROUP * HDIM

    @pl.when(step == 0)
    def _():
        low = dr_ref[...].astype(BF)
        dat[...] = low
        da_ref[...] = dr_ref[...]
        sumo_ref[...] = jnp.zeros_like(sumo_ref)
        sumo_ref[0:1] = colsum(low.astype(F32))

    d = dat[...]
    grad_o = dot(o_ref[...], d, 0, 0).astype(BF)
    wq, wk, wv, wo = attn_weights(place_ref[1] == 0, (w0, w1, w2, w3, w4, w5))
    do_sc[...] = dot(d, wo, 1, 1).astype(BF)
    dk[...] = jnp.zeros_like(dk)
    dv[...] = jnp.zeros_like(dv)
    lane = lax.broadcasted_iota(jnp.int32, (BLOCK, 2 * HDIM), 1)
    tiles = [(b, pair) for b in range(blocks) for pair in range(GROUP // 2)]

    def products(b, pair):
        lo, hi = near(b, blocks)
        rows, lanes = block_of(b, pair)
        same = sk_ref[lo:hi, 0:1] == sq_ref[0:1, rows]
        query = two_heads(q_ref[rows, lanes] * SCALE, lane)
        d_out = two_heads(do_sc[rows, lanes], lane)
        scores = dot(k_ref[lo:hi, lanes], query, 1, 1)
        scores = jnp.where(jnp.concatenate([same, same], axis=1), scores, -1000000000.0)
        return query, d_out, scores, dot(v_ref[lo:hi, lanes], d_out, 1, 1)

    ahead = products(*tiles[0])
    for j, (b, pair) in enumerate(tiles):
        lo, hi = near(b, blocks)
        rows, lanes = block_of(b, pair)
        query, d_out, scores, d_probs = ahead
        if j + 1 < len(tiles):
            ahead = products(*tiles[j + 1])
        grown = jnp.exp(scores - jnp.max(scores, axis=0, keepdims=True))
        probs = grown * (1.0 / jnp.sum(grown, axis=0, keepdims=True))
        d_scores = probs * (d_probs - jnp.sum(probs * d_probs, axis=0, keepdims=True))
        d_scores = d_scores.astype(BF)
        dv[lo:hi, lanes] += dot(probs.astype(BF), d_out)
        dk[lo:hi, lanes] += dot(d_scores, query)
        d_query = dot(d_scores, k_ref[lo:hi, lanes], 0, 0)
        dq[rows, lanes] = jnp.where(lane < HDIM, d_query[:BLOCK], d_query[BLOCK:]) * SCALE
    a = a_ref[...]
    out = da_ref[...]
    lows = (dq[...].astype(BF), dk[...].astype(BF), dv[...].astype(BF))
    made = []
    for low, weight in zip(lows, (wq, wk, wv)):
        made.append(dot(a, low, 0, 0).astype(BF))
        out = out + dot(low, weight, 1, 1)
    da_ref[...] = out
    sums_ref[...] = jnp.zeros_like(sums_ref)
    sums_ref[0:1] = colsum(lows[0].astype(F32))
    sums_ref[1:2] = colsum(lows[2].astype(F32))
    steps = HEADS // GROUP
    for j in range(steps):
        @pl.when(step == j)
        def _(j=j):
            here = slice(j * cols, (j + 1) * cols)
            for unit in range(3):
                grads[unit, :, here] = made[unit]
            grads[3, here, :] = grad_o

    @pl.when(step == steps - 1)
    def _():
        def copies(plane):
            out = []
            for unit in range(4):
                to = keep_ref if unit // 2 == plane else send_ref
                at = (unit % 2) * size
                core = unit // 2
                for block in range(quads * outer):
                    rel = send_index(block % quads, place_ref, core)
                    out.append(
                        pltpu.make_async_copy(
                            grads.at[unit, block * size : (block + 1) * size, :],
                            to.at[rel, outer_index(block // quads, core), at : at + size, :],
                            sem.at[unit, block],
                        )
                    )
            return out

        def move(plane):
            items = copies(plane)
            copy_all(items, True)
            copy_all(items, False)

        by_section(place_ref[1], move)


def attn_bwd(place, outer, dr, a, seg_col, seg_row, q, k, v, o, planes):
    length, width = a.shape
    size = width // (4 * outer)
    cols = GROUP * HDIM
    group = pl.BlockSpec((length, cols), lambda g: (0, g))
    chunk = shape_of((4, outer, 2 * size, width), BF)
    return pl.pallas_call(
        attn_bwd_kernel,
        grid=(HEADS // GROUP,),
        in_specs=[
            pl.BlockSpec(memory_space=pltpu.SMEM),
            whole_block(length, width),
            whole_block(length, width),
            whole_block(8, length),
            whole_block(length, 128),
        ]
        + [group] * 4
        + attn_weight_blocks(width, cols),
        out_specs=[
            pl.BlockSpec(memory_space=pl.ANY),
            pl.BlockSpec(memory_space=pl.ANY),
            whole_block(length, width),
            pl.BlockSpec((8, cols), lambda g: (0, g)),
            whole_block(8, width),
        ],
        out_shape=[chunk, chunk, shape_of((length, width), F32), shape_of((8, width), F32), shape_of((8, width), F32)],
        scratch_shapes=[pltpu.VMEM((length, width), BF), pltpu.VMEM((length, cols), BF)]
        + [pltpu.VMEM((length, cols), F32)] * 3
        + [pltpu.VMEM((4, width, width), BF), pltpu.SemaphoreType.DMA((4, 4 * outer))],
        cost_estimate=NO_COST,
        name="attn_bwd",
    )(place, dr, a, seg_row, seg_col, q, k, v, o, *attn_weight_args(planes))


def flip(value, mask, other=None):
    count = lax.axis_size("dp")
    masks = (mask, mask if other is None else other)
    pairs = [(s * count + i, s * count + (i ^ masks[s])) for s in range(2) for i in range(count)]
    return lax.ppermute(value, BOTH, pairs)


def swap(value):
    count = lax.axis_size("dp")
    pairs = [(s * count + i, (1 - s) * count + i) for s in range(2) for i in range(count)]
    return lax.ppermute(value, BOTH, pairs)


class Order:
    def __init__(self, mark):
        self.mark = mark

    def wait(self, *values):
        leaves, tree = jax.tree.flatten(values)
        *leaves, self.mark = lax.optimization_barrier((*leaves, self.mark))
        out = jax.tree.unflatten(tree, leaves)
        return out[0] if len(values) == 1 else out

    def now(self, *values):
        leaves, tree = jax.tree.flatten(values)
        leaves = lax.optimization_barrier((*leaves, self.mark))[:-1]
        out = jax.tree.unflatten(tree, leaves)
        return out[0] if len(values) == 1 else out


class Gather:
    def __init__(self, order, block):
        self.order, self.own, self.bit = order, block[None], 4

    def bits(self):
        return (self.bit, 12 - self.bit) if is_small(lax.axis_size("dp")) else (self.bit, self.bit)

    def outer(self):
        self.got = flip(self.order.now(self.own), *self.bits())

    def outer_done(self):
        bits = self.bits()
        me, section = lax.axis_index("dp"), lax.axis_index("section")
        self.join((me & jnp.where(section == 0, *bits)) != 0)
        self.bit *= 2

    def join(self, high):
        own, got = self.own, self.got
        self.own = jnp.where(high, jnp.concatenate([got, own]), jnp.concatenate([own, got]))

    def rest_of_outer(self):
        while self.bit < lax.axis_size("dp") // 2:
            self.outer()
            self.outer_done()

    def first(self):
        self.got = flip(self.order.now(self.own), 1, 2)

    def first_done(self):
        me = lax.axis_index("dp")
        self.own, self.got = self.own[None], self.got[None]
        self.join(jnp.where(lax.axis_index("section") == 0, me & 1, me >> 1 & 1) != 0)

    def second(self):
        self.got = flip(self.order.now(self.own), 2, 1)

    def wait(self):
        self.got = self.order.wait(self.got)

    def assembled(self, place, units, size):
        return assemble(place, units, size, self.own, self.got)


def assemble_kernel(units, size, place_ref, own_ref, got_ref, out, sem):
    outer = own_ref.shape[1]
    attn = len(out.shape) == 3
    section = place_ref[1]
    bit = (place_ref[0] >> (1 - section)) & 1

    def move(plane):
        moves = []
        for p, ref in enumerate((own_ref, got_ref)):
            for i in range(2):
                q = i * (1 + section) + (bit ^ p) * (2 - section)
                if attn:
                    tiles = size // PAD
                    chips = 4 * outer
                    more = ref.shape[2] - units * tiles
                    for z in range(outer):
                        chip = outer_index(z, section) * 4 + q
                        for u in range(units):
                            to = pl.ds((u * chips + chip) * tiles, tiles)
                            moves.append((ref.at[i, z, u * tiles : (u + 1) * tiles], out.at[to]))
                        if more:
                            to = pl.ds(units * chips * tiles + chip * more, more)
                            moves.append((ref.at[i, z, units * tiles :], out.at[to]))
                else:
                    for z in range(outer):
                        at = outer_index(z, section)
                        if plane == 0:
                            moves += [(ref.at[i, z, u], out.at[u, at, q]) for u in range(units)]
                        else:
                            moves.append((ref.at[i, z], out.at[at, q]))
        copies = [pltpu.make_async_copy(*item, sem.at[j]) for j, item in enumerate(moves)]
        copy_all(copies, True)
        copy_all(copies, False)

    if attn:
        move(0)
    else:
        by_section(section, move)


def assemble(place, units, size, own, got):
    _, outer, rows, width = own.shape
    attn = units == 2
    if is_small(4 * outer):
        if attn:
            shape = (4 * outer * rows // PAD, PAD, width)
            inner = (rows // PAD, PAD, width)
        else:
            shape = (units, outer, 4, size, width)
            inner = (units, size, width)
        whole = pl.pallas_call(
            lambda *refs: assemble_kernel(units, size, *refs),
            in_specs=[SCALARS] + [pl.BlockSpec(memory_space=pl.ANY)] * 2,
            out_specs=pl.BlockSpec(memory_space=pltpu.VMEM),
            out_shape=shape_of(shape, BF),
            scratch_shapes=[pltpu.SemaphoreType.DMA((4 * outer * (units + 1),))],
            cost_estimate=NO_COST,
            name="assemble",
        )(place, own.reshape((2, outer) + inner), got.reshape((2, outer) + inner))
        return whole.reshape((-1, width) if attn else (units, width, width))
    section = place[1]
    bit = (place[0] >> (1 - section)) & 1
    whole = jnp.zeros((outer, 4, rows, width), BF)
    for p, half in enumerate((own, got)):
        for i in range(2):
            q = i * (1 + section) + (bit ^ p) * (2 - section)
            whole = lax.dynamic_update_slice(whole, half[i][:, None], (0, q, 0, 0))
    whole = whole.reshape(4 * outer, rows, width)
    by_unit = [whole[:, j * size : (j + 1) * size].reshape(width, width) for j in range(units)]
    if attn:
        return jnp.concatenate(by_unit + [whole[:, units * size :].reshape(-1, width)])
    return jnp.where(section == 0, jnp.stack(by_unit), whole.reshape(units, width, width))


SWAPPED = (0, 2, 1, 3)


def is_small(count):
    return count == 16


def in_chips(chunk, place, units, count, core):
    quads, outer, rows, width = chunk.shape
    size = width // count
    if core:
        chunk = jnp.stack([chunk[:, z] for z in SWAPPED], axis=1)
        chunk = jnp.stack([chunk[q] for q in SWAPPED])
    if units:
        natural = chunk.reshape(quads, outer, units, -1, width).transpose(2, 1, 0, 3, 4)
        block = natural.reshape(units, count // 4, 4, size, width).transpose(2, 1, 0, 3, 4)
        block = block.reshape(4, count // 4, units * size, width)
    else:
        natural = chunk.transpose(1, 0, 2, 3).reshape(count // 4, 4, -1, width)
        block = natural.transpose(1, 0, 2, 3)
    return relative(block, place, core)


def in_planes(keep, send, place, units, count):
    if is_small(count):
        return keep, send
    first = place[1] == 0
    keeps, sends = [[in_chips(item, place, units[core], count, core) for core in range(2)] for item in (keep, send)]
    return jnp.where(first, *keeps), jnp.where(first, sends[1], sends[0])


def relative(block, place, core):
    at = [place[0] ^ (SWAPPED[rel] if core else rel) for rel in range(4)]
    block = jnp.stack([lax.dynamic_index_in_dim(block, q, 0, False) for q in at])
    if core == 0 or not is_small(lax.axis_size("dp")):
        return block
    return jnp.stack([block[:, z] for z in SWAPPED], axis=1)


def low(value):
    return value.astype(BF)


class Reduce:
    def __init__(self, order, keep, send):
        self.order = order
        self.keep = keep.reshape((2, 2) + keep.shape[1:])
        self.got = swap(order.now(send)).reshape(self.keep.shape)

    def wait(self):
        self.got = self.order.wait(self.got)

    def send(self, value, *masks):
        self.got = flip(self.order.now(low(value)), *masks)

    def second(self):
        self.terms = (self.keep, self.got)
        self.send(self.total(1), 2, 1)

    def total(self, which):
        return sum((item[which].astype(F32) for item in self.terms), 0.0)

    def first(self):
        self.terms = (self.terms[0][0], self.terms[1][0], self.got)
        self.send(self.total(1), 1, 2)

    def outer(self):
        self.rest = self.total(0) + self.got.astype(F32)
        self.bit = lax.axis_size("dp") // 2
        self.halve()

    def halve(self):
        size = self.rest.shape[0] // 2
        me, section = lax.axis_index("dp"), lax.axis_index("section")
        bits = (self.bit, 12 - self.bit) if is_small(lax.axis_size("dp")) else (self.bit, self.bit)
        high = (me & jnp.where(section == 0, *bits)) != 0
        low_half, high_half = self.rest[:size], self.rest[size:]
        self.rest = jnp.where(high, high_half, low_half)
        self.send(jnp.where(high, low_half, high_half), *bits)

    def next_outer(self):
        self.rest = self.rest + self.got.astype(F32)
        self.bit //= 2
        self.halve()

    def rest_of_outer(self):
        while self.bit > 8:
            self.next_outer()
        if self.bit > 4:
            self.next_outer()

    def finish(self):
        return (self.rest + self.got.astype(F32))[0]


def shards(tokens, segment_ids, cotangent, qkv_w, out_w, up_w, down_w, gains_w, shifts_w, up_b, head_w):
    count = lax.axis_size("dp")
    section = lax.axis_index("section")
    me = lax.axis_index("dp")
    first = section == 0
    place = jnp.stack([me & 3, section]).astype(jnp.int32)
    grad_place = place if is_small(count) else jnp.stack([jnp.zeros_like(section), section]).astype(jnp.int32)
    rows_dev, length, width = tokens.shape
    mine = rows_dev // 2
    size = width // count
    ff = up_w.shape[2]
    units = ff // width

    def cols(array, n):
        return [array[:, j * width : (j + 1) * width] for j in range(n)]

    q_u, k_u, v_u = cols(low(qkv_w[0]), 3)
    plane = (
        jnp.concatenate([q_u, k_u] + cols(low(up_w[0]), units)),
        jnp.concatenate([v_u, low(out_w[0]), low(down_w[0])]),
    )
    got = swap(jnp.where(first, plane[1], plane[0]))
    zero = jnp.where(first, plane[0], got)
    one = jnp.where(first, got, plane[1])
    small = low(jnp.concatenate([gains_w.reshape(-1), shifts_w.reshape(-1), up_b.reshape(-1)]))
    small_n = small.shape[0]
    small_rows = -(-small_n // width)
    head_n = head_w.shape[0] * head_w.shape[1]
    head_rows = -(-head_n // width)
    pad_rows = -(-(small_rows + head_rows) // PAD) * PAD

    def to_rows(flat, rows):
        return jnp.pad(flat, (0, rows * width - flat.shape[0])).reshape(rows, width)

    extra = jnp.concatenate(
        [
            to_rows(small, small_rows),
            to_rows(low(head_w).reshape(-1), head_rows),
            jnp.zeros((pad_rows - small_rows - head_rows, width), BF),
        ]
    )
    cut = 2 * size

    order = Order(place)
    a0_g = Gather(order, jnp.concatenate([zero[:cut], extra]))
    f0_g, a1_g, f1_g = Gather(order, zero[cut:]), Gather(order, one[:cut]), Gather(order, one[cut:])

    def both(chunk, units):
        own = chunk.assembled(place, units, size)
        return own, swap(order.now(own))

    a0_g.outer()
    a0_g.wait()
    a0_g.outer_done()
    a0_g.rest_of_outer()
    a0_g.outer()
    a0_g.wait()
    a0_g.outer_done()
    a0_g.first()
    f0_g.outer()
    a0_g.got, f0_g.got = order.wait(a0_g.got, f0_g.got)
    a0_g.first_done()
    f0_g.outer_done()
    f0_g.rest_of_outer()
    a0_g.second()
    f0_g.outer()
    a1_g.outer()
    a0_g.got, f0_g.got, a1_g.got = order.wait(a0_g.got, f0_g.got, a1_g.got)
    f0_g.outer_done()
    f0_g.first()
    a1_g.outer_done()
    a1_g.rest_of_outer()
    a1_g.outer()
    f1_g.outer()
    planes_a0 = both(a0_g, 2)
    planes_a0, f0_g.got, a1_g.got, f1_g.got = order.wait(planes_a0, f0_g.got, a1_g.got, f1_g.got)
    f0_g.first_done()
    f0_g.second()
    a1_g.outer_done()
    a1_g.first()
    f1_g.outer_done()
    f1_g.rest_of_outer()
    f1_g.outer()
    tails = [item[2 * width :] for item in planes_a0]

    smalls, heads = [], []
    tails_full = (jnp.where(first, tails[0], tails[1]), jnp.where(first, tails[1], tails[0]))
    tails_full = [item.reshape(count, pad_rows, width) for item in tails_full]
    n_g = gains_w.shape[1] * size
    n_s = shifts_w.shape[1] * size
    for tail in tails_full:
        flat = tail[:, :small_rows].reshape(count, -1)[:, :small_n].astype(F32)
        gains = flat[:, :n_g].reshape(count, -1, size).transpose(1, 0, 2).reshape(-1, width)
        shift = flat[:, n_g : n_g + n_s].reshape(count, -1, size).transpose(1, 0, 2).reshape(-1, width)
        cup = flat[:, n_g + n_s :].reshape(-1)
        eight = lambda item: jnp.pad(item, ((0, 8 - item.shape[0]), (0, 0)))
        smalls.append((eight(gains), eight(shift), cup))
        block = tail[:, small_rows : small_rows + head_rows].reshape(count, -1)[:, :head_n]
        heads.append(block.reshape(count * head_w.shape[0], head_w.shape[1]))
    head = jnp.concatenate(heads)
    (gain0, shift0, cup0), (gain1, shift1, cup1) = smalls

    own = lax.dynamic_slice_in_dim(tokens, section * mine, mine, 0)
    seg = lax.dynamic_slice_in_dim(segment_ids, section * mine, mine, 0)
    cot = lax.dynamic_slice_in_dim(cotangent, section * mine, mine, 0)
    rows = range(mine)
    seg_col = [jnp.broadcast_to(seg[r][:, None], (length, 128)) for r in rows]
    seg_row = [jnp.broadcast_to(seg[r][None], (8, length)) for r in rows]

    a0 = order.now([own[r] for r in rows])
    kept_a0 = [attn_fwd(place, a0[r], seg_col[r], seg_row[r], planes_a0, shift0) for r in rows]
    kept_a0, f0_g.got, a1_g.got, f1_g.got = order.wait(kept_a0, f0_g.got, a1_g.got, f1_g.got)
    a1_g.first_done()
    a1_g.second()
    f1_g.outer_done()
    f1_g.first()
    planes_f0 = order.wait(both(f0_g, units))
    n1 = [kept[4] for kept in kept_a0]
    n1 = order.now(n1)
    kept_f0 = [ffn_fwd(place, n1[r], planes_f0, cup0, gain0, shift0) for r in rows]
    kept_f0, a1_g.got, f1_g.got = order.wait(kept_f0, a1_g.got, f1_g.got)
    f1_g.first_done()
    f1_g.second()
    planes_a1 = order.wait(both(a1_g, 2))
    a1 = [kept[4] for kept in kept_f0]
    a1 = order.now(a1)
    kept_a1 = [attn_fwd(place, a1[r], seg_col[r], seg_row[r], planes_a1, shift1) for r in rows]
    kept_a1, f1_g.got = order.wait(kept_a1, f1_g.got)
    planes_f1 = both(f1_g, units)
    n1 = [kept[4] for kept in kept_a1]
    kept_f1 = [ffn_fwd(place, n1[r], planes_f1, cup1, gain1, shift1) for r in rows]

    d_y1, g_head = [], 0.0
    for r in rows:
        y1 = kept_f1[r][4]
        proj = dot(y1, head)
        rho = lax.rsqrt(jnp.sum(proj * proj, axis=-1, keepdims=True) + norm_eps)
        c = cot[r].astype(F32)
        d_proj = low(rho * c - rho * rho * rho * proj * jnp.sum(proj * c, axis=-1, keepdims=True))
        g_head = g_head + dot(y1, d_proj, 0, 0)
        d_y1.append(dot(d_proj, head, 1, 1))

    def total(items):
        out = items[0]
        for item in items[1:]:
            out = jax.tree.map(lambda x, y: (x.astype(F32) + y.astype(F32)).astype(x.dtype), out, item)
        return out

    def ffn_back(d_out, kept_a, kept_f, planes, gain, shift):
        outs = [
            ffn_bwd(grad_place, 4, d_out[r], *kept_f[r][2:4], *kept_f[r][:2], planes, *kept_a[r][4:6], gain, shift)
            for r in rows
        ]
        keep, send, sums, cup = total([(o[0], o[1], o[3], o[4]) for o in outs])
        keep, send = in_planes(keep, send, place, (units, 0), count)
        return keep, send, [o[2] for o in outs], sums, cup

    def attn_back(d_out, a, kept, planes):
        outs = [attn_bwd(grad_place, 4, d_out[r], a[r], seg_col[r], seg_row[r], *kept[r][:4], planes) for r in rows]
        keep, send, sums, sumo = total([(o[0], o[1], o[3], o[4]) for o in outs])
        keep, send = in_planes(keep, send, place, (2, 2), count)
        return keep, send, [o[2] for o in outs], sums, sumo

    keep, send, d_r, sums_f1, g_cup1 = ffn_back(d_y1, kept_a1, kept_f1, planes_f1, gain1, shift1)
    f1_r = Reduce(order, keep, send)
    f1_r.wait()
    f1_r.second()
    d_r = order.now(d_r)
    keep, send, d_a1, sums_a1, sumo_a1 = attn_back(d_r, a1, kept_a1, planes_a1)
    d_a1, f1_r.got = order.wait(d_a1, f1_r.got)
    a1_r = Reduce(order, keep, send)
    f1_r.first()
    a1_r.wait()
    a1_r.second()
    d_y0 = order.now([low(item) for item in d_a1])
    keep, send, d_r, sums_f0, g_cup0 = ffn_back(d_y0, kept_a0, kept_f0, planes_f0, gain0, shift0)
    d_r, f1_r.got, a1_r.got = order.wait(d_r, f1_r.got, a1_r.got)
    f0_r = Reduce(order, keep, send)
    f1_r.outer()
    a1_r.first()
    f0_r.wait()
    f0_r.second()
    d_r = order.now(d_r)
    keep, send, d_a0, sums_a0, sumo_a0 = attn_back(d_r, a0, kept_a0, planes_a0)

    f1_r.got, a1_r.got, f0_r.got, d_a0 = order.wait(f1_r.got, a1_r.got, f0_r.got, d_a0)

    def small_block(sums_a, sumo, sums_f, g_cup, head_part, core):
        gains = jnp.stack([sums_f[0], sums_f[1]]).reshape(2, count, size).transpose(1, 0, 2)
        shift = jnp.stack([sums_a[0], sums_a[1], sumo[0], sums_f[3], sums_f[4], sums_f[2]])
        shift = shift.reshape(6, count, size).transpose(1, 0, 2)
        flat = jnp.concatenate(
            [gains.reshape(count, -1), shift.reshape(count, -1), g_cup.reshape(count, -1)], axis=1
        )
        flat = jnp.pad(flat, ((0, 0), (0, small_rows * width - small_n)))
        piece = jnp.pad(head_part.reshape(count, -1), ((0, 0), (0, head_rows * width - head_n)))
        block = jnp.concatenate(
            [
                flat.reshape(count, small_rows, width),
                piece.reshape(count, head_rows, width),
                jnp.zeros((count, pad_rows - small_rows - head_rows, width), F32),
            ],
            axis=1,
        )
        return relative(low(block).reshape(count // 4, 4, pad_rows, width).transpose(1, 0, 2, 3), place, core)

    half_head = g_head.reshape(2, -1, head_w.shape[1])
    tail0 = small_block(sums_a0, sumo_a0, sums_f0, g_cup0, half_head[0], 0)
    tail1 = small_block(sums_a1, sumo_a1, sums_f1, g_cup1, half_head[1], 1)
    keep = jnp.concatenate([keep, jnp.where(first, tail0, tail1)], axis=2)
    send = jnp.concatenate([send, jnp.where(first, tail1, tail0)], axis=2)
    a0_r = Reduce(order, keep, send)
    f1_r.rest_of_outer()
    a1_r.outer()
    f0_r.first()
    a0_r.wait()
    a0_r.second()
    a1_r.got, f1_r.got, f0_r.got = order.wait(a1_r.got, f1_r.got, f0_r.got)
    a1_r.rest_of_outer()
    f0_r.outer()
    a0_r.wait()
    a0_r.first()
    a1_r.got, f0_r.got, a0_r.got = order.wait(a1_r.got, f0_r.got, a0_r.got)
    f0_r.rest_of_outer()
    a0_r.outer()
    a0_r.got, f0_r.got = order.wait(a0_r.got, f0_r.got)
    a0_r.rest_of_outer()
    done_f1, done_a1, done_f0, done_a0 = [item.finish() for item in (f1_r, a1_r, f0_r, a0_r)]

    sums_zero = jnp.concatenate([done_a0[:cut], done_f0])
    sums_one = jnp.concatenate([done_a1, done_f1])
    other = swap(jnp.where(first, sums_one, sums_zero))
    low_plane = jnp.where(first, sums_zero, other)
    high_plane = jnp.where(first, other, sums_one)

    def unit(array, j):
        return array[j * size : (j + 1) * size]

    qkv_grad = jnp.concatenate([unit(low_plane, 0), unit(low_plane, 1), unit(high_plane, 0)], axis=1)
    out_grad = unit(high_plane, 1)
    up_grad = jnp.concatenate([unit(low_plane, 2 + j) for j in range(units)], axis=1)
    down_grad = high_plane[cut:]
    tail = done_a0[cut:]
    flat = tail[:small_rows].reshape(-1)[:small_n]
    gain_grad = flat[:n_g].reshape(gains_w.shape)
    shift_grad = flat[n_g : n_g + n_s].reshape(shifts_w.shape)
    cup_grad = flat[n_g + n_s :].reshape(up_b.shape)
    head_grad = tail[small_rows : small_rows + head_rows].reshape(-1)[:head_n].reshape(head_w.shape)

    d_first, d_second = jnp.stack(d_a0), jnp.stack(d_a1)
    got = swap(jnp.where(first, d_second, d_first))
    keep = jnp.where(first, d_first, d_second)
    input_grads = jnp.where(first, jnp.concatenate([keep, got]), jnp.concatenate([got, keep]))
    return (
        qkv_grad[None],
        out_grad[None],
        up_grad[None],
        down_grad[None],
        gain_grad,
        shift_grad,
        cup_grad,
        head_grad,
        input_grads[None],
    )


def solution(mesh):
    return jax.shard_map(
        shards,
        mesh=mesh,
        in_specs=(
            P("dp", None, None),
            P("dp", None),
            P("dp", None, None),
            P("section", "dp", None),
            P("section", "dp", None),
            P("section", "dp", None),
            P("section", "dp", None),
            P("section", None, "dp"),
            P("section", None, "dp"),
            P("section", "dp"),
            P(("section", "dp"), None),
        ),
        out_specs=(
            P("section", "dp", None),
            P("section", "dp", None),
            P("section", "dp", None),
            P("section", "dp", None),
            P("section", None, "dp"),
            P("section", None, "dp"),
            P("section", "dp"),
            P(("section", "dp"), None),
            P("section", "dp", None, None),
        ),
        check_vma=False,
    )
```

```python
import jax
import jax.numpy as jnp
from jax import lax
from jax.experimental import pallas as pl
from jax.experimental.pallas import tpu as pltpu
from jax.sharding import PartitionSpec as P

HEADS = 12
HDIM = 64
GROUP = 4
BLOCK = 128
PAD = 16
norm_eps = 1e-06
BF = jnp.bfloat16
F32 = jnp.float32
BOTH = ("section", "dp")
SCALE = HDIM ** (-0.5)

ERF_SCALE = 0.425
ERF_POLY = (
    0.11985147519825406,
    0.12072713574380309,
    0.10159474513684189,
    0.12334456743816431,
    -0.0435293372534038,
    0.19486821903107854,
    -0.15132025578595443,
    0.03446332841595847,
)


def dot(left, right, over_left=1, over_right=0):
    return lax.dot_general(
        left, right, (((over_left,), (over_right,)), ((), ())), preferred_element_type=F32
    )


def shape_of(shape, dtype):
    return jax.ShapeDtypeStruct(shape, dtype)


def whole_block(*shape):
    return pl.BlockSpec(shape, lambda g: (0,) * len(shape))


def gelu_pair(u):
    bell = jnp.exp(u * u * -0.5)
    t = 1.0 / (1.0 + (ERF_SCALE * 0.7071067811865476) * jnp.abs(u))
    poly = ERF_POLY[-1]
    for item in ERF_POLY[-2::-1]:
        poly = poly * t + item
    tail = bell * (poly * t)
    cdf = jnp.where(u < 0.0, tail, 1.0 - tail)
    return u * cdf, cdf + u * bell * 0.3989422804014327


def norm_stats(v):
    center = v - jnp.mean(v, axis=-1, keepdims=True)
    t = lax.rsqrt(jnp.mean(center * center, axis=-1, keepdims=True) + norm_eps)
    return center * t, t


def norm_back(dy, n, t, gain):
    dn = dy * gain
    mean = jnp.mean(dn, axis=-1, keepdims=True)
    along = jnp.mean(dn * n, axis=-1, keepdims=True)
    return t * (dn - mean - n * along)


def colsum(v):
    return jnp.sum(v, axis=0, keepdims=True)


def near(b, blocks):
    return max(0, b - 1) * BLOCK, min(blocks, b + 2) * BLOCK


def is_small(count):
    return count == 16


def steps_of(count, core, near_first):
    outer = [4 << j for j in range((count // 4).bit_length() - 1)]
    quad = [1, 2]
    if core:
        quad = [2, 1]
        if is_small(count):
            outer = outer[::-1]
    return quad + outer if near_first else outer + quad


def bit_of(me, mask):
    return (me >> (mask.bit_length() - 1)) & 1


def send_index(chip_z, chip_q, me, core, near_first):
    index = 0
    rel = (chip_z * 4 + chip_q) ^ me
    for j, mask in enumerate(steps_of(16, core, near_first)):
        index = index + bit_of(rel, mask) * (1 << j)
    return index


def each(count, body):
    lax.fori_loop(0, count, lambda j, _: (body(j), 0)[1], 0)


class Loads:
    def __init__(self, near_first, place_ref, own, other, targets, sem):
        self.near_first, self.place, self.planes = near_first, place_ref, (own, other)
        self.targets, self.sem = targets, sem

    def at(self, plane, unit, chip):
        target = self.targets[plane]
        if len(target.shape) == 5:
            return target.at[unit, chip >> 2, chip & 3]
        return target.at[chip >> 2, chip & 3]

    def start(self, plane, unit, first, count):
        order = steps_of(16, plane, self.near_first)
        target = self.targets[plane]
        size = target.shape[-2]

        def by_chip(section, chip):
            pieces = self.planes[0] if plane == section else self.planes[1]
            to, sem = self.at(plane, unit, chip), self.sem.at[plane, unit, chip]
            if len(pieces) == 1:
                source = pieces[0].reshape(*target.shape)
                at = source.at[unit] if len(target.shape) == 5 else source
                pltpu.make_async_copy(at.at[chip >> 2, chip & 3], to, sem).start()
                return
            index = sum(bit_of(chip, order[j]) << j for j in range(3))
            far = bit_of(chip ^ self.place[0], order[3])
            for p in range(2):
                @pl.when(far == p)
                def _():
                    rows = pl.ds(pl.multiple_of(unit * size, PAD), size)
                    pltpu.make_async_copy(pieces[p].at[index, rows, :], to, sem).start()

        by_section(self.place[1], lambda section: each(count, lambda j: by_chip(section, first + j)))

    def wait(self, plane, unit, first, count):
        def by_chip(chip):
            to = self.at(plane, unit, chip)
            pltpu.make_async_copy(to, to, self.sem.at[plane, unit, chip]).wait()

        each(count, lambda j: by_chip(first + j))


def block_of(b, pair):
    return slice(b * BLOCK, (b + 1) * BLOCK), slice(pair * 2 * HDIM, (pair + 1) * 2 * HDIM)


def two_heads(pair, lane):
    zero = jnp.zeros_like(pair)
    return jnp.concatenate([jnp.where(lane < HDIM, pair, zero), jnp.where(lane >= HDIM, pair, zero)])


def attn_fwd_kernel(near_first, halves, place_ref, *refs):
    own, other = refs[:halves], refs[halves : 2 * halves]
    a_ref, sq_ref, sk_ref, bias_ref, shift_ref = refs[2 * halves : 2 * halves + 5]
    q_ref, k_ref, v_ref, o_ref, n_ref, t_ref, acc, low_w, high_w, sem = refs[2 * halves + 5 :]
    step = pl.program_id(0)
    length, width = a_ref.shape
    blocks = length // BLOCK
    a = a_ref[...]
    loads = Loads(near_first, place_ref, own, other, (low_w, high_w), sem)

    @pl.when(step == 0)
    def _():
        for plane, unit in ((0, 0), (0, 1), (1, 0), (1, 1)):
            loads.start(plane, unit, 0, 16)
        for plane, unit in ((0, 0), (0, 1), (1, 0)):
            loads.wait(plane, unit, 0, 16)

    cols = GROUP * HDIM
    here = pl.ds(pl.multiple_of(step * cols, cols), cols)

    def column(ref, j):
        return ref[j, :, :, :, here].reshape(width, cols)

    q_ref[...] = (dot(a, column(low_w, 0)) + bias_ref[2:3]).astype(BF)
    k_ref[...] = dot(a, column(low_w, 1)).astype(BF)
    v_ref[...] = (dot(a, column(high_w, 0)) + bias_ref[3:4]).astype(BF)
    lane = lax.broadcasted_iota(jnp.int32, (BLOCK, 2 * HDIM), 1)
    tiles = [(b, pair) for b in range(blocks) for pair in range(GROUP // 2)]

    def scores_of(b, pair):
        lo, hi = near(b, blocks)
        rows, lanes = block_of(b, pair)
        same = sq_ref[rows, 0:1] == sk_ref[0:1, lo:hi]
        scores = dot(two_heads(q_ref[rows, lanes] * SCALE, lane), k_ref[lo:hi, lanes], 1, 1)
        return jnp.where(jnp.concatenate([same, same]), scores, -1000000000.0)

    ahead = scores_of(*tiles[0])
    for j, (b, pair) in enumerate(tiles):
        lo, hi = near(b, blocks)
        rows, lanes = block_of(b, pair)
        scores = ahead
        if j + 1 < len(tiles):
            ahead = scores_of(*tiles[j + 1])
        grown = jnp.exp(scores - jnp.max(scores, axis=-1, keepdims=True))
        scale = 1.0 / jnp.sum(grown, axis=-1, keepdims=True)
        out = dot((grown * scale).astype(BF), v_ref[lo:hi, lanes])
        o_ref[rows, lanes] = jnp.where(lane < HDIM, out[:BLOCK], out[BLOCK:]).astype(BF)
    @pl.when(step == 0)
    def _():
        loads.wait(1, 1, 0, 16)

    part = dot(o_ref[...], high_w.at[1].reshape(width, width)[here, :])

    @pl.when(step == 0)
    def _():
        acc[...] = a.astype(F32) + shift_ref[4:5] + part

    @pl.when(step != 0)
    def _():
        acc[...] += part

    @pl.when(step == pl.num_programs(0) - 1)
    def _():
        n, t = norm_stats(acc[...])
        n_ref[...] = n
        t_ref[...] = jnp.broadcast_to(t, t_ref.shape)


SCALARS = pl.BlockSpec(memory_space=pltpu.SMEM)
NO_COST = pl.CostEstimate(flops=0, bytes_accessed=0, transcendentals=0)


ANYWHERE = pl.BlockSpec(memory_space=pl.ANY)


def attn_fwd(near_first, place, a, seg_col, seg_row, planes, shift):
    length, width = a.shape
    cols = GROUP * HDIM
    group = pl.BlockSpec((length, cols), lambda g: (0, g))
    half = (2, 4, 4, width // 16, width)
    halves = len(planes[0])
    return pl.pallas_call(
        lambda *refs: attn_fwd_kernel(near_first, halves, *refs),
        grid=(HEADS // GROUP,),
        in_specs=[SCALARS]
        + [ANYWHERE] * (2 * halves)
        + [whole_block(length, width), whole_block(length, 128), whole_block(8, length)]
        + [pl.BlockSpec((8, cols), lambda g: (0, g)), whole_block(8, width)],
        out_specs=[group] * 4 + [whole_block(length, width), whole_block(length, 128)],
        out_shape=[shape_of((length, width), BF)] * 4
        + [shape_of((length, width), F32), shape_of((length, 128), F32)],
        scratch_shapes=[
            pltpu.VMEM((length, width), F32),
            pltpu.VMEM(half, BF),
            pltpu.VMEM(half, BF),
            pltpu.SemaphoreType.DMA((2, 2, 16)),
        ],
        cost_estimate=NO_COST,
        name="attn_fwd",
    )(place, *planes[0], *planes[1], a, seg_col, seg_row, shift, shift)


def ffn_fwd_kernel(near_first, halves, place_ref, *refs):
    own, other = refs[:halves], refs[halves : 2 * halves]
    n1_ref, cup_ref, gain_ref, shift_ref = refs[2 * halves : 2 * halves + 4]
    g_ref, gp_ref, n_ref, t_ref, y_ref = refs[2 * halves + 4 : 2 * halves + 9]
    h1, acc, up_w, down_w, sem = refs[2 * halves + 9 :]
    step = pl.program_id(0)
    width = n1_ref.shape[1]
    loads = Loads(near_first, place_ref, own, other, (up_w, down_w), sem)
    units = up_w.shape[0]

    @pl.when(step == 0)
    def _():
        loads.start(0, 0, 0, 16)
        loads.start(1, 0, 0, 4)

    @pl.when(step == 0)
    def _():
        hidden = n1_ref[...] * gain_ref[0:1] + shift_ref[6:7]
        h1[...] = hidden.astype(BF)
        acc[...] = hidden + shift_ref[5:6]

    loads.wait(0, step, 0, 16)

    @pl.when(step + 1 < units)
    def _():
        loads.start(0, step + 1, 0, 16)
        loads.start(1, 0, 4 * (step + 1), 4)

    loads.wait(1, 0, 4 * step, 4)
    up = up_w[step].reshape(width, width)
    down = down_w[step].reshape(width, width)
    wide = 256
    parts = h1.shape[1] // wide

    def upper(j):
        cols = slice(j * wide, (j + 1) * wide)
        return dot(h1[...], up[:, cols]) + cup_ref[0, :, cols]

    ahead = upper(0)
    total = acc[...]
    for j in range(parts):
        cols = slice(j * wide, (j + 1) * wide)
        here = ahead
        if j + 1 < parts:
            ahead = upper(j + 1)
        g, slope = gelu_pair(here)
        g = g.astype(BF)
        g_ref[:, cols] = g
        gp_ref[:, cols] = slope.astype(BF)
        total = total + dot(g, down[cols])
    acc[...] = total

    @pl.when(step == pl.num_programs(0) - 1)
    def _():
        n, t = norm_stats(acc[...])
        n_ref[...] = n
        t_ref[...] = jnp.broadcast_to(t, t_ref.shape)
        y_ref[...] = (n * gain_ref[1:2] + shift_ref[7:8]).astype(BF)


def ffn_fwd(near_first, place, n1, planes, cup, gain, shift):
    length, width = n1.shape
    units = cup.shape[0]
    column = pl.BlockSpec((length, width), lambda g: (0, g))
    up = (units, 4, 4, width // 16, width)
    down = (4, 4, units * width // 16, width)
    halves = len(planes[0])
    return pl.pallas_call(
        lambda *refs: ffn_fwd_kernel(near_first, halves, *refs),
        grid=(units,),
        in_specs=[SCALARS]
        + [ANYWHERE] * (2 * halves)
        + [
            whole_block(length, width),
            pl.BlockSpec((1, 1, width), lambda g: (g, 0, 0)),
            whole_block(8, width),
            whole_block(8, width),
        ],
        out_specs=[column, column, whole_block(length, width), whole_block(length, 128), whole_block(length, width)],
        out_shape=[shape_of((length, units * width), BF)] * 2
        + [shape_of((length, width), F32), shape_of((length, 128), F32), shape_of((length, width), BF)],
        scratch_shapes=[
            pltpu.VMEM((length, width), BF),
            pltpu.VMEM((length, width), F32),
            pltpu.VMEM(up, BF),
            pltpu.VMEM(down, BF),
            pltpu.SemaphoreType.DMA((2, units, 16)),
        ],
        cost_estimate=NO_COST,
        name="ffn_fwd",
    )(place, *planes[0], *planes[1], n1, cup, gain, shift)


def by_section(section, action):
    for plane in range(2):
        pl.when(section == plane)(lambda plane=plane: action(plane))


def ffn_bwd_kernel(near_first, halves, place_ref, *refs):
    own, other = refs[:halves], refs[halves : 2 * halves]
    dy_ref, n2_ref, t2_ref, g_ref, gp_ref, n1_ref, t1_ref, gain_ref, shift_ref = refs[2 * halves : 2 * halves + 9]
    keep_ref, send_ref, dr1_ref, sums_ref, cup_ref = refs[2 * halves + 9 : 2 * halves + 14]
    h1, df, acc, gup, gdown, up_w, down_w, sem, load_sem = refs[2 * halves + 14 :]
    step = pl.program_id(0)
    loads = Loads(near_first, place_ref, own, other, (up_w, down_w), load_sem)

    @pl.when(step == 0)
    def _():
        loads.start(1, 0, 0, 4)
        loads.start(0, 0, 0, 16)

    last = pl.num_programs(0) - 1
    quads = outer = 4
    width = h1.shape[1]
    size = width // (quads * outer)

    @pl.when(step == 0)
    def _():
        n2 = n2_ref[...]
        dy = dy_ref[...].astype(F32)
        dr2 = norm_back(dy, n2, t2_ref[:, 0:1], gain_ref[1:2])
        low = dr2.astype(BF)
        df[...] = low
        acc[...] = dr2
        h1[...] = (n1_ref[...] * gain_ref[0:1] + shift_ref[6:7]).astype(BF)
        sums_ref[...] = jnp.zeros_like(sums_ref)
        sums_ref[1:2] = colsum(dy * n2)
        sums_ref[2:3] = colsum(dy)
        sums_ref[3:4] = colsum(low.astype(F32))

    loads.wait(1, 0, 4 * step, 4)
    loads.wait(0, step, 0, 16)

    @pl.when(step < last)
    def _():
        loads.start(1, 0, 4 * (step + 1), 4)
        loads.start(0, step + 1, 0, 16)

    d = df[...]
    down = dot(g_ref[...], d, 0, 0).astype(BF)
    gdown[step] = down.reshape(quads, width // quads, width)
    du = (dot(d, down_w[step].reshape(width, width), 1, 1) * gp_ref[...].astype(F32)).astype(BF)
    cup_ref[0] = colsum(du.astype(F32))
    up = dot(h1[...], du, 0, 0).astype(BF)
    gup[step] = up.reshape(outer, quads, size, width)
    acc[...] += dot(du, up_w[step].reshape(width, width), 1, 1)

    def up_copy(section, j, chip):
        to = (keep_ref if section == 0 else send_ref).at[send_index(chip >> 2, chip & 3, place_ref[0], 0, near_first)]
        rows = pl.ds(pl.multiple_of(j * size, PAD), size)
        return pltpu.make_async_copy(gup.at[j, chip >> 2, chip & 3], to.at[rows, :], sem.at[j, chip])

    def down_copy(section, j, q):
        to = (send_ref if section == 0 else keep_ref).at[send_index(j, q, place_ref[0], 1, near_first)]
        return pltpu.make_async_copy(gdown.at[j, q], to, sem.at[j, 16 + q])

    def begin(section):
        each(16, lambda chip: up_copy(section, step, chip).start())
        each(4, lambda q: down_copy(section, step, q).start())

    by_section(place_ref[1], begin)

    @pl.when(step == last)
    def _():
        dh = acc[...]
        n1 = n1_ref[...]
        dr1_ref[...] = norm_back(dh, n1, t1_ref[:, 0:1], gain_ref[0:1])
        sums_ref[0:1] = colsum(dh * n1)
        sums_ref[4:5] = colsum(dh)

        def finish(section):
            def one(j):
                each(16, lambda chip: up_copy(section, j, chip).wait())
                each(4, lambda q: down_copy(section, j, q).wait())

            each(gup.shape[0], one)

        by_section(place_ref[1], finish)


def ffn_bwd(near_first, place, dy, n2, t2, g, gp, planes, n1, t1, gain, shift):
    length, width = n1.shape
    units = g.shape[1] // width
    outer, size = 4, width // 16
    halves = len(planes[0])
    up = (units, outer, 4, size, width)
    down = (outer, 4, units * size, width)
    column = pl.BlockSpec((length, width), lambda g: (0, g))
    chunk = shape_of((16, units * size, width), BF)
    return pl.pallas_call(
        lambda *refs: ffn_bwd_kernel(near_first, halves, *refs),
        grid=(units,),
        in_specs=[
            SCALARS,
            *[ANYWHERE] * (2 * halves),
            whole_block(length, width),
            whole_block(length, width),
            whole_block(length, 128),
            column,
            column,
            whole_block(length, width),
            whole_block(length, 128),
            whole_block(8, width),
            whole_block(8, width),
        ],
        out_specs=[
            pl.BlockSpec(memory_space=pl.ANY),
            pl.BlockSpec(memory_space=pl.ANY),
            whole_block(length, width),
            whole_block(8, width),
            pl.BlockSpec((1, 1, width), lambda g: (g, 0, 0)),
        ],
        out_shape=[chunk, chunk, shape_of((length, width), F32), shape_of((8, width), F32), shape_of((units, 1, width), F32)],
        scratch_shapes=[
            pltpu.VMEM((length, width), BF),
            pltpu.VMEM((length, width), BF),
            pltpu.VMEM((length, width), F32),
            pltpu.VMEM((units, outer, 4, size, width), BF),
            pltpu.VMEM((units, 4, width // 4, width), BF),
            pltpu.VMEM(up, BF),
            pltpu.VMEM(down, BF),
            pltpu.SemaphoreType.DMA((units, 20)),
            pltpu.SemaphoreType.DMA((2, units, 16)),
        ],
        cost_estimate=NO_COST,
        name="ffn_bwd",
    )(place, *planes[0], *planes[1], dy, n2, t2, g, gp, n1, t1, gain, shift)


def attn_bwd_kernel(near_first, halves, place_ref, *refs):
    own, other = refs[:halves], refs[halves : 2 * halves]
    dr_ref, a_ref, sq_ref, sk_ref, q_ref, k_ref, v_ref, o_ref = refs[2 * halves : 2 * halves + 8]
    keep_ref, send_ref, da_ref, sums_ref, sumo_ref = refs[2 * halves + 8 : 2 * halves + 13]
    dat, do_sc, dq, dk, dv, grads, low_w, high_w, sem, load_sem = refs[2 * halves + 13 :]
    step = pl.program_id(0)
    loads = Loads(near_first, place_ref, own, other, (low_w, high_w), load_sem)

    @pl.when(step == 0)
    def _():
        for plane, unit in ((1, 1), (0, 0), (0, 1), (1, 0)):
            loads.start(plane, unit, 0, 16)

    length, width = a_ref.shape
    blocks = length // BLOCK
    quads = outer = 4
    size = width // (quads * outer)
    cols = GROUP * HDIM

    @pl.when(step == 0)
    def _():
        low = dr_ref[...].astype(BF)
        dat[...] = low
        da_ref[...] = dr_ref[...]
        sumo_ref[...] = jnp.zeros_like(sumo_ref)
        sumo_ref[0:1] = colsum(low.astype(F32))

    d = dat[...]
    grad_o = dot(o_ref[...], d, 0, 0).astype(BF)

    @pl.when(step == 0)
    def _():
        loads.wait(1, 1, 0, 16)

    now = pl.ds(pl.multiple_of(step * cols, cols), cols)
    do_sc[...] = dot(d, high_w.at[1].reshape(width, width)[now, :], 1, 1).astype(BF)
    dk[...] = jnp.zeros_like(dk)
    dv[...] = jnp.zeros_like(dv)
    lane = lax.broadcasted_iota(jnp.int32, (BLOCK, 2 * HDIM), 1)
    tiles = [(b, pair) for b in range(blocks) for pair in range(GROUP // 2)]

    def products(b, pair):
        lo, hi = near(b, blocks)
        rows, lanes = block_of(b, pair)
        same = sk_ref[lo:hi, 0:1] == sq_ref[0:1, rows]
        query = two_heads(q_ref[rows, lanes] * SCALE, lane)
        d_out = two_heads(do_sc[rows, lanes], lane)
        scores = dot(k_ref[lo:hi, lanes], query, 1, 1)
        scores = jnp.where(jnp.concatenate([same, same], axis=1), scores, -1000000000.0)
        return query, d_out, scores, dot(v_ref[lo:hi, lanes], d_out, 1, 1)

    ahead = products(*tiles[0])
    for j, (b, pair) in enumerate(tiles):
        lo, hi = near(b, blocks)
        rows, lanes = block_of(b, pair)
        query, d_out, scores, d_probs = ahead
        if j + 1 < len(tiles):
            ahead = products(*tiles[j + 1])
        grown = jnp.exp(scores - jnp.max(scores, axis=0, keepdims=True))
        probs = grown * (1.0 / jnp.sum(grown, axis=0, keepdims=True))
        d_scores = probs * (d_probs - jnp.sum(probs * d_probs, axis=0, keepdims=True))
        d_scores = d_scores.astype(BF)
        dv[lo:hi, lanes] += dot(probs.astype(BF), d_out)
        dk[lo:hi, lanes] += dot(d_scores, query)
        d_query = dot(d_scores, k_ref[lo:hi, lanes], 0, 0)
        dq[rows, lanes] = jnp.where(lane < HDIM, d_query[:BLOCK], d_query[BLOCK:]) * SCALE
    a = a_ref[...]
    out = da_ref[...]
    lows = (dq[...].astype(BF), dk[...].astype(BF), dv[...].astype(BF))
    made = []

    @pl.when(step == 0)
    def _():
        for plane, unit in ((0, 0), (0, 1), (1, 0)):
            loads.wait(plane, unit, 0, 16)

    for low, (w_ref, j) in zip(lows, ((low_w, 0), (low_w, 1), (high_w, 0))):
        made.append(dot(a, low, 0, 0).astype(BF))
        out = out + dot(low, w_ref[j, :, :, :, now].reshape(width, cols), 1, 1)
    da_ref[...] = out
    sums_ref[...] = jnp.zeros_like(sums_ref)
    sums_ref[0:1] = colsum(lows[0].astype(F32))
    sums_ref[1:2] = colsum(lows[2].astype(F32))
    steps = HEADS // GROUP
    for j in range(steps):
        @pl.when(step == j)
        def _(j=j):
            here = slice(j * cols, (j + 1) * cols)
            for unit in range(3):
                grads[unit, :, here] = made[unit]
            grads[3, here, :] = grad_o

    @pl.when(step == steps - 1)
    def _():
        def copy(section, unit, chip):
            core = unit // 2
            to = (keep_ref if core == section else send_ref).at[
                send_index(chip >> 2, chip & 3, place_ref[0], core, near_first)
            ]
            rows = pl.ds(pl.multiple_of(chip * size, PAD), size)
            at = (unit % 2) * size
            return pltpu.make_async_copy(grads.at[unit, rows, :], to.at[at : at + size, :], sem.at[unit, chip])

        def move(section):
            for unit in range(4):
                each(16, lambda chip: copy(section, unit, chip).start())
            for unit in range(4):
                each(16, lambda chip: copy(section, unit, chip).wait())

        by_section(place_ref[1], move)


def attn_bwd(near_first, more, place, dr, a, seg_col, seg_row, q, k, v, o, planes):
    length, width = a.shape
    outer, size = 4, width // 16
    halves = len(planes[0])
    half = (2, outer, 4, size, width)
    cols = GROUP * HDIM
    group = pl.BlockSpec((length, cols), lambda g: (0, g))
    chunk = shape_of((16, 2 * size + more, width), BF)
    return pl.pallas_call(
        lambda *refs: attn_bwd_kernel(near_first, halves, *refs),
        grid=(HEADS // GROUP,),
        in_specs=[
            SCALARS,
            *[ANYWHERE] * (2 * halves),
            whole_block(length, width),
            whole_block(length, width),
            whole_block(8, length),
            whole_block(length, 128),
        ]
        + [group] * 4,
        out_specs=[
            pl.BlockSpec(memory_space=pl.ANY),
            pl.BlockSpec(memory_space=pl.ANY),
            whole_block(length, width),
            pl.BlockSpec((8, cols), lambda g: (0, g)),
            whole_block(8, width),
        ],
        out_shape=[chunk, chunk, shape_of((length, width), F32), shape_of((8, width), F32), shape_of((8, width), F32)],
        scratch_shapes=[pltpu.VMEM((length, width), BF), pltpu.VMEM((length, cols), BF)]
        + [pltpu.VMEM((length, cols), F32)] * 3
        + [pltpu.VMEM((4, width, width), BF), pltpu.VMEM(half, BF), pltpu.VMEM(half, BF)]
        + [pltpu.SemaphoreType.DMA((4, 4 * outer)), pltpu.SemaphoreType.DMA((2, 2, 16))],
        cost_estimate=NO_COST,
        name="attn_bwd",
    )(place, *planes[0], *planes[1], dr, a, seg_row, seg_col, q, k, v, o)


def flip(value, mask, other=None):
    count = lax.axis_size("dp")
    masks = (mask, mask if other is None else other)
    pairs = [(s * count + i, s * count + (i ^ masks[s])) for s in range(2) for i in range(count)]
    return lax.ppermute(value, BOTH, pairs)


def swap(value):
    count = lax.axis_size("dp")
    pairs = [(s * count + i, (1 - s) * count + i) for s in range(2) for i in range(count)]
    return lax.ppermute(value, BOTH, pairs)


def across(value, source):
    count = lax.axis_size("dp")
    return lax.ppermute(value, BOTH, [(source * count + i, (1 - source) * count + i) for i in range(count)])


class Order:
    def __init__(self, mark):
        self.mark = mark

    def wait(self, *values):
        leaves, tree = jax.tree.flatten(values)
        *leaves, self.mark = lax.optimization_barrier((*leaves, self.mark))
        out = jax.tree.unflatten(tree, leaves)
        return out[0] if len(values) == 1 else out

    def now(self, *values):
        leaves, tree = jax.tree.flatten(values)
        leaves = lax.optimization_barrier((*leaves, self.mark))[:-1]
        out = jax.tree.unflatten(tree, leaves)
        return out[0] if len(values) == 1 else out


class Gather:
    def __init__(self, order, block, near_first=False):
        self.order, self.own, self.near_first = order, block[None], near_first
        self.left = list(zip(*[steps_of(lax.axis_size("dp"), core, near_first) for core in range(2)]))

    def start(self):
        self.got = flip(self.order.now(self.own), *self.left[0])

    def start_part(self, part):
        half = self.own.shape[0] // 2
        return flip(self.order.now(self.own[part * half : (part + 1) * half]), *self.left[0])

    def done(self):
        masks = self.left.pop(0)
        high = (lax.axis_index("dp") & jnp.where(lax.axis_index("section") == 0, *masks)) != 0
        own, got = self.own, self.got
        self.own = jnp.where(high, jnp.concatenate([got, own]), jnp.concatenate([own, got]))

    def spare(self, steps):
        while len(self.left) > steps:
            self.start()
            self.done()

    def wait(self):
        self.got = self.order.wait(self.got)

    def swap_own(self):
        self.other_own = swap(self.order.now(self.own))

    def swap_got(self):
        self.other_got = swap(self.order.now(self.got))

    def halves(self, place, units, size):
        pairs = tuple(
            (own,) + (got if isinstance(got, tuple) else (got,))
            for own, got in ((self.own, self.got), (self.other_own, self.other_got))
        )
        if is_small(lax.axis_size("dp")):
            return pairs
        return natural_planes(place, units, size, self.near_first, *pairs)


def natural_planes(place, units, size, near_first, own, other):
    count = lax.axis_size("dp")
    out = []
    for section, halves in ((place[1], own), (1 - place[1], other)):
        both = jnp.concatenate(halves)
        at = []
        for core in range(2):
            order = steps_of(count, core, near_first)
            chips = jnp.arange(count)
            index = sum(bit_of(chips, mask) << j for j, mask in enumerate(order))
            at.append(index ^ (bit_of(place[0], order[-1]) << (len(order) - 1)))
        whole = jnp.take(both, jnp.where(section == 0, *at), axis=0)
        rows, width = whole.shape[1:]
        if size:
            by_unit = jnp.stack([whole[:, j * size : (j + 1) * size].reshape(width, width) for j in range(units)])
            if units != 2:
                flat = whole.reshape(units, width, width)
                by_unit = jnp.where(section == 0, by_unit.reshape(flat.shape), flat)
            whole = by_unit.reshape(units, 4, 4, width // 16, width)
        out.append((whole,))
    return out


def tail_kernel(cut, place_ref, *refs):
    halves, (vec_ref, cup_ref, head_ref, pieces, sem) = refs[:4], refs[4:]

    def move(section):
        for start in (True, False):
            for plane in range(2):
                order = steps_of(16, plane, False)
                for p in range(2):
                    source = halves[p if plane == section else 2 + p].at[:, cut:, :]

                    def by_index(index):
                        chip = sum(bit_of(index, 1 << j) * order[j] for j in range(3))
                        chip = chip + order[3] * (bit_of(place_ref[0], order[3]) ^ p)
                        to = pieces.at[plane, chip >> 2, chip & 3]
                        copy = pltpu.make_async_copy(source.at[index], to, sem.at[plane, 8 * p + index])
                        copy.start() if start else copy.wait()

                    each(8, by_index)

    by_section(place_ref[1], move)
    size = vec_ref.shape[2] // 16
    wide = cup_ref.shape[1] * size
    height = head_ref.shape[0] // 32
    for plane in range(2):
        for chip in range(16):
            piece = pieces[plane, chip // 4, chip % 4].astype(F32)
            vec_ref[plane, :, chip * size : (chip + 1) * size] = piece[:8, :size]
            at = (chip % 4) * wide
            cup_ref[plane, chip // 4, :, at : at + wide] = piece[8:9, :wide]
            for k in range(height // 8):
                row = (plane * 16 + chip) * height + 8 * k
                head_ref[row : row + 8, :] = piece[:8, 384 + 128 * k : 512 + 128 * k]


def tails_of(place, cut, units, own, other):
    width = own[0].shape[2]
    return pl.pallas_call(
        lambda *refs: tail_kernel(cut, *refs),
        in_specs=[SCALARS] + [ANYWHERE] * 4,
        out_specs=[pl.BlockSpec(memory_space=pltpu.VMEM)] * 3,
        out_shape=[shape_of((2, 8, width), F32), shape_of((2, units, 1, width), F32), shape_of((width, 128), F32)],
        scratch_shapes=[pltpu.VMEM((2, 4, 4, PAD, width), BF), pltpu.SemaphoreType.DMA((2, 16))],
        cost_estimate=NO_COST,
        name="tails",
    )(place, *own, *other)


def natural_tails(place, cut, own, other):
    own, other = jax.tree.map(lambda item: item[:, cut:], (own, other))
    (mine,), (there,) = natural_planes(place, 0, 0, False, own, other)
    first = place[1] == 0
    return jnp.where(first, mine, there), jnp.where(first, there, mine)


def pack_kernel(cut, place_ref, *refs):
    sums = (refs[0:4], refs[4:8])
    head_ref, _, _, keep_ref, send_ref, pieces, sem = refs[8:]
    width = pieces.shape[3]
    size = width // 16
    height = head_ref.shape[0] // 32
    pieces[...] = jnp.zeros_like(pieces)
    for plane, (attn, out, ffn, cup) in enumerate(sums):
        wide = cup.shape[0] * size
        rows = [ffn[0:1], ffn[1:2], attn[0:1], attn[1:2], out[0:1], ffn[3:4], ffn[4:5], ffn[2:3]]
        vec = jnp.concatenate(rows)
        for chip in range(16):
            pieces[plane, chip, :8, :size] = vec[:, chip * size : (chip + 1) * size].astype(BF)
            at = (chip % 4) * wide
            pieces[plane, chip, 8:9, :wide] = cup[chip // 4, :, at : at + wide].astype(BF)
            for k in range(height // 8):
                row = (plane * 16 + chip) * height + 8 * k
                pieces[plane, chip, :8, 384 + 128 * k : 512 + 128 * k] = head_ref[row : row + 8, :].astype(BF)

    def move(section):
        for start in (True, False):
            for plane in range(2):
                to = keep_ref if plane == section else send_ref

                def by_chip(chip):
                    at = send_index(chip >> 2, chip & 3, place_ref[0], plane, False)
                    copy = pltpu.make_async_copy(pieces.at[plane, chip], to.at[at, cut:, :], sem.at[plane, chip])
                    copy.start() if start else copy.wait()

                each(16, by_chip)

    by_section(place_ref[1], move)


def pack_tails(place, cut, layer0, layer1, g_head, keep, send):
    return pl.pallas_call(
        lambda *refs: pack_kernel(cut, *refs),
        in_specs=[SCALARS] + [pl.BlockSpec(memory_space=pltpu.VMEM)] * 9 + [ANYWHERE] * 2,
        out_specs=[ANYWHERE] * 2,
        out_shape=[shape_of(keep.shape, BF)] * 2,
        input_output_aliases={10: 0, 11: 1},
        scratch_shapes=[pltpu.VMEM((2, 16, PAD, keep.shape[2]), BF), pltpu.SemaphoreType.DMA((2, 16))],
        cost_estimate=NO_COST,
        name="pack",
    )(place, *layer0, *layer1, g_head, keep, send)


def in_chips(chunk, place, units, count, core, near_first):
    chips = jnp.arange(16)
    at = sum(bit_of(chips, mask) << j for j, mask in enumerate(steps_of(16, core, near_first)))
    chunk = jnp.take(chunk, at, axis=0)
    width = chunk.shape[2]
    if units:
        natural = chunk.reshape(16, units, -1, width).transpose(1, 0, 2, 3).reshape(units, count, -1, width)
        natural = natural.transpose(1, 0, 2, 3).reshape(count, -1, width)
    else:
        natural = chunk.reshape(count, -1, width)
    return relative(natural, place, core, near_first)


def in_planes(keep, send, place, units, count, near_first):
    if is_small(count):
        return keep, send
    first = place[1] == 0
    keeps, sends = [
        [in_chips(item, place, units[core], count, core, near_first) for core in range(2)] for item in (keep, send)
    ]
    return jnp.where(first, *keeps), jnp.where(first, sends[1], sends[0])


def relative(block, place, core, near_first=False):
    order = steps_of(block.shape[0], core, near_first)
    index = jnp.arange(block.shape[0])
    chips = sum(bit_of(index, 1 << j) * mask for j, mask in enumerate(order))
    return jnp.take(block, chips ^ place[0], axis=0)


def low(value):
    return value.astype(BF)


def add_low(terms, start, count):
    return low(sum(item[start : start + count].astype(F32) for item in terms))


class Reduce:
    def __init__(self, order, keep, send, near_first=False):
        self.order = order
        self.left = list(zip(*[steps_of(lax.axis_size("dp"), core, near_first) for core in range(2)]))
        self.terms = [keep]
        self.got = swap(order.now(send))

    def wait(self):
        self.got = self.order.wait(self.got)

    def start(self):
        self.terms.append(self.got)
        half = self.got.shape[0] // 2
        self.got = flip(self.order.now(add_low(self.terms, half, half)), *self.left.pop())

    def start_upper(self):
        self.terms.append(self.got)
        self.part = self.got.shape[0] // 4
        self.masks = self.left.pop()
        self.upper = flip(self.order.now(add_low(self.terms, 3 * self.part, self.part)), *self.masks)

    def start_lower(self):
        self.got = flip(self.order.now(add_low(self.terms, 2 * self.part, self.part)), *self.masks)

    def start_from_upper(self):
        part = self.part
        terms = [item[part : 2 * part] for item in self.terms] + [self.upper]
        self.ahead = flip(self.order.now(add_low(terms, 0, part)), *self.left.pop())

    def join(self):
        self.terms.append(self.got)
        self.got = self.ahead

    def spare(self, steps):
        while len(self.left) > steps:
            self.start()

    def finish(self):
        return sum(item[0].astype(F32) for item in self.terms + [self.got])


def shards(tokens, segment_ids, cotangent, qkv_w, out_w, up_w, down_w, gains_w, shifts_w, up_b, head_w):
    count = lax.axis_size("dp")
    section = lax.axis_index("section")
    me = lax.axis_index("dp")
    first = section == 0
    place = jnp.stack([me, section]).astype(jnp.int32)
    grad_place = place if is_small(count) else jnp.stack([jnp.zeros_like(section), section]).astype(jnp.int32)
    rows_dev, length, width = tokens.shape
    mine = rows_dev // 2
    size = width // count
    ff = up_w.shape[2]
    units = ff // width

    def cols(array, n):
        return [array[:, j * width : (j + 1) * width] for j in range(n)]

    def planes_of(low_units, high_units):
        low_plane, high_plane = jnp.concatenate(low_units), jnp.concatenate(high_units)
        got = swap(jnp.where(first, high_plane, low_plane))
        return jnp.where(first, low_plane, got), jnp.where(first, got, high_plane)

    q_u, k_u, v_u = cols(low(qkv_w[0]), 3)
    a_zero, a_one = planes_of([q_u, k_u], [v_u, low(out_w[0])])
    f_zero, f_one = planes_of(cols(low(up_w[0]), units), [low(down_w[0])])
    small = low(jnp.concatenate([gains_w.reshape(-1), shifts_w.reshape(-1), up_b.reshape(-1)]))
    small_n = small.shape[0]
    small_rows = -(-small_n // width)
    head_n = head_w.shape[0] * head_w.shape[1]
    head_rows = -(-head_n // width)
    pad_rows = -(-(small_rows + head_rows) // PAD) * PAD

    def to_rows(flat, rows):
        return jnp.pad(flat, (0, rows * width - flat.shape[0])).reshape(rows, width)

    if is_small(count):
        vec = jnp.concatenate([low(gains_w[0]), low(shifts_w[0])])
        eights = [low(head_w[8 * k : 8 * k + 8]) for k in range(3)]
        above = jnp.concatenate([jnp.pad(vec, ((0, 0), (0, 384 - size)))] + eights, axis=1)
        extra = jnp.concatenate([above, jnp.pad(low(up_b), ((0, 7), (0, width - up_b.shape[1])))])
    else:
        extra = jnp.concatenate(
            [
                to_rows(small, small_rows),
                to_rows(low(head_w).reshape(-1), head_rows),
                jnp.zeros((pad_rows - small_rows - head_rows, width), BF),
            ]
        )
    cut = 2 * size

    order = Order(place)
    a0_g = Gather(order, jnp.concatenate([a_zero, extra]))
    f0_g, a1_g, f1_g = Gather(order, f_zero), Gather(order, a_one, True), Gather(order, f_one)
    a0_g.spare(4)
    f0_g.spare(4)
    f1_g.spare(4)
    a0_g.start()
    a1_g.start()
    a0_g.got, a1_g.got = order.wait(a0_g.got, a1_g.got)
    a0_g.done()
    a0_g.start()
    f0_g.start()
    a1_g.done()
    a1_g.start()
    a0_g.got, f0_g.got, a1_g.got = order.wait(a0_g.got, f0_g.got, a1_g.got)
    a0_g.done()
    a0_g.start()
    f0_g.done()
    f0_g.start()
    a1_g.done()
    a1_g.spare(2)
    a0_g.got, f0_g.got = order.wait(a0_g.got, f0_g.got)
    a0_g.done()
    a0_g.start()
    f0_g.done()
    f0_g.start()
    a1_g.start()
    f1_g.start()
    a0_g.swap_own()
    a0_g.got, f0_g.got, a1_g.got, a0_g.other_own, f1_g.got = order.wait(
        a0_g.got, f0_g.got, a1_g.got, a0_g.other_own, f1_g.got
    )
    f0_g.done()
    f0_g.start()
    a1_g.done()
    f1_g.done()
    f1_g.start()
    a0_g.swap_got()
    a0_g.other_got = order.wait(a0_g.other_got)
    a0_half = a0_g.halves(place, 2, size)
    n_g = gains_w.shape[1] * size
    n_s = shifts_w.shape[1] * size
    tail_halves = (a0_g.own, a0_g.got), (a0_g.other_own, a0_g.other_got)
    if is_small(count):
        vecs, cups, head = tails_of(place, cut, units, *tail_halves)
        head = low(head)
    else:
        vecs, cups, heads = [], [], []
        for tail in natural_tails(place, cut, *tail_halves):
            flat = tail[:, :small_rows].reshape(count, -1)[:, :small_n].astype(F32)
            vec = flat[:, : n_g + n_s].reshape(count, -1, size).transpose(1, 0, 2).reshape(-1, width)
            vecs.append(vec)
            cups.append(flat[:, n_g + n_s :].reshape(units, 1, width))
            block = tail[:, small_rows : small_rows + head_rows].reshape(count, -1)[:, :head_n]
            heads.append(block.reshape(count * head_w.shape[0], head_w.shape[1]))
        head = jnp.concatenate(heads)
    gain0 = shift0 = vecs[0]
    gain1 = shift1 = vecs[1]
    cup0, cup1 = cups[0], cups[1]

    own = lax.dynamic_slice_in_dim(tokens, section * mine, mine, 0)
    seg = lax.dynamic_slice_in_dim(segment_ids, section * mine, mine, 0)
    cot = lax.dynamic_slice_in_dim(cotangent, section * mine, mine, 0)
    rows = range(mine)
    seg_col = [jnp.broadcast_to(seg[r][:, None], (length, 128)) for r in rows]
    seg_row = [jnp.broadcast_to(seg[r][None], (8, length)) for r in rows]

    a0 = order.now([own[r] for r in rows])
    kept_a0 = [attn_fwd(False, place, a0[r], seg_col[r], seg_row[r], a0_half, shift0) for r in rows]
    kept_a0, f0_g.got, f1_g.got = order.wait(kept_a0, f0_g.got, f1_g.got)
    f0_g.swap_own()
    f0_g.swap_got()
    a1_g.start()
    f1_g.done()
    f1_g.start()
    f0_g.other_own, f0_g.other_got = order.wait(f0_g.other_own, f0_g.other_got)
    n1 = order.now([kept[4] for kept in kept_a0])
    f0_half = f0_g.halves(place, units, size)
    a1_g.swap_own()
    kept_f0 = [ffn_fwd(False, place, n1[r], f0_half, cup0, gain0, shift0) for r in rows]
    kept_f0, a1_g.other_own, a1_g.got, f1_g.got = order.wait(kept_f0, a1_g.other_own, a1_g.got, f1_g.got)
    a1_g.swap_got()
    f1_g.done()
    f1_g.start()
    a1_g.other_got = order.wait(a1_g.other_got)
    a1 = order.now([kept[4] for kept in kept_f0])
    a1_half = a1_g.halves(place, 2, size)
    f1_g.swap_own()
    kept_a1 = [attn_fwd(True, place, a1[r], seg_col[r], seg_row[r], a1_half, shift1) for r in rows]
    kept_a1, f1_g.other_own, f1_g.got = order.wait(kept_a1, f1_g.other_own, f1_g.got)
    f1_g.swap_got()
    n1 = [kept[4] for kept in kept_a1]
    f1_half = f1_g.halves(place, units, size)
    kept_f1 = [ffn_fwd(False, place, n1[r], f1_half, cup1, gain1, shift1) for r in rows]

    d_y1, g_head = [], 0.0
    for r in rows:
        y1 = kept_f1[r][4]
        proj = dot(y1, head)
        rho = lax.rsqrt(jnp.sum(proj * proj, axis=-1, keepdims=True) + norm_eps)
        c = cot[r].astype(F32)
        d_proj = low(rho * c - rho * rho * rho * proj * jnp.sum(proj * c, axis=-1, keepdims=True))
        g_head = g_head + dot(y1, d_proj, 0, 0)
        d_y1.append(dot(d_proj, head, 1, 1))

    def total(items):
        out = items[0]
        for item in items[1:]:
            out = jax.tree.map(lambda x, y: (x.astype(F32) + y.astype(F32)).astype(x.dtype), out, item)
        return out

    def ffn_back(near_first, d_out, kept_a, kept_f, planes, gain, shift):
        outs = [
            ffn_bwd(near_first, grad_place, d_out[r], *kept_f[r][2:4], *kept_f[r][:2], planes, *kept_a[r][4:6], gain, shift)
            for r in rows
        ]
        keep, send, sums, cup = total([(o[0], o[1], o[3], o[4]) for o in outs])
        keep, send = in_planes(keep, send, place, (units, 0), count, near_first)
        return keep, send, [o[2] for o in outs], sums, cup

    def attn_back(near_first, more, d_out, a, kept, planes):
        outs = [attn_bwd(near_first, more, grad_place, d_out[r], a[r], seg_col[r], seg_row[r], *kept[r][:4], planes) for r in rows]
        keep, send, sums, sumo = total([(o[0], o[1], o[3], o[4]) for o in outs])
        keep, send = in_planes(keep, send, place, (2, 2), count, near_first)
        return keep, send, [o[2] for o in outs], sums, sumo

    keep, send, d_r, sums_f1, g_cup1 = ffn_back(False, d_y1, kept_a1, kept_f1, f1_half, gain1, shift1)
    f1_r = Reduce(order, keep, send)
    f1_r.wait()
    f1_r.start_upper()
    d_r = order.now(d_r)
    keep, send, d_a1, sums_a1, sumo_a1 = attn_back(True, 0, d_r, a1, kept_a1, a1_half)
    d_a1, f1_r.upper = order.wait(d_a1, f1_r.upper)
    a1_r = Reduce(order, keep, send, True)
    f1_r.start_lower()
    f1_r.start_from_upper()
    a1_r.wait()
    a1_r.spare(4)
    a1_r.start_upper()
    d_y0 = order.now([low(item) for item in d_a1])
    keep, send, d_r, sums_f0, g_cup0 = ffn_back(False, d_y0, kept_a0, kept_f0, f0_half, gain0, shift0)
    d_r, f1_r.got, f1_r.ahead, a1_r.upper = order.wait(d_r, f1_r.got, f1_r.ahead, a1_r.upper)
    f0_r = Reduce(order, keep, send)
    f1_r.join()
    f1_r.start()
    a1_r.start_lower()
    f0_r.wait()
    f0_r.start()
    d_r = order.now(d_r)
    keep, send, d_a0, sums_a0, sumo_a0 = attn_back(
        False, PAD if is_small(count) else 0, d_r, a0, kept_a0, a0_half
    )
    d_a0, a1_r.got, f1_r.got, f0_r.got = order.wait(d_a0, a1_r.got, f1_r.got, f0_r.got)

    def small_block(sums_a, sumo, sums_f, g_cup, head_part, core):
        gains = jnp.stack([sums_f[0], sums_f[1]]).reshape(2, count, size).transpose(1, 0, 2)
        shift = jnp.stack([sums_a[0], sums_a[1], sumo[0], sums_f[3], sums_f[4], sums_f[2]])
        shift = shift.reshape(6, count, size).transpose(1, 0, 2)
        flat = jnp.concatenate(
            [gains.reshape(count, -1), shift.reshape(count, -1), g_cup.reshape(count, -1)], axis=1
        )
        flat = jnp.pad(flat, ((0, 0), (0, small_rows * width - small_n)))
        piece = jnp.pad(head_part.reshape(count, -1), ((0, 0), (0, head_rows * width - head_n)))
        block = jnp.concatenate(
            [
                flat.reshape(count, small_rows, width),
                piece.reshape(count, head_rows, width),
                jnp.zeros((count, pad_rows - small_rows - head_rows, width), F32),
            ],
            axis=1,
        )
        return relative(low(block), place, core)

    if is_small(count):
        layer0 = (sums_a0, sumo_a0, sums_f0, g_cup0)
        layer1 = (sums_a1, sumo_a1, sums_f1, g_cup1)
        keep, send = pack_tails(place, cut, layer0, layer1, g_head, keep, send)
    else:
        half_head = g_head.reshape(2, -1, head_w.shape[1])
        tail0 = small_block(sums_a0, sumo_a0, sums_f0, g_cup0, half_head[0], 0)
        tail1 = small_block(sums_a1, sumo_a1, sums_f1, g_cup1, half_head[1], 1)
        keep = jnp.concatenate([keep, jnp.where(first, tail0, tail1)], axis=1)
        send = jnp.concatenate([send, jnp.where(first, tail1, tail0)], axis=1)
    a0_r = Reduce(order, keep, send)
    a0_r.wait()
    a0_r.start()
    f0_r.start()
    f1_r.spare(1)
    f1_r.start()
    a1_r.start_from_upper()
    d_first, d_second = jnp.stack(d_a0), jnp.stack(d_a1)
    a0_r.got, a1_r.ahead, f1_r.got = order.wait(a0_r.got, a1_r.ahead, f1_r.got)
    a0_r.start()
    a1_r.join()
    f0_r.wait()
    f0_r.start()
    a1_r.start()
    got = across(order.now(d_first), 1), across(order.now(d_second), 0)
    a0_r.got, a1_r.got = order.wait(a0_r.got, a1_r.got)
    a0_r.spare(2)
    a0_r.start()
    done_f1 = f1_r.finish()
    a1_r.start()
    f0_r.got, got, done_f1 = order.wait(f0_r.got, got, done_f1)
    f0_r.spare(1)
    f0_r.start()
    input_grads = jnp.where(first, jnp.concatenate([d_first, got[0]]), jnp.concatenate([got[1], d_second]))
    a0_r.got, a1_r.got, input_grads = order.wait(a0_r.got, a1_r.got, input_grads)
    a0_r.spare(1)
    a0_r.start()
    done_a1 = a1_r.finish()
    f0_r.got, done_a1 = order.wait(f0_r.got, done_a1)
    done_f0 = f0_r.finish()

    def unite(zero_part, one_part):
        got = swap(jnp.where(first, one_part, zero_part))
        return jnp.where(first, zero_part, got), jnp.where(first, got, one_part)

    up_plane, down_plane = unite(done_f0, done_f1)
    a0_r.got, up_plane, down_plane = order.wait(a0_r.got, up_plane, down_plane)
    done_a0 = a0_r.finish()
    low_plane, high_plane = unite(done_a0[:cut], done_a1)

    def unit(array, j):
        return array[j * size : (j + 1) * size]

    qkv_grad = jnp.concatenate([unit(low_plane, 0), unit(low_plane, 1), unit(high_plane, 0)], axis=1)
    out_grad = unit(high_plane, 1)
    up_grad = jnp.concatenate([unit(up_plane, j) for j in range(units)], axis=1)
    down_grad = down_plane
    tail = done_a0[cut:]
    if is_small(count):
        gain_grad = tail[None, :2, :size]
        shift_grad = tail[None, 2:8, :size]
        cup_grad = tail[8:9, : up_b.shape[1]]
        head_grad = jnp.concatenate([tail[:8, 384 + 128 * k : 512 + 128 * k] for k in range(3)])
    else:
        flat = tail[:small_rows].reshape(-1)[:small_n]
        gain_grad = flat[:n_g].reshape(gains_w.shape)
        shift_grad = flat[n_g : n_g + n_s].reshape(shifts_w.shape)
        cup_grad = flat[n_g + n_s :].reshape(up_b.shape)
        head_grad = tail[small_rows : small_rows + head_rows].reshape(-1)[:head_n].reshape(head_w.shape)

    return (
        qkv_grad[None],
        out_grad[None],
        up_grad[None],
        down_grad[None],
        gain_grad,
        shift_grad,
        cup_grad,
        head_grad,
        input_grads[None],
    )


def solution(mesh):
    return jax.shard_map(
        shards,
        mesh=mesh,
        in_specs=(
            P("dp", None, None),
            P("dp", None),
            P("dp", None, None),
            P("section", "dp", None),
            P("section", "dp", None),
            P("section", "dp", None),
            P("section", "dp", None),
            P("section", None, "dp"),
            P("section", None, "dp"),
            P("section", "dp"),
            P(("section", "dp"), None),
        ),
        out_specs=(
            P("section", "dp", None),
            P("section", "dp", None),
            P("section", "dp", None),
            P("section", "dp", None),
            P("section", None, "dp"),
            P("section", None, "dp"),
            P("section", "dp"),
            P(("section", "dp"), None),
            P("section", "dp", None, None),
        ),
        check_vma=False,
    )
```

```python
import jax
import jax.numpy as jnp
from jax import lax
from jax.experimental import pallas as pl
from jax.experimental.pallas import tpu as pltpu
from jax.sharding import PartitionSpec as P

HEADS = 12
HDIM = 64
GROUP = 4
BLOCK = 128
PAD = 16
norm_eps = 1e-06
BF = jnp.bfloat16
F32 = jnp.float32
BOTH = ("section", "dp")
SCALE = HDIM ** (-0.5)

ERF_SCALE = 0.425
ERF_POLY = (
    0.11985147519825406,
    0.12072713574380309,
    0.10159474513684189,
    0.12334456743816431,
    -0.0435293372534038,
    0.19486821903107854,
    -0.15132025578595443,
    0.03446332841595847,
)


def dot(left, right, over_left=1, over_right=0):
    return lax.dot_general(
        left, right, (((over_left,), (over_right,)), ((), ())), preferred_element_type=F32
    )


def shape_of(shape, dtype):
    return jax.ShapeDtypeStruct(shape, dtype)


def whole_block(*shape):
    return pl.BlockSpec(shape, lambda g: (0,) * len(shape))


def gelu_pair(u):
    bell = jnp.exp(u * u * -0.5)
    t = 1.0 / (1.0 + (ERF_SCALE * 0.7071067811865476) * jnp.abs(u))
    poly = ERF_POLY[-1]
    for item in ERF_POLY[-2::-1]:
        poly = poly * t + item
    tail = bell * (poly * t)
    cdf = jnp.where(u < 0.0, tail, 1.0 - tail)
    return u * cdf, cdf + u * bell * 0.3989422804014327


def norm_stats(v):
    center = v - jnp.mean(v, axis=-1, keepdims=True)
    t = lax.rsqrt(jnp.mean(center * center, axis=-1, keepdims=True) + norm_eps)
    return center * t, t


def norm_back(dy, n, t, gain):
    dn = dy * gain
    mean = jnp.mean(dn, axis=-1, keepdims=True)
    along = jnp.mean(dn * n, axis=-1, keepdims=True)
    return t * (dn - mean - n * along)


def colsum(v):
    return jnp.sum(v, axis=0, keepdims=True)


def near(b, blocks):
    return max(0, b - 1) * BLOCK, min(blocks, b + 2) * BLOCK


def is_small(count):
    return count == 16


def steps_of(count, core, near_first):
    outer = [4 << j for j in range((count // 4).bit_length() - 1)]
    quad = [1, 2]
    if core:
        quad = [2, 1]
        if is_small(count):
            outer = outer[::-1]
    return quad + outer if near_first else outer + quad


def bit_of(me, mask):
    return (me >> (mask.bit_length() - 1)) & 1


def send_index(chip_z, chip_q, me, core, near_first):
    index = 0
    rel = (chip_z * 4 + chip_q) ^ me
    for j, mask in enumerate(steps_of(16, core, near_first)):
        index = index + bit_of(rel, mask) * (1 << j)
    return index


def each(count, body):
    lax.fori_loop(0, count, lambda j, _: (body(j), 0)[1], 0)


CHIP_BITS = (8, 4, 2, 1)


class Loads:
    def __init__(self, near_first, place_ref, own, other, targets, sem):
        self.near_first, self.place, self.planes = near_first, place_ref, (own, other)
        self.targets, self.sem = targets, sem

    def groups(self, plane, unit):
        order = steps_of(16, plane, self.near_first)
        together = len(self.targets[plane].shape) == 6
        out = []
        for p in range(2):
            for b2 in range(2):
                fixed = {order[3]: bit_of(self.place[0], order[3]) ^ p, order[2]: b2}
                if together:
                    assert plane and not self.near_first
                    fixed.update({8: unit >> 1, 4: unit & 1})
                    bits = [(unit & 1, unit >> 1)]
                elif plane == 0:
                    bits = [()]
                else:
                    bits = [(0,), (1,)]
                for lead in bits:
                    if lead and not together:
                        fixed = {**fixed, order[1]: lead[0]}
                    chips = tuple(fixed.get(mask, slice(None)) for mask in CHIP_BITS)
                    out.append((p, b2, lead, chips if together else (unit,) + chips))
        return out

    def start(self, plane, unit):
        size = self.targets[plane].shape[-2]

        def begin(section):
            pieces = self.planes[0] if plane == section else self.planes[1]
            if len(pieces) == 1:
                source = pieces[0].reshape(*self.targets[plane].shape)
            for k, (p, b2, lead, at) in enumerate(self.groups(plane, unit)):
                if len(pieces) == 1:
                    piece = source.at[at]
                else:
                    piece = pieces[1 + b2] if p and len(pieces) == 3 else pieces[p].at[b2]
                    for bit in lead:
                        piece = piece.at[bit]
                    if len(at) == 5:
                        rows = pl.ds(pl.multiple_of(unit * size, PAD), size)
                        piece = piece.at[(slice(None),) * (len(piece.shape) - 2) + (rows,)]
                pltpu.make_async_copy(piece, self.targets[plane].at[at], self.sem.at[plane, unit, k]).start()

        by_section(self.place[1], begin)

    def wait(self, plane, unit):
        for k, (_, _, _, at) in enumerate(self.groups(plane, unit)):
            to = self.targets[plane].at[at]
            pltpu.make_async_copy(to, to, self.sem.at[plane, unit, k]).wait()


def halves_view(pieces):
    if len(pieces) == 1:
        return pieces
    return [item.reshape((2,) * (item.shape[0].bit_length() - 1) + item.shape[1:]) for item in pieces]


def block_of(b, pair):
    return slice(b * BLOCK, (b + 1) * BLOCK), slice(pair * 2 * HDIM, (pair + 1) * 2 * HDIM)


def two_heads(pair, lane):
    zero = jnp.zeros_like(pair)
    return jnp.concatenate([jnp.where(lane < HDIM, pair, zero), jnp.where(lane >= HDIM, pair, zero)])


def attn_fwd_kernel(near_first, halves, place_ref, *refs):
    own, other = refs[:halves], refs[halves : 2 * halves]
    a_ref, sq_ref, sk_ref, bias_ref, shift_ref = refs[2 * halves : 2 * halves + 5]
    q_ref, k_ref, v_ref, o_ref, n_ref, t_ref, acc, low_w, high_w, sem = refs[2 * halves + 5 :]
    step = pl.program_id(0)
    length, width = a_ref.shape
    blocks = length // BLOCK
    a = a_ref[...]
    loads = Loads(near_first, place_ref, own, other, (low_w, high_w), sem)

    @pl.when(step == 0)
    def _():
        for plane, unit in ((0, 0), (0, 1), (1, 0), (1, 1)):
            loads.start(plane, unit)
        for plane, unit in ((0, 0), (0, 1), (1, 0)):
            loads.wait(plane, unit)

    cols = GROUP * HDIM
    here = pl.ds(pl.multiple_of(step * cols, cols), cols)

    def column(ref, j):
        return ref[j, :, :, :, :, :, here].reshape(width, cols)

    q_ref[...] = (dot(a, column(low_w, 0)) + bias_ref[2:3]).astype(BF)
    k_ref[...] = dot(a, column(low_w, 1)).astype(BF)
    v_ref[...] = (dot(a, column(high_w, 0)) + bias_ref[3:4]).astype(BF)
    lane = lax.broadcasted_iota(jnp.int32, (BLOCK, 2 * HDIM), 1)
    tiles = [(b, pair) for b in range(blocks) for pair in range(GROUP // 2)]

    def scores_of(b, pair):
        lo, hi = near(b, blocks)
        rows, lanes = block_of(b, pair)
        same = sq_ref[rows, 0:1] == sk_ref[0:1, lo:hi]
        scores = dot(two_heads(q_ref[rows, lanes] * SCALE, lane), k_ref[lo:hi, lanes], 1, 1)
        return jnp.where(jnp.concatenate([same, same]), scores, -1000000000.0)

    ahead = scores_of(*tiles[0])
    for j, (b, pair) in enumerate(tiles):
        lo, hi = near(b, blocks)
        rows, lanes = block_of(b, pair)
        scores = ahead
        if j + 1 < len(tiles):
            ahead = scores_of(*tiles[j + 1])
        grown = jnp.exp(scores - jnp.max(scores, axis=-1, keepdims=True))
        scale = 1.0 / jnp.sum(grown, axis=-1, keepdims=True)
        out = dot((grown * scale).astype(BF), v_ref[lo:hi, lanes])
        o_ref[rows, lanes] = jnp.where(lane < HDIM, out[:BLOCK], out[BLOCK:]).astype(BF)
    @pl.when(step == 0)
    def _():
        loads.wait(1, 1)

    part = dot(o_ref[...], high_w.at[1].reshape(width, width)[here, :])

    @pl.when(step == 0)
    def _():
        acc[...] = a.astype(F32) + shift_ref[4:5] + part

    @pl.when(step != 0)
    def _():
        acc[...] += part

    @pl.when(step == pl.num_programs(0) - 1)
    def _():
        n, t = norm_stats(acc[...])
        n_ref[...] = n
        t_ref[...] = jnp.broadcast_to(t, t_ref.shape)


SCALARS = pl.BlockSpec(memory_space=pltpu.SMEM)
NO_COST = pl.CostEstimate(flops=0, bytes_accessed=0, transcendentals=0)


ANYWHERE = pl.BlockSpec(memory_space=pl.ANY)


def attn_fwd(near_first, place, a, seg_col, seg_row, planes, shift):
    length, width = a.shape
    cols = GROUP * HDIM
    group = pl.BlockSpec((length, cols), lambda g: (0, g))
    half = (2, 2, 2, 2, 2, width // 16, width)
    halves = len(planes[0])
    return pl.pallas_call(
        lambda *refs: attn_fwd_kernel(near_first, halves, *refs),
        grid=(HEADS // GROUP,),
        in_specs=[SCALARS]
        + [ANYWHERE] * (2 * halves)
        + [whole_block(length, width), whole_block(length, 128), whole_block(8, length)]
        + [pl.BlockSpec((8, cols), lambda g: (0, g)), whole_block(8, width)],
        out_specs=[group] * 4 + [whole_block(length, width), whole_block(length, 128)],
        out_shape=[shape_of((length, width), BF)] * 4
        + [shape_of((length, width), F32), shape_of((length, 128), F32)],
        scratch_shapes=[
            pltpu.VMEM((length, width), F32),
            pltpu.VMEM(half, BF),
            pltpu.VMEM(half, BF),
            pltpu.SemaphoreType.DMA((2, 2, 8)),
        ],
        cost_estimate=NO_COST,
        name="attn_fwd",
    )(place, *halves_view(planes[0]), *halves_view(planes[1]), a, seg_col, seg_row, shift, shift)


def ffn_fwd_kernel(near_first, halves, place_ref, *refs):
    own, other = refs[:halves], refs[halves : 2 * halves]
    n1_ref, cup_ref, gain_ref, shift_ref = refs[2 * halves : 2 * halves + 4]
    g_ref, gp_ref, n_ref, t_ref, y_ref = refs[2 * halves + 4 : 2 * halves + 9]
    h1, acc, up_w, down_w, sem = refs[2 * halves + 9 :]
    step = pl.program_id(0)
    width = n1_ref.shape[1]
    loads = Loads(near_first, place_ref, own, other, (up_w, down_w), sem)
    units = up_w.shape[0]

    @pl.when(step == 0)
    def _():
        loads.start(0, 0)
        loads.start(1, 0)

    @pl.when(step == 0)
    def _():
        hidden = n1_ref[...] * gain_ref[0:1] + shift_ref[6:7]
        h1[...] = hidden.astype(BF)
        acc[...] = hidden + shift_ref[5:6]

    loads.wait(0, step)

    @pl.when(step + 1 < units)
    def _():
        loads.start(0, step + 1)
        loads.start(1, step + 1)

    loads.wait(1, step)
    up = up_w[step].reshape(width, width)
    down = down_w[step >> 1, step & 1].reshape(width, width)
    wide = 256
    parts = h1.shape[1] // wide

    def upper(j):
        cols = slice(j * wide, (j + 1) * wide)
        return dot(h1[...], up[:, cols]) + cup_ref[0, :, cols]

    ahead = upper(0)
    total = acc[...]
    for j in range(parts):
        cols = slice(j * wide, (j + 1) * wide)
        here = ahead
        if j + 1 < parts:
            ahead = upper(j + 1)
        g, slope = gelu_pair(here)
        g = g.astype(BF)
        g_ref[:, cols] = g
        gp_ref[:, cols] = slope.astype(BF)
        total = total + dot(g, down[cols])
    acc[...] = total

    @pl.when(step == pl.num_programs(0) - 1)
    def _():
        n, t = norm_stats(acc[...])
        n_ref[...] = n
        t_ref[...] = jnp.broadcast_to(t, t_ref.shape)
        y_ref[...] = (n * gain_ref[1:2] + shift_ref[7:8]).astype(BF)


def ffn_fwd(near_first, place, n1, planes, cup, gain, shift):
    length, width = n1.shape
    units = cup.shape[0]
    column = pl.BlockSpec((length, width), lambda g: (0, g))
    up = (units, 2, 2, 2, 2, width // 16, width)
    down = (2, 2, 2, 2, units * width // 16, width)
    halves = len(planes[0])
    return pl.pallas_call(
        lambda *refs: ffn_fwd_kernel(near_first, halves, *refs),
        grid=(units,),
        in_specs=[SCALARS]
        + [ANYWHERE] * (2 * halves)
        + [
            whole_block(length, width),
            pl.BlockSpec((1, 1, width), lambda g: (g, 0, 0)),
            whole_block(8, width),
            whole_block(8, width),
        ],
        out_specs=[column, column, whole_block(length, width), whole_block(length, 128), whole_block(length, width)],
        out_shape=[shape_of((length, units * width), BF)] * 2
        + [shape_of((length, width), F32), shape_of((length, 128), F32), shape_of((length, width), BF)],
        scratch_shapes=[
            pltpu.VMEM((length, width), BF),
            pltpu.VMEM((length, width), F32),
            pltpu.VMEM(up, BF),
            pltpu.VMEM(down, BF),
            pltpu.SemaphoreType.DMA((2, units, 4)),
        ],
        cost_estimate=NO_COST,
        name="ffn_fwd",
    )(place, *halves_view(planes[0]), *halves_view(planes[1]), n1, cup, gain, shift)


def by_section(section, action):
    for plane in range(2):
        pl.when(section == plane)(lambda plane=plane: action(plane))


def ffn_bwd_kernel(near_first, halves, place_ref, *refs):
    own, other = refs[:halves], refs[halves : 2 * halves]
    dy_ref, n2_ref, t2_ref, g_ref, gp_ref, n1_ref, t1_ref, gain_ref, shift_ref = refs[2 * halves : 2 * halves + 9]
    keep_ref, high_ref, low_ref, dr1_ref, sums_ref, cup_ref = refs[2 * halves + 9 : 2 * halves + 15]
    h1, df, acc, gup, gdown, up_w, down_w, sem, load_sem = refs[2 * halves + 15 :]
    step = pl.program_id(0)
    loads = Loads(near_first, place_ref, own, other, (up_w, down_w), load_sem)

    @pl.when(step == 0)
    def _():
        loads.start(1, 0)
        loads.start(0, 0)

    last = pl.num_programs(0) - 1
    quads = outer = 4
    width = h1.shape[1]
    size = width // (quads * outer)

    @pl.when(step == 0)
    def _():
        n2 = n2_ref[...]
        dy = dy_ref[...].astype(F32)
        dr2 = norm_back(dy, n2, t2_ref[:, 0:1], gain_ref[1:2])
        low = dr2.astype(BF)
        df[...] = low
        acc[...] = dr2
        h1[...] = (n1_ref[...] * gain_ref[0:1] + shift_ref[6:7]).astype(BF)
        sums_ref[...] = jnp.zeros_like(sums_ref)
        sums_ref[1:2] = colsum(dy * n2)
        sums_ref[2:3] = colsum(dy)
        sums_ref[3:4] = colsum(low.astype(F32))

    loads.wait(1, step)
    loads.wait(0, step)

    @pl.when(step < last)
    def _():
        loads.start(1, step + 1)
        loads.start(0, step + 1)

    d = df[...]
    down = dot(g_ref[...], d, 0, 0).astype(BF)
    tall = width // quads
    for q in range(quads):
        gdown[send_index(step, q, place_ref[0], 1, near_first)] = down[q * tall : (q + 1) * tall]
    du = (dot(d, down_w[step >> 1, step & 1].reshape(width, width), 1, 1) * gp_ref[...].astype(F32)).astype(BF)
    cup_ref[0] = colsum(du.astype(F32))
    up = dot(h1[...], du, 0, 0).astype(BF)
    for chip in range(quads * outer):
        at = send_index(chip // quads, chip % quads, place_ref[0], 0, near_first)
        gup[step, at] = up[chip * size : (chip + 1) * size]
    acc[...] += dot(du, up_w[step].reshape(width, width), 1, 1)

    def up_copies(section, j):
        rows = pl.ds(pl.multiple_of(j * size, PAD), size)
        if section == 0:
            return [pltpu.make_async_copy(gup.at[j], keep_ref.at[:, rows, :], sem.at[j, 0])]
        return [
            pltpu.make_async_copy(gup.at[j, :8], low_ref.at[:, rows, :], sem.at[j, 0]),
            pltpu.make_async_copy(gup.at[j, 8:], high_ref.at[:, rows, :], sem.at[j, 1]),
        ]

    def down_copies(section, j, start):
        for q in range(quads):
            at = send_index(j, q, place_ref[0], 1, near_first)
            if section == 1:
                copy = pltpu.make_async_copy(gdown.at[at], keep_ref.at[at], sem.at[j, 2 + q])
                copy.start() if start else copy.wait()
            elif not start:
                pltpu.make_async_copy(gdown.at[at], low_ref.at[0], sem.at[j, 2 + q]).wait()
            else:
                for part, ref in enumerate((low_ref, high_ref)):
                    @pl.when(at >> 3 == part)
                    def _():
                        pltpu.make_async_copy(gdown.at[at], ref.at[at & 7], sem.at[j, 2 + q]).start()

    def begin(section):
        for item in up_copies(section, step):
            item.start()
        down_copies(section, step, True)

    by_section(place_ref[1], begin)

    @pl.when(step == last)
    def _():
        dh = acc[...]
        n1 = n1_ref[...]
        dr1_ref[...] = norm_back(dh, n1, t1_ref[:, 0:1], gain_ref[0:1])
        sums_ref[0:1] = colsum(dh * n1)
        sums_ref[4:5] = colsum(dh)

        def finish(section):
            def one(j):
                for item in up_copies(section, j):
                    item.wait()
                down_copies(section, j, False)

            each(gup.shape[0], one)

        by_section(place_ref[1], finish)


def ffn_bwd(near_first, place, dy, n2, t2, g, gp, planes, n1, t1, gain, shift):
    length, width = n1.shape
    units = g.shape[1] // width
    outer, size = 4, width // 16
    halves = len(planes[0])
    up = (units, 2, 2, 2, 2, size, width)
    down = (2, 2, 2, 2, units * size, width)
    column = pl.BlockSpec((length, width), lambda g: (0, g))
    chunk, half_chunk = [shape_of((n, units * size, width), BF) for n in (16, 8)]
    return pl.pallas_call(
        lambda *refs: ffn_bwd_kernel(near_first, halves, *refs),
        grid=(units,),
        in_specs=[
            SCALARS,
            *[ANYWHERE] * (2 * halves),
            whole_block(length, width),
            whole_block(length, width),
            whole_block(length, 128),
            column,
            column,
            whole_block(length, width),
            whole_block(length, 128),
            whole_block(8, width),
            whole_block(8, width),
        ],
        out_specs=[
            ANYWHERE,
            ANYWHERE,
            ANYWHERE,
            whole_block(length, width),
            whole_block(8, width),
            pl.BlockSpec((1, 1, width), lambda g: (g, 0, 0)),
        ],
        out_shape=[chunk, half_chunk, half_chunk, shape_of((length, width), F32), shape_of((8, width), F32), shape_of((units, 1, width), F32)],
        scratch_shapes=[
            pltpu.VMEM((length, width), BF),
            pltpu.VMEM((length, width), BF),
            pltpu.VMEM((length, width), F32),
            pltpu.VMEM((units, 16, size, width), BF),
            pltpu.VMEM((16, units * size, width), BF),
            pltpu.VMEM(up, BF),
            pltpu.VMEM(down, BF),
            pltpu.SemaphoreType.DMA((units, 6)),
            pltpu.SemaphoreType.DMA((2, units, 4)),
        ],
        cost_estimate=NO_COST,
        name="ffn_bwd",
    )(place, *halves_view(planes[0]), *halves_view(planes[1]), dy, n2, t2, g, gp, n1, t1, gain, shift)


def attn_bwd_kernel(near_first, halves, place_ref, *refs):
    own, other = refs[:halves], refs[halves : 2 * halves]
    dr_ref, a_ref, sq_ref, sk_ref, q_ref, k_ref, v_ref, o_ref = refs[2 * halves : 2 * halves + 8]
    keep_ref, high_ref, low_ref, da_ref, sums_ref, sumo_ref = refs[2 * halves + 8 : 2 * halves + 14]
    dat, do_sc, dq, dk, dv, grads, low_w, high_w, sem, load_sem = refs[2 * halves + 14 :]
    step = pl.program_id(0)
    loads = Loads(near_first, place_ref, own, other, (low_w, high_w), load_sem)

    @pl.when(step == 0)
    def _():
        for plane, unit in ((1, 1), (0, 0), (0, 1), (1, 0)):
            loads.start(plane, unit)

    length, width = a_ref.shape
    blocks = length // BLOCK
    quads = outer = 4
    size = width // (quads * outer)
    cols = GROUP * HDIM

    @pl.when(step == 0)
    def _():
        low = dr_ref[...].astype(BF)
        dat[...] = low
        da_ref[...] = dr_ref[...]
        sumo_ref[...] = jnp.zeros_like(sumo_ref)
        sumo_ref[0:1] = colsum(low.astype(F32))

    d = dat[...]
    grad_o = dot(o_ref[...], d, 0, 0).astype(BF)

    @pl.when(step == 0)
    def _():
        loads.wait(1, 1)

    now = pl.ds(pl.multiple_of(step * cols, cols), cols)
    do_sc[...] = dot(d, high_w.at[1].reshape(width, width)[now, :], 1, 1).astype(BF)
    dk[...] = jnp.zeros_like(dk)
    dv[...] = jnp.zeros_like(dv)
    lane = lax.broadcasted_iota(jnp.int32, (BLOCK, 2 * HDIM), 1)
    tiles = [(b, pair) for b in range(blocks) for pair in range(GROUP // 2)]

    def products(b, pair):
        lo, hi = near(b, blocks)
        rows, lanes = block_of(b, pair)
        same = sk_ref[lo:hi, 0:1] == sq_ref[0:1, rows]
        query = two_heads(q_ref[rows, lanes] * SCALE, lane)
        d_out = two_heads(do_sc[rows, lanes], lane)
        scores = dot(k_ref[lo:hi, lanes], query, 1, 1)
        scores = jnp.where(jnp.concatenate([same, same], axis=1), scores, -1000000000.0)
        return query, d_out, scores, dot(v_ref[lo:hi, lanes], d_out, 1, 1)

    ahead = products(*tiles[0])
    for j, (b, pair) in enumerate(tiles):
        lo, hi = near(b, blocks)
        rows, lanes = block_of(b, pair)
        query, d_out, scores, d_probs = ahead
        if j + 1 < len(tiles):
            ahead = products(*tiles[j + 1])
        grown = jnp.exp(scores - jnp.max(scores, axis=0, keepdims=True))
        probs = grown * (1.0 / jnp.sum(grown, axis=0, keepdims=True))
        d_scores = probs * (d_probs - jnp.sum(probs * d_probs, axis=0, keepdims=True))
        d_scores = d_scores.astype(BF)
        dv[lo:hi, lanes] += dot(probs.astype(BF), d_out)
        dk[lo:hi, lanes] += dot(d_scores, query)
        d_query = dot(d_scores, k_ref[lo:hi, lanes], 0, 0)
        dq[rows, lanes] = jnp.where(lane < HDIM, d_query[:BLOCK], d_query[BLOCK:]) * SCALE
    a = a_ref[...]
    out = da_ref[...]
    lows = (dq[...].astype(BF), dk[...].astype(BF), dv[...].astype(BF))
    made = []

    @pl.when(step == 0)
    def _():
        for plane, unit in ((0, 0), (0, 1), (1, 0)):
            loads.wait(plane, unit)

    for low, (w_ref, j) in zip(lows, ((low_w, 0), (low_w, 1), (high_w, 0))):
        made.append(dot(a, low, 0, 0).astype(BF))
        out = out + dot(low, w_ref[j, :, :, :, :, :, now].reshape(width, cols), 1, 1)
    da_ref[...] = out
    sums_ref[...] = jnp.zeros_like(sums_ref)
    sums_ref[0:1] = colsum(lows[0].astype(F32))
    sums_ref[1:2] = colsum(lows[2].astype(F32))
    steps = HEADS // GROUP

    def place_of(chip, core):
        return send_index(chip // quads, chip % quads, place_ref[0], core, near_first)

    for unit in range(3):
        for chip in range(quads * outer):
            grads[unit, place_of(chip, unit // 2), :, now] = made[unit][chip * size : (chip + 1) * size]
    for j in range(steps):
        @pl.when(step == j)
        def _(j=j):
            for chip in range(quads * outer):
                start, end = max(chip * size, j * cols), min((chip + 1) * size, (j + 1) * cols)
                if start < end:
                    rows = slice(start - chip * size, end - chip * size)
                    grads[3, place_of(chip, 1), rows, :] = grad_o[start - j * cols : end - j * cols]

    @pl.when(step == steps - 1)
    def _():
        def move(section):
            copies = []
            for unit in range(4):
                rows = slice((unit % 2) * size, (unit % 2 + 1) * size)
                if unit // 2 == section:
                    copies.append(pltpu.make_async_copy(grads.at[unit], keep_ref.at[:, rows, :], sem.at[unit, 0]))
                else:
                    copies += [
                        pltpu.make_async_copy(grads.at[unit, :8], low_ref.at[:, rows, :], sem.at[unit, 0]),
                        pltpu.make_async_copy(grads.at[unit, 8:], high_ref.at[:, rows, :], sem.at[unit, 1]),
                    ]
            for item in copies:
                item.start()
            for item in copies:
                item.wait()

        by_section(place_ref[1], move)


def attn_bwd(near_first, more, place, dr, a, seg_col, seg_row, q, k, v, o, planes):
    length, width = a.shape
    outer, size = 4, width // 16
    halves = len(planes[0])
    half = (2, 2, 2, 2, 2, size, width)
    cols = GROUP * HDIM
    group = pl.BlockSpec((length, cols), lambda g: (0, g))
    chunk, half_chunk = [shape_of((n, 2 * size + more, width), BF) for n in (16, 8)]
    return pl.pallas_call(
        lambda *refs: attn_bwd_kernel(near_first, halves, *refs),
        grid=(HEADS // GROUP,),
        in_specs=[
            SCALARS,
            *[ANYWHERE] * (2 * halves),
            whole_block(length, width),
            whole_block(length, width),
            whole_block(8, length),
            whole_block(length, 128),
        ]
        + [group] * 4,
        out_specs=[
            ANYWHERE,
            ANYWHERE,
            ANYWHERE,
            whole_block(length, width),
            pl.BlockSpec((8, cols), lambda g: (0, g)),
            whole_block(8, width),
        ],
        out_shape=[chunk, half_chunk, half_chunk, shape_of((length, width), F32), shape_of((8, width), F32), shape_of((8, width), F32)],
        scratch_shapes=[pltpu.VMEM((length, width), BF), pltpu.VMEM((length, cols), BF)]
        + [pltpu.VMEM((length, cols), F32)] * 3
        + [pltpu.VMEM((4, 16, size, width), BF), pltpu.VMEM(half, BF), pltpu.VMEM(half, BF)]
        + [pltpu.SemaphoreType.DMA((4, 2)), pltpu.SemaphoreType.DMA((2, 2, 8))],
        cost_estimate=NO_COST,
        name="attn_bwd",
    )(place, *halves_view(planes[0]), *halves_view(planes[1]), dr, a, seg_row, seg_col, q, k, v, o)


def flip(value, mask, other=None):
    count = lax.axis_size("dp")
    masks = (mask, mask if other is None else other)
    pairs = [(s * count + i, s * count + (i ^ masks[s])) for s in range(2) for i in range(count)]
    return lax.ppermute(value, BOTH, pairs)


def swap(value):
    count = lax.axis_size("dp")
    pairs = [(s * count + i, (1 - s) * count + i) for s in range(2) for i in range(count)]
    return lax.ppermute(value, BOTH, pairs)


def across(value, source):
    count = lax.axis_size("dp")
    return lax.ppermute(value, BOTH, [(source * count + i, (1 - source) * count + i) for i in range(count)])


class Order:
    def __init__(self, mark):
        self.mark = mark

    def wait(self, *values):
        leaves, tree = jax.tree.flatten(values)
        *leaves, self.mark = lax.optimization_barrier((*leaves, self.mark))
        out = jax.tree.unflatten(tree, leaves)
        return out[0] if len(values) == 1 else out

    def now(self, *values):
        leaves, tree = jax.tree.flatten(values)
        leaves = lax.optimization_barrier((*leaves, self.mark))[:-1]
        out = jax.tree.unflatten(tree, leaves)
        return out[0] if len(values) == 1 else out


class Gather:
    def __init__(self, order, block, near_first=False):
        self.order, self.own, self.near_first = order, block[None], near_first
        self.left = list(zip(*[steps_of(lax.axis_size("dp"), core, near_first) for core in range(2)]))

    def start(self):
        self.got = flip(self.order.now(self.own), *self.left[0])

    def start_part(self, part):
        half = self.own.shape[0] // 2
        return flip(self.order.now(self.own[part * half : (part + 1) * half]), *self.left[0])

    def done(self):
        masks = self.left.pop(0)
        high = (lax.axis_index("dp") & jnp.where(lax.axis_index("section") == 0, *masks)) != 0
        own, got = self.own, self.got
        self.own = jnp.where(high, jnp.concatenate([got, own]), jnp.concatenate([own, got]))

    def spare(self, steps):
        while len(self.left) > steps:
            self.start()
            self.done()

    def wait(self):
        self.got = self.order.wait(self.got)

    def swap_own(self):
        self.other_own = swap(self.order.now(self.own))

    def swap_got(self):
        self.other_got = jax.tree.map(lambda item: swap(self.order.now(item)), self.got)

    def halves(self, place, units, size):
        pairs = tuple(
            (own,) + (got if isinstance(got, tuple) else (got,))
            for own, got in ((self.own, self.got), (self.other_own, self.other_got))
        )
        if is_small(lax.axis_size("dp")):
            return pairs
        return natural_planes(place, units, size, self.near_first, *pairs)


def natural_planes(place, units, size, near_first, own, other):
    count = lax.axis_size("dp")
    out = []
    for section, halves in ((place[1], own), (1 - place[1], other)):
        both = jnp.concatenate(halves)
        at = []
        for core in range(2):
            order = steps_of(count, core, near_first)
            chips = jnp.arange(count)
            index = sum(bit_of(chips, mask) << j for j, mask in enumerate(order))
            at.append(index ^ (bit_of(place[0], order[-1]) << (len(order) - 1)))
        whole = jnp.take(both, jnp.where(section == 0, *at), axis=0)
        rows, width = whole.shape[1:]
        if size:
            by_unit = jnp.stack([whole[:, j * size : (j + 1) * size].reshape(width, width) for j in range(units)])
            if units != 2:
                flat = whole.reshape(units, width, width)
                by_unit = jnp.where(section == 0, by_unit.reshape(flat.shape), flat)
            whole = by_unit.reshape(units, 4, 4, width // 16, width)
        out.append((whole,))
    return out


def tail_kernel(cut, place_ref, *refs):
    halves, (vec_ref, cup_ref, head_ref, pieces, sem) = refs[:4], refs[4:]

    def move(section):
        for start in (True, False):
            for plane in range(2):
                order = steps_of(16, plane, False)
                for p in range(2):
                    source = halves[p if plane == section else 2 + p].at[:, cut:, :]

                    def by_index(index):
                        chip = sum(bit_of(index, 1 << j) * order[j] for j in range(3))
                        chip = chip + order[3] * (bit_of(place_ref[0], order[3]) ^ p)
                        to = pieces.at[plane, chip >> 2, chip & 3]
                        copy = pltpu.make_async_copy(source.at[index], to, sem.at[plane, 8 * p + index])
                        copy.start() if start else copy.wait()

                    each(8, by_index)

    by_section(place_ref[1], move)
    size = vec_ref.shape[2] // 16
    wide = cup_ref.shape[1] * size
    height = head_ref.shape[0] // 32
    for plane in range(2):
        for chip in range(16):
            piece = pieces[plane, chip // 4, chip % 4].astype(F32)
            vec_ref[plane, :, chip * size : (chip + 1) * size] = piece[:8, :size]
            at = (chip % 4) * wide
            cup_ref[plane, chip // 4, :, at : at + wide] = piece[8:9, :wide]
            for k in range(height // 8):
                row = (plane * 16 + chip) * height + 8 * k
                head_ref[row : row + 8, :] = piece[:8, 384 + 128 * k : 512 + 128 * k]


def tails_of(place, cut, units, own, other):
    width = own[0].shape[2]
    return pl.pallas_call(
        lambda *refs: tail_kernel(cut, *refs),
        in_specs=[SCALARS] + [ANYWHERE] * 4,
        out_specs=[pl.BlockSpec(memory_space=pltpu.VMEM)] * 3,
        out_shape=[shape_of((2, 8, width), F32), shape_of((2, units, 1, width), F32), shape_of((width, 128), F32)],
        scratch_shapes=[pltpu.VMEM((2, 4, 4, PAD, width), BF), pltpu.SemaphoreType.DMA((2, 16))],
        cost_estimate=NO_COST,
        name="tails",
    )(place, *own, *other)


def natural_tails(place, cut, own, other):
    own, other = jax.tree.map(lambda item: item[:, cut:], (own, other))
    (mine,), (there,) = natural_planes(place, 0, 0, False, own, other)
    first = place[1] == 0
    return jnp.where(first, mine, there), jnp.where(first, there, mine)


def pack_kernel(cut, place_ref, *refs):
    sums = (refs[0:4], refs[4:8])
    head_ref, _, _, _, keep_ref, high_ref, low_ref, pieces, sem = refs[8:]
    width = pieces.shape[3]
    size = width // 16
    height = head_ref.shape[0] // 32
    pieces[...] = jnp.zeros_like(pieces)
    for plane, (attn, out, ffn, cup) in enumerate(sums):
        wide = cup.shape[0] * size
        rows = [ffn[0:1], ffn[1:2], attn[0:1], attn[1:2], out[0:1], ffn[3:4], ffn[4:5], ffn[2:3]]
        vec = jnp.concatenate(rows)
        for chip in range(16):
            pieces[plane, chip, :8, :size] = vec[:, chip * size : (chip + 1) * size].astype(BF)
            at = (chip % 4) * wide
            pieces[plane, chip, 8:9, :wide] = cup[chip // 4, :, at : at + wide].astype(BF)
            for k in range(height // 8):
                row = (plane * 16 + chip) * height + 8 * k
                pieces[plane, chip, :8, 384 + 128 * k : 512 + 128 * k] = head_ref[row : row + 8, :].astype(BF)

    def move(section):
        for plane in range(2):
            def by_chip(chip):
                at = send_index(chip >> 2, chip & 3, place_ref[0], plane, False)
                source, this = pieces.at[plane, chip], sem.at[plane, chip]
                if plane == section:
                    pltpu.make_async_copy(source, keep_ref.at[at, cut:, :], this).start()
                    return
                for part, ref in enumerate((low_ref, high_ref)):
                    @pl.when(at >> 3 == part)
                    def _():
                        pltpu.make_async_copy(source, ref.at[at & 7, cut:, :], this).start()

            each(16, by_chip)
        for plane in range(2):
            def wait(chip):
                pltpu.make_async_copy(pieces.at[plane, chip], keep_ref.at[0, cut:, :], sem.at[plane, chip]).wait()

            each(16, wait)

    by_section(place_ref[1], move)


def pack_tails(place, cut, layer0, layer1, g_head, chunk):
    return pl.pallas_call(
        lambda *refs: pack_kernel(cut, *refs),
        in_specs=[SCALARS] + [pl.BlockSpec(memory_space=pltpu.VMEM)] * 9 + [ANYWHERE] * 3,
        out_specs=[ANYWHERE] * 3,
        out_shape=[shape_of(item.shape, BF) for item in chunk],
        input_output_aliases={10: 0, 11: 1, 12: 2},
        scratch_shapes=[pltpu.VMEM((2, 16, PAD, chunk[0].shape[2]), BF), pltpu.SemaphoreType.DMA((2, 16))],
        cost_estimate=NO_COST,
        name="pack",
    )(place, *layer0, *layer1, g_head, *chunk)


def in_chips(chunk, place, units, count, core, near_first):
    chips = jnp.arange(16)
    at = sum(bit_of(chips, mask) << j for j, mask in enumerate(steps_of(16, core, near_first)))
    chunk = jnp.take(chunk, at, axis=0)
    width = chunk.shape[2]
    if units:
        natural = chunk.reshape(16, units, -1, width).transpose(1, 0, 2, 3).reshape(units, count, -1, width)
        natural = natural.transpose(1, 0, 2, 3).reshape(count, -1, width)
    else:
        natural = chunk.reshape(count, -1, width)
    return relative(natural, place, core, near_first)


def in_planes(keep, high, low_half, place, units, count, near_first):
    if is_small(count):
        return keep, high, low_half
    send = jnp.concatenate([low_half, high])
    first = place[1] == 0
    keeps, sends = [
        [in_chips(item, place, units[core], count, core, near_first) for core in range(2)] for item in (keep, send)
    ]
    return (jnp.where(first, *keeps),) + in_halves(jnp.where(first, sends[1], sends[0]))


def in_halves(send):
    half = send.shape[0] // 2
    return send[half:], send[:half]


def relative(block, place, core, near_first=False):
    order = steps_of(block.shape[0], core, near_first)
    index = jnp.arange(block.shape[0])
    chips = sum(bit_of(index, 1 << j) * mask for j, mask in enumerate(order))
    return jnp.take(block, chips ^ place[0], axis=0)


def low(value):
    return value.astype(BF)


def add_low(terms, start, count):
    return low(sum(item[start : start + count].astype(F32) for item in terms))


class Reduce:
    def __init__(self, order, chunk, near_first=False):
        keep, high, low_half = chunk
        self.order = order
        self.left = list(zip(*[steps_of(lax.axis_size("dp"), core, near_first) for core in range(2)]))
        self.keep = keep
        self.got = swap(order.now(high))
        self.there = swap(order.now(low_half))
        self.terms = None

    def wait(self):
        self.got = self.order.wait(self.got)

    def start(self):
        if self.terms is None:
            half = self.got.shape[0]
            sent = add_low([self.keep[half:], self.got], 0, half)
            self.terms = [self.keep[:half], self.there]
        else:
            self.terms.append(self.got)
            half = self.got.shape[0] // 2
            sent = add_low(self.terms, half, half)
        self.got = flip(self.order.now(sent), *self.left.pop())

    def start_upper(self):
        self.half = self.got.shape[0]
        self.part = self.half // 2
        self.masks = self.left.pop()
        sent = add_low([self.keep[self.half :], self.got], self.part, self.part)
        self.upper = flip(self.order.now(sent), *self.masks)

    def start_lower(self):
        sent = add_low([self.keep[self.half :], self.got], 0, self.part)
        self.got = flip(self.order.now(sent), *self.masks)
        self.terms = [self.keep[: self.half], self.there]

    def start_from_upper(self):
        part = self.part
        terms = [item[part : 2 * part] for item in self.terms] + [self.upper]
        self.ahead = flip(self.order.now(add_low(terms, 0, part)), *self.left.pop())

    def join(self):
        self.terms.append(self.got)
        self.got = self.ahead

    def spare(self, steps):
        while len(self.left) > steps:
            self.start()

    def finish(self):
        return sum(item[0].astype(F32) for item in self.terms + [self.got])


def shards(tokens, segment_ids, cotangent, qkv_w, out_w, up_w, down_w, gains_w, shifts_w, up_b, head_w):
    count = lax.axis_size("dp")
    section = lax.axis_index("section")
    me = lax.axis_index("dp")
    first = section == 0
    place = jnp.stack([me, section]).astype(jnp.int32)
    grad_place = place if is_small(count) else jnp.stack([jnp.zeros_like(section), section]).astype(jnp.int32)
    rows_dev, length, width = tokens.shape
    mine = rows_dev // 2
    size = width // count
    ff = up_w.shape[2]
    units = ff // width

    def cols(array, n):
        return [array[:, j * width : (j + 1) * width] for j in range(n)]

    def planes_of(low_units, high_units):
        low_plane, high_plane = jnp.concatenate(low_units), jnp.concatenate(high_units)
        got = swap(jnp.where(first, high_plane, low_plane))
        return jnp.where(first, low_plane, got), jnp.where(first, got, high_plane)

    q_u, k_u, v_u = cols(low(qkv_w[0]), 3)
    a_zero, a_one = planes_of([q_u, k_u], [v_u, low(out_w[0])])
    f_zero, f_one = planes_of(cols(low(up_w[0]), units), [low(down_w[0])])
    small = low(jnp.concatenate([gains_w.reshape(-1), shifts_w.reshape(-1), up_b.reshape(-1)]))
    small_n = small.shape[0]
    small_rows = -(-small_n // width)
    head_n = head_w.shape[0] * head_w.shape[1]
    head_rows = -(-head_n // width)
    pad_rows = -(-(small_rows + head_rows) // PAD) * PAD

    def to_rows(flat, rows):
        return jnp.pad(flat, (0, rows * width - flat.shape[0])).reshape(rows, width)

    if is_small(count):
        vec = jnp.concatenate([low(gains_w[0]), low(shifts_w[0])])
        eights = [low(head_w[8 * k : 8 * k + 8]) for k in range(3)]
        above = jnp.concatenate([jnp.pad(vec, ((0, 0), (0, 384 - size)))] + eights, axis=1)
        extra = jnp.concatenate([above, jnp.pad(low(up_b), ((0, 7), (0, width - up_b.shape[1])))])
    else:
        extra = jnp.concatenate(
            [
                to_rows(small, small_rows),
                to_rows(low(head_w).reshape(-1), head_rows),
                jnp.zeros((pad_rows - small_rows - head_rows, width), BF),
            ]
        )
    cut = 2 * size

    order = Order(place)
    a0_g = Gather(order, jnp.concatenate([a_zero, extra]))
    f0_g, a1_g, f1_g = Gather(order, f_zero), Gather(order, a_one, True), Gather(order, f_one)
    a0_g.spare(4)
    f0_g.spare(4)
    f1_g.spare(4)
    a0_g.start()
    a1_g.start()
    a0_g.got, a1_g.got = order.wait(a0_g.got, a1_g.got)
    a0_g.done()
    a0_g.start()
    f0_g.start()
    a1_g.done()
    a1_g.start()
    a0_g.got, f0_g.got, a1_g.got = order.wait(a0_g.got, f0_g.got, a1_g.got)
    a0_g.done()
    a0_g.start()
    f0_g.done()
    f0_g.start()
    a1_g.done()
    a1_g.spare(2)
    a0_g.got, f0_g.got = order.wait(a0_g.got, f0_g.got)
    a0_g.done()
    a0_g.start()
    f0_g.done()
    f0_g.start()
    a1_g.start()
    f1_g.start()
    a0_g.swap_own()
    a0_g.got, f0_g.got, a1_g.got, a0_g.other_own, f1_g.got = order.wait(
        a0_g.got, f0_g.got, a1_g.got, a0_g.other_own, f1_g.got
    )
    f0_g.done()
    f0_g.start()
    a1_g.done()
    f1_g.done()
    f1_g.start()
    a1_part = a1_g.start_part(0)
    a0_g.swap_got()
    a0_g.other_got = order.wait(a0_g.other_got)
    a0_half = a0_g.halves(place, 2, size)
    n_g = gains_w.shape[1] * size
    n_s = shifts_w.shape[1] * size
    tail_halves = (a0_g.own, a0_g.got), (a0_g.other_own, a0_g.other_got)
    if is_small(count):
        vecs, cups, head = tails_of(place, cut, units, *tail_halves)
        head = low(head)
    else:
        vecs, cups, heads = [], [], []
        for tail in natural_tails(place, cut, *tail_halves):
            flat = tail[:, :small_rows].reshape(count, -1)[:, :small_n].astype(F32)
            vec = flat[:, : n_g + n_s].reshape(count, -1, size).transpose(1, 0, 2).reshape(-1, width)
            vecs.append(vec)
            cups.append(flat[:, n_g + n_s :].reshape(units, 1, width))
            block = tail[:, small_rows : small_rows + head_rows].reshape(count, -1)[:, :head_n]
            heads.append(block.reshape(count * head_w.shape[0], head_w.shape[1]))
        head = jnp.concatenate(heads)
    gain0 = shift0 = vecs[0]
    gain1 = shift1 = vecs[1]
    cup0, cup1 = cups[0], cups[1]

    own = lax.dynamic_slice_in_dim(tokens, section * mine, mine, 0)
    seg = lax.dynamic_slice_in_dim(segment_ids, section * mine, mine, 0)
    cot = lax.dynamic_slice_in_dim(cotangent, section * mine, mine, 0)
    rows = range(mine)
    seg_col = [jnp.broadcast_to(seg[r][:, None], (length, 128)) for r in rows]
    seg_row = [jnp.broadcast_to(seg[r][None], (8, length)) for r in rows]

    a0 = order.now([own[r] for r in rows])
    kept_a0 = [attn_fwd(False, place, a0[r], seg_col[r], seg_row[r], a0_half, shift0) for r in rows]
    kept_a0, f0_g.got, f1_g.got, a1_part = order.wait(kept_a0, f0_g.got, f1_g.got, a1_part)
    f0_g.swap_own()
    f0_g.swap_got()
    a1_g.got = (a1_part, a1_g.start_part(1))
    f1_g.done()
    f1_g.start()
    f0_g.other_own, f0_g.other_got = order.wait(f0_g.other_own, f0_g.other_got)
    n1 = order.now([kept[4] for kept in kept_a0])
    f0_half = f0_g.halves(place, units, size)
    a1_g.swap_own()
    kept_f0 = [ffn_fwd(False, place, n1[r], f0_half, cup0, gain0, shift0) for r in rows]
    kept_f0, a1_g.other_own, a1_g.got, f1_g.got = order.wait(kept_f0, a1_g.other_own, a1_g.got, f1_g.got)
    a1_g.swap_got()
    f1_g.done()
    f1_g.start()
    a1_g.other_got = order.wait(a1_g.other_got)
    a1 = order.now([kept[4] for kept in kept_f0])
    a1_half = a1_g.halves(place, 2, size)
    f1_g.swap_own()
    kept_a1 = [attn_fwd(True, place, a1[r], seg_col[r], seg_row[r], a1_half, shift1) for r in rows]
    kept_a1, f1_g.other_own, f1_g.got = order.wait(kept_a1, f1_g.other_own, f1_g.got)
    f1_g.swap_got()
    n1 = [kept[4] for kept in kept_a1]
    f1_half = f1_g.halves(place, units, size)
    kept_f1 = [ffn_fwd(False, place, n1[r], f1_half, cup1, gain1, shift1) for r in rows]

    d_y1, g_head = [], 0.0
    for r in rows:
        y1 = kept_f1[r][4]
        proj = dot(y1, head)
        rho = lax.rsqrt(jnp.sum(proj * proj, axis=-1, keepdims=True) + norm_eps)
        c = cot[r].astype(F32)
        d_proj = low(rho * c - rho * rho * rho * proj * jnp.sum(proj * c, axis=-1, keepdims=True))
        g_head = g_head + dot(y1, d_proj, 0, 0)
        d_y1.append(dot(d_proj, head, 1, 1))

    def total(items):
        out = items[0]
        for item in items[1:]:
            out = jax.tree.map(lambda x, y: (x.astype(F32) + y.astype(F32)).astype(x.dtype), out, item)
        return out

    def ffn_back(near_first, d_out, kept_a, kept_f, planes, gain, shift):
        outs = [
            ffn_bwd(near_first, grad_place, d_out[r], *kept_f[r][2:4], *kept_f[r][:2], planes, *kept_a[r][4:6], gain, shift)
            for r in rows
        ]
        *chunk, sums, cup = total([(*o[:3], o[4], o[5]) for o in outs])
        return in_planes(*chunk, place, (units, 0), count, near_first), [o[3] for o in outs], sums, cup

    def attn_back(near_first, more, d_out, a, kept, planes):
        outs = [attn_bwd(near_first, more, grad_place, d_out[r], a[r], seg_col[r], seg_row[r], *kept[r][:4], planes) for r in rows]
        *chunk, sums, sumo = total([(*o[:3], o[4], o[5]) for o in outs])
        return in_planes(*chunk, place, (2, 2), count, near_first), [o[3] for o in outs], sums, sumo

    chunk, d_r, sums_f1, g_cup1 = ffn_back(False, d_y1, kept_a1, kept_f1, f1_half, gain1, shift1)
    f1_r = Reduce(order, chunk)
    f1_r.wait()
    f1_r.start_upper()
    d_r = order.now(d_r)
    chunk, d_a1, sums_a1, sumo_a1 = attn_back(True, 0, d_r, a1, kept_a1, a1_half)
    d_a1, f1_r.upper, f1_r.there = order.wait(d_a1, f1_r.upper, f1_r.there)
    a1_r = Reduce(order, chunk, True)
    f1_r.start_lower()
    f1_r.start_from_upper()
    a1_r.wait()
    a1_r.spare(4)
    a1_r.start_upper()
    d_y0 = order.now([low(item) for item in d_a1])
    chunk, d_r, sums_f0, g_cup0 = ffn_back(False, d_y0, kept_a0, kept_f0, f0_half, gain0, shift0)
    d_r, f1_r.got, f1_r.ahead, a1_r.upper, a1_r.there = order.wait(
        d_r, f1_r.got, f1_r.ahead, a1_r.upper, a1_r.there
    )
    f0_r = Reduce(order, chunk)
    f1_r.join()
    f1_r.start()
    a1_r.start_lower()
    f0_r.wait()
    f0_r.start()
    d_r = order.now(d_r)
    chunk, d_a0, sums_a0, sumo_a0 = attn_back(
        False, PAD if is_small(count) else 0, d_r, a0, kept_a0, a0_half
    )
    d_a0, a1_r.got, f1_r.got, f0_r.got, there = order.wait(d_a0, a1_r.got, f1_r.got, f0_r.got, f0_r.there)
    f0_r.terms[1] = there

    def small_block(sums_a, sumo, sums_f, g_cup, head_part, core):
        gains = jnp.stack([sums_f[0], sums_f[1]]).reshape(2, count, size).transpose(1, 0, 2)
        shift = jnp.stack([sums_a[0], sums_a[1], sumo[0], sums_f[3], sums_f[4], sums_f[2]])
        shift = shift.reshape(6, count, size).transpose(1, 0, 2)
        flat = jnp.concatenate(
            [gains.reshape(count, -1), shift.reshape(count, -1), g_cup.reshape(count, -1)], axis=1
        )
        flat = jnp.pad(flat, ((0, 0), (0, small_rows * width - small_n)))
        piece = jnp.pad(head_part.reshape(count, -1), ((0, 0), (0, head_rows * width - head_n)))
        block = jnp.concatenate(
            [
                flat.reshape(count, small_rows, width),
                piece.reshape(count, head_rows, width),
                jnp.zeros((count, pad_rows - small_rows - head_rows, width), F32),
            ],
            axis=1,
        )
        return relative(low(block), place, core)

    if is_small(count):
        layer0 = (sums_a0, sumo_a0, sums_f0, g_cup0)
        layer1 = (sums_a1, sumo_a1, sums_f1, g_cup1)
        chunk = pack_tails(place, cut, layer0, layer1, g_head, chunk)
    else:
        half_head = g_head.reshape(2, -1, head_w.shape[1])
        tail0 = small_block(sums_a0, sumo_a0, sums_f0, g_cup0, half_head[0], 0)
        tail1 = small_block(sums_a1, sumo_a1, sums_f1, g_cup1, half_head[1], 1)
        tails = (jnp.where(first, tail0, tail1),) + in_halves(jnp.where(first, tail1, tail0))
        chunk = [jnp.concatenate(pair, axis=1) for pair in zip(chunk, tails)]
    a0_r = Reduce(order, chunk)
    a0_r.wait()
    a0_r.start()
    f0_r.start()
    f1_r.spare(1)
    f1_r.start()
    a1_r.start_from_upper()
    d_first, d_second = jnp.stack(d_a0), jnp.stack(d_a1)
    a0_r.got, a1_r.ahead, f1_r.got = order.wait(a0_r.got, a1_r.ahead, f1_r.got)
    a0_r.start()
    a1_r.join()
    f0_r.wait()
    f0_r.start()
    a1_r.start()
    got = across(order.now(d_first), 1), across(order.now(d_second), 0)
    a0_r.got, a1_r.got = order.wait(a0_r.got, a1_r.got)
    a0_r.spare(2)
    a0_r.start()
    done_f1 = f1_r.finish()
    a1_r.start()
    f0_r.got, got, done_f1 = order.wait(f0_r.got, got, done_f1)
    f0_r.spare(1)
    f0_r.start()
    input_grads = jnp.where(first, jnp.concatenate([d_first, got[0]]), jnp.concatenate([got[1], d_second]))
    a0_r.got, a1_r.got, input_grads = order.wait(a0_r.got, a1_r.got, input_grads)
    a0_r.spare(1)
    a0_r.start()
    done_a1 = a1_r.finish()
    f0_r.got, done_a1 = order.wait(f0_r.got, done_a1)
    done_f0 = f0_r.finish()

    def unite(zero_part, one_part):
        got = swap(jnp.where(first, one_part, zero_part))
        return jnp.where(first, zero_part, got), jnp.where(first, got, one_part)

    up_plane, down_plane = unite(done_f0, done_f1)
    a0_r.got, up_plane, down_plane = order.wait(a0_r.got, up_plane, down_plane)
    done_a0 = a0_r.finish()
    low_plane, high_plane = unite(done_a0[:cut], done_a1)

    def unit(array, j):
        return array[j * size : (j + 1) * size]

    qkv_grad = jnp.concatenate([unit(low_plane, 0), unit(low_plane, 1), unit(high_plane, 0)], axis=1)
    out_grad = unit(high_plane, 1)
    up_grad = jnp.concatenate([unit(up_plane, j) for j in range(units)], axis=1)
    down_grad = down_plane
    tail = done_a0[cut:]
    if is_small(count):
        gain_grad = tail[None, :2, :size]
        shift_grad = tail[None, 2:8, :size]
        cup_grad = tail[8:9, : up_b.shape[1]]
        head_grad = jnp.concatenate([tail[:8, 384 + 128 * k : 512 + 128 * k] for k in range(3)])
    else:
        flat = tail[:small_rows].reshape(-1)[:small_n]
        gain_grad = flat[:n_g].reshape(gains_w.shape)
        shift_grad = flat[n_g : n_g + n_s].reshape(shifts_w.shape)
        cup_grad = flat[n_g + n_s :].reshape(up_b.shape)
        head_grad = tail[small_rows : small_rows + head_rows].reshape(-1)[:head_n].reshape(head_w.shape)

    return (
        qkv_grad[None],
        out_grad[None],
        up_grad[None],
        down_grad[None],
        gain_grad,
        shift_grad,
        cup_grad,
        head_grad,
        input_grads[None],
    )


def solution(mesh):
    return jax.shard_map(
        shards,
        mesh=mesh,
        in_specs=(
            P("dp", None, None),
            P("dp", None),
            P("dp", None, None),
            P("section", "dp", None),
            P("section", "dp", None),
            P("section", "dp", None),
            P("section", "dp", None),
            P("section", None, "dp"),
            P("section", None, "dp"),
            P("section", "dp"),
            P(("section", "dp"), None),
        ),
        out_specs=(
            P("section", "dp", None),
            P("section", "dp", None),
            P("section", "dp", None),
            P("section", "dp", None),
            P("section", None, "dp"),
            P("section", None, "dp"),
            P("section", "dp"),
            P(("section", "dp"), None),
            P("section", "dp", None, None),
        ),
        check_vma=False,
    )
```

```python
import jax
import jax.numpy as jnp
from jax import lax
from jax.experimental import pallas as pl
from jax.experimental.pallas import tpu as pltpu
from jax.sharding import PartitionSpec as P

HEADS = 12
HDIM = 64
GROUP = 4
BLOCK = 128
PAD = 16
norm_eps = 1e-06
BF = jnp.bfloat16
F32 = jnp.float32
BOTH = ("section", "dp")
SCALE = HDIM ** (-0.5)

ERF_SCALE = 0.425
ERF_POLY = (
    0.11985147519825406,
    0.12072713574380309,
    0.10159474513684189,
    0.12334456743816431,
    -0.0435293372534038,
    0.19486821903107854,
    -0.15132025578595443,
    0.03446332841595847,
)


def dot(left, right, over_left=1, over_right=0):
    return lax.dot_general(
        left, right, (((over_left,), (over_right,)), ((), ())), preferred_element_type=F32
    )


def shape_of(shape, dtype):
    return jax.ShapeDtypeStruct(shape, dtype)


def whole_block(*shape):
    return pl.BlockSpec(shape, lambda g: (0,) * len(shape))


def gelu_pair(u):
    bell = jnp.exp(u * u * -0.5)
    t = 1.0 / (1.0 + (ERF_SCALE * 0.7071067811865476) * jnp.abs(u))
    poly = ERF_POLY[-1]
    for item in ERF_POLY[-2::-1]:
        poly = poly * t + item
    tail = bell * (poly * t)
    cdf = jnp.where(u < 0.0, tail, 1.0 - tail)
    return u * cdf, cdf + u * bell * 0.3989422804014327


def norm_stats(v):
    center = v - jnp.mean(v, axis=-1, keepdims=True)
    t = lax.rsqrt(jnp.mean(center * center, axis=-1, keepdims=True) + norm_eps)
    return center * t, t


def norm_back(dy, n, t, gain):
    dn = dy * gain
    mean = jnp.mean(dn, axis=-1, keepdims=True)
    along = jnp.mean(dn * n, axis=-1, keepdims=True)
    return t * (dn - mean - n * along)


def colsum(v):
    return jnp.sum(v, axis=0, keepdims=True)


def near(b, blocks):
    return max(0, b - 1) * BLOCK, min(blocks, b + 2) * BLOCK


def is_small(count):
    return count == 16


def steps_of(count, core, near_first):
    outer = [4 << j for j in range((count // 4).bit_length() - 1)]
    quad = [1, 2]
    if core:
        quad = [2, 1]
        if is_small(count):
            outer = outer[::-1]
    return quad + outer if near_first else outer + quad


def bit_of(me, mask):
    return (me >> (mask.bit_length() - 1)) & 1


def send_index(chip_z, chip_q, me, core, near_first):
    index = 0
    rel = (chip_z * 4 + chip_q) ^ me
    for j, mask in enumerate(steps_of(16, core, near_first)):
        index = index + bit_of(rel, mask) * (1 << j)
    return index


def each(count, body):
    lax.fori_loop(0, count, lambda j, _: (body(j), 0)[1], 0)


CHIP_BITS = (8, 4, 2, 1)


class Loads:
    def __init__(self, near_first, place_ref, own, other, targets, sem):
        self.near_first, self.place, self.planes = near_first, place_ref, (own, other)
        self.targets, self.sem = targets, sem

    def groups(self, plane, unit):
        order = steps_of(16, plane, self.near_first)
        together = len(self.targets[plane].shape) == 6
        out = []
        for p in range(2):
            for b2 in range(2):
                fixed = {order[3]: bit_of(self.place[0], order[3]) ^ p, order[2]: b2}
                if together:
                    assert plane and not self.near_first
                    fixed.update({8: unit >> 1, 4: unit & 1})
                    bits = [(unit & 1, unit >> 1)]
                elif plane == 0:
                    bits = [()]
                else:
                    bits = [(0,), (1,)]
                for lead in bits:
                    if lead and not together:
                        fixed = {**fixed, order[1]: lead[0]}
                    chips = tuple(fixed.get(mask, slice(None)) for mask in CHIP_BITS)
                    out.append((p, b2, lead, chips if together else (unit,) + chips))
        return out

    def start(self, plane, unit):
        size = self.targets[plane].shape[-2]

        def begin(section):
            pieces = self.planes[0] if plane == section else self.planes[1]
            if len(pieces) == 1:
                source = pieces[0].reshape(*self.targets[plane].shape)
            for k, (p, b2, lead, at) in enumerate(self.groups(plane, unit)):
                if len(pieces) == 1:
                    piece = source.at[at]
                else:
                    piece = pieces[1 + b2] if p and len(pieces) == 3 else pieces[p].at[b2]
                    for bit in lead:
                        piece = piece.at[bit]
                    if len(at) == 5:
                        rows = pl.ds(pl.multiple_of(unit * size, PAD), size)
                        piece = piece.at[(slice(None),) * (len(piece.shape) - 2) + (rows,)]
                pltpu.make_async_copy(piece, self.targets[plane].at[at], self.sem.at[plane, unit, k]).start()

        by_section(self.place[1], begin)

    def wait(self, plane, unit):
        for k, (_, _, _, at) in enumerate(self.groups(plane, unit)):
            to = self.targets[plane].at[at]
            pltpu.make_async_copy(to, to, self.sem.at[plane, unit, k]).wait()


def halves_view(pieces):
    if len(pieces) == 1:
        return pieces
    return [item.reshape((2,) * (item.shape[0].bit_length() - 1) + item.shape[1:]) for item in pieces]


def block_of(b, pair):
    return slice(b * BLOCK, (b + 1) * BLOCK), slice(pair * 2 * HDIM, (pair + 1) * 2 * HDIM)


def two_heads(pair, lane):
    zero = jnp.zeros_like(pair)
    return jnp.concatenate([jnp.where(lane < HDIM, pair, zero), jnp.where(lane >= HDIM, pair, zero)])


def attn_fwd_kernel(near_first, halves, place_ref, *refs):
    own, other = refs[:halves], refs[halves : 2 * halves]
    a_ref, sq_ref, sk_ref, bias_ref, shift_ref = refs[2 * halves : 2 * halves + 5]
    q_ref, k_ref, v_ref, o_ref, n_ref, t_ref, acc, low_w, high_w, sem = refs[2 * halves + 5 :]
    step = pl.program_id(0)
    length, width = a_ref.shape
    blocks = length // BLOCK
    a = a_ref[...]
    loads = Loads(near_first, place_ref, own, other, (low_w, high_w), sem)

    @pl.when(step == 0)
    def _():
        for plane, unit in ((0, 0), (0, 1), (1, 0), (1, 1)):
            loads.start(plane, unit)
        for plane, unit in ((0, 0), (0, 1), (1, 0)):
            loads.wait(plane, unit)

    cols = GROUP * HDIM
    here = pl.ds(pl.multiple_of(step * cols, cols), cols)

    def column(ref, j):
        return ref[j, :, :, :, :, :, here].reshape(width, cols)

    q_ref[...] = (dot(a, column(low_w, 0)) + bias_ref[2:3]).astype(BF)
    k_ref[...] = dot(a, column(low_w, 1)).astype(BF)
    v_ref[...] = (dot(a, column(high_w, 0)) + bias_ref[3:4]).astype(BF)
    lane = lax.broadcasted_iota(jnp.int32, (BLOCK, 2 * HDIM), 1)
    tiles = [(b, pair) for b in range(blocks) for pair in range(GROUP // 2)]

    def scores_of(b, pair):
        lo, hi = near(b, blocks)
        rows, lanes = block_of(b, pair)
        same = sq_ref[rows, 0:1] == sk_ref[0:1, lo:hi]
        scores = dot(two_heads(q_ref[rows, lanes] * SCALE, lane), k_ref[lo:hi, lanes], 1, 1)
        return jnp.where(jnp.concatenate([same, same]), scores, -1000000000.0)

    ahead = scores_of(*tiles[0])
    for j, (b, pair) in enumerate(tiles):
        lo, hi = near(b, blocks)
        rows, lanes = block_of(b, pair)
        scores = ahead
        if j + 1 < len(tiles):
            ahead = scores_of(*tiles[j + 1])
        grown = jnp.exp(scores - jnp.max(scores, axis=-1, keepdims=True))
        scale = 1.0 / jnp.sum(grown, axis=-1, keepdims=True)
        out = dot((grown * scale).astype(BF), v_ref[lo:hi, lanes])
        o_ref[rows, lanes] = jnp.where(lane < HDIM, out[:BLOCK], out[BLOCK:]).astype(BF)
    @pl.when(step == 0)
    def _():
        loads.wait(1, 1)

    part = dot(o_ref[...], high_w.at[1].reshape(width, width)[here, :])

    @pl.when(step == 0)
    def _():
        acc[...] = a.astype(F32) + shift_ref[4:5] + part

    @pl.when(step != 0)
    def _():
        acc[...] += part

    @pl.when(step == pl.num_programs(0) - 1)
    def _():
        n, t = norm_stats(acc[...])
        n_ref[...] = n
        t_ref[...] = jnp.broadcast_to(t, t_ref.shape)


SCALARS = pl.BlockSpec(memory_space=pltpu.SMEM)
NO_COST = pl.CostEstimate(flops=0, bytes_accessed=0, transcendentals=0)


ANYWHERE = pl.BlockSpec(memory_space=pl.ANY)


def attn_fwd(near_first, place, a, seg_col, seg_row, planes, shift):
    length, width = a.shape
    cols = GROUP * HDIM
    group = pl.BlockSpec((length, cols), lambda g: (0, g))
    half = (2, 2, 2, 2, 2, width // 16, width)
    halves = len(planes[0])
    return pl.pallas_call(
        lambda *refs: attn_fwd_kernel(near_first, halves, *refs),
        grid=(HEADS // GROUP,),
        in_specs=[SCALARS]
        + [ANYWHERE] * (2 * halves)
        + [whole_block(length, width), whole_block(length, 128), whole_block(8, length)]
        + [pl.BlockSpec((8, cols), lambda g: (0, g)), whole_block(8, width)],
        out_specs=[group] * 4 + [whole_block(length, width), whole_block(length, 128)],
        out_shape=[shape_of((length, width), BF)] * 4
        + [shape_of((length, width), F32), shape_of((length, 128), F32)],
        scratch_shapes=[
            pltpu.VMEM((length, width), F32),
            pltpu.VMEM(half, BF),
            pltpu.VMEM(half, BF),
            pltpu.SemaphoreType.DMA((2, 2, 8)),
        ],
        cost_estimate=NO_COST,
        name="attn_fwd",
    )(place, *halves_view(planes[0]), *halves_view(planes[1]), a, seg_col, seg_row, shift, shift)


def ffn_fwd_kernel(near_first, halves, place_ref, *refs):
    own, other = refs[:halves], refs[halves : 2 * halves]
    n1_ref, cup_ref, gain_ref, shift_ref = refs[2 * halves : 2 * halves + 4]
    g_ref, gp_ref, n_ref, t_ref, y_ref = refs[2 * halves + 4 : 2 * halves + 9]
    h1, acc, up_w, down_w, sem = refs[2 * halves + 9 :]
    step = pl.program_id(0)
    width = n1_ref.shape[1]
    loads = Loads(near_first, place_ref, own, other, (up_w, down_w), sem)
    units = up_w.shape[0]

    @pl.when(step == 0)
    def _():
        loads.start(0, 0)
        loads.start(1, 0)

    @pl.when(step == 0)
    def _():
        hidden = n1_ref[...] * gain_ref[0:1] + shift_ref[6:7]
        h1[...] = hidden.astype(BF)
        acc[...] = hidden + shift_ref[5:6]

    loads.wait(0, step)

    @pl.when(step + 1 < units)
    def _():
        loads.start(0, step + 1)
        loads.start(1, step + 1)

    loads.wait(1, step)
    up = up_w[step].reshape(width, width)
    down = down_w[step >> 1, step & 1].reshape(width, width)
    wide = 256
    parts = h1.shape[1] // wide

    def upper(j):
        cols = slice(j * wide, (j + 1) * wide)
        return dot(h1[...], up[:, cols]) + cup_ref[0, :, cols]

    ahead = upper(0)
    total = acc[...]
    for j in range(parts):
        cols = slice(j * wide, (j + 1) * wide)
        here = ahead
        if j + 1 < parts:
            ahead = upper(j + 1)
        g, slope = gelu_pair(here)
        g = g.astype(BF)
        g_ref[:, cols] = g
        gp_ref[:, cols] = slope.astype(BF)
        total = total + dot(g, down[cols])
    acc[...] = total

    @pl.when(step == pl.num_programs(0) - 1)
    def _():
        n, t = norm_stats(acc[...])
        n_ref[...] = n
        t_ref[...] = jnp.broadcast_to(t, t_ref.shape)
        y_ref[...] = (n * gain_ref[1:2] + shift_ref[7:8]).astype(BF)


def ffn_fwd(near_first, place, n1, planes, cup, gain, shift):
    length, width = n1.shape
    units = cup.shape[0]
    column = pl.BlockSpec((length, width), lambda g: (0, g))
    up = (units, 2, 2, 2, 2, width // 16, width)
    down = (2, 2, 2, 2, units * width // 16, width)
    halves = len(planes[0])
    return pl.pallas_call(
        lambda *refs: ffn_fwd_kernel(near_first, halves, *refs),
        grid=(units,),
        in_specs=[SCALARS]
        + [ANYWHERE] * (2 * halves)
        + [
            whole_block(length, width),
            pl.BlockSpec((1, 1, width), lambda g: (g, 0, 0)),
            whole_block(8, width),
            whole_block(8, width),
        ],
        out_specs=[column, column, whole_block(length, width), whole_block(length, 128), whole_block(length, width)],
        out_shape=[shape_of((length, units * width), BF)] * 2
        + [shape_of((length, width), F32), shape_of((length, 128), F32), shape_of((length, width), BF)],
        scratch_shapes=[
            pltpu.VMEM((length, width), BF),
            pltpu.VMEM((length, width), F32),
            pltpu.VMEM(up, BF),
            pltpu.VMEM(down, BF),
            pltpu.SemaphoreType.DMA((2, units, 4)),
        ],
        cost_estimate=NO_COST,
        name="ffn_fwd",
    )(place, *halves_view(planes[0]), *halves_view(planes[1]), n1, cup, gain, shift)


def by_section(section, action):
    for plane in range(2):
        pl.when(section == plane)(lambda plane=plane: action(plane))


def ffn_bwd_kernel(near_first, halves, head, place_ref, *refs):
    own, other = refs[:halves], refs[halves : 2 * halves]
    if head:
        y_ref, cot_ref, head_ref, g_head_ref = refs[2 * halves], refs[2 * halves + 1], refs[2 * halves + 2], refs[2 * halves + 17]
        refs = refs[: 2 * halves] + (None,) + refs[2 * halves + 3 : 2 * halves + 17] + refs[2 * halves + 18 :]
    dy_ref, n2_ref, t2_ref, g_ref, gp_ref, n1_ref, t1_ref, gain_ref, shift_ref = refs[2 * halves : 2 * halves + 9]
    keep_ref, high_ref, low_ref, dr1_ref, sums_ref, cup_ref = refs[2 * halves + 9 : 2 * halves + 15]
    h1, df, acc, gup, gdown, up_w, down_w, sem, load_sem = refs[2 * halves + 15 :]
    step = pl.program_id(0)
    loads = Loads(near_first, place_ref, own, other, (up_w, down_w), load_sem)

    @pl.when(step == 0)
    def _():
        loads.start(1, 0)
        loads.start(0, 0)

    last = pl.num_programs(0) - 1
    quads = outer = 4
    width = h1.shape[1]
    size = width // (quads * outer)

    @pl.when(step == 0)
    def _():
        n2 = n2_ref[...]
        if head:
            y = y_ref[...]
            proj = dot(y, head_ref[...])
            rho = lax.rsqrt(jnp.sum(proj * proj, axis=-1, keepdims=True) + norm_eps)
            cot = cot_ref[...].astype(F32)
            along = jnp.sum(proj * cot, axis=-1, keepdims=True)
            d_proj = (rho * cot - rho * rho * rho * proj * along).astype(BF)
            g_head_ref[...] = dot(y, d_proj, 0, 0)
            dy = dot(d_proj, head_ref[...], 1, 1)
        else:
            dy = dy_ref[...].astype(F32)
        dr2 = norm_back(dy, n2, t2_ref[:, 0:1], gain_ref[1:2])
        low = dr2.astype(BF)
        df[...] = low
        acc[...] = dr2
        h1[...] = (n1_ref[...] * gain_ref[0:1] + shift_ref[6:7]).astype(BF)
        sums_ref[...] = jnp.zeros_like(sums_ref)
        sums_ref[1:2] = colsum(dy * n2)
        sums_ref[2:3] = colsum(dy)
        sums_ref[3:4] = colsum(low.astype(F32))

    loads.wait(1, step)
    loads.wait(0, step)

    @pl.when(step < last)
    def _():
        loads.start(1, step + 1)
        loads.start(0, step + 1)

    d = df[...]
    down = dot(g_ref[...], d, 0, 0).astype(BF)
    tall = width // quads
    for q in range(quads):
        gdown[send_index(step, q, place_ref[0], 1, near_first)] = down[q * tall : (q + 1) * tall]
    du = (dot(d, down_w[step >> 1, step & 1].reshape(width, width), 1, 1) * gp_ref[...].astype(F32)).astype(BF)
    cup_ref[0] = colsum(du.astype(F32))
    up = dot(h1[...], du, 0, 0).astype(BF)
    for chip in range(quads * outer):
        at = send_index(chip // quads, chip % quads, place_ref[0], 0, near_first)
        gup[step, at] = up[chip * size : (chip + 1) * size]
    acc[...] += dot(du, up_w[step].reshape(width, width), 1, 1)

    def up_copies(section, j):
        rows = pl.ds(pl.multiple_of(j * size, PAD), size)
        if section == 0:
            return [pltpu.make_async_copy(gup.at[j], keep_ref.at[:, rows, :], sem.at[j, 0])]
        return [
            pltpu.make_async_copy(gup.at[j, :8], low_ref.at[:, rows, :], sem.at[j, 0]),
            pltpu.make_async_copy(gup.at[j, 8:], high_ref.at[:, rows, :], sem.at[j, 1]),
        ]

    def down_copies(section, j, start):
        for q in range(quads):
            at = send_index(j, q, place_ref[0], 1, near_first)
            if section == 1:
                copy = pltpu.make_async_copy(gdown.at[at], keep_ref.at[at], sem.at[j, 2 + q])
                copy.start() if start else copy.wait()
            elif not start:
                pltpu.make_async_copy(gdown.at[at], low_ref.at[0], sem.at[j, 2 + q]).wait()
            else:
                for part, ref in enumerate((low_ref, high_ref)):
                    @pl.when(at >> 3 == part)
                    def _():
                        pltpu.make_async_copy(gdown.at[at], ref.at[at & 7], sem.at[j, 2 + q]).start()

    def begin(section):
        for item in up_copies(section, step):
            item.start()
        down_copies(section, step, True)

    by_section(place_ref[1], begin)

    @pl.when(step == last)
    def _():
        dh = acc[...]
        n1 = n1_ref[...]
        dr1_ref[...] = norm_back(dh, n1, t1_ref[:, 0:1], gain_ref[0:1])
        sums_ref[0:1] = colsum(dh * n1)
        sums_ref[4:5] = colsum(dh)

        def finish(section):
            def one(j):
                for item in up_copies(section, j):
                    item.wait()
                down_copies(section, j, False)

            each(gup.shape[0], one)

        by_section(place_ref[1], finish)


def ffn_bwd(near_first, place, given, n2, t2, g, gp, planes, n1, t1, gain, shift):
    length, width = n1.shape
    units = g.shape[1] // width
    outer, size = 4, width // 16
    halves = len(planes[0])
    head = len(given) == 3
    up = (units, 2, 2, 2, 2, size, width)
    down = (2, 2, 2, 2, units * size, width)
    column = pl.BlockSpec((length, width), lambda g: (0, g))
    chunk, half_chunk = [shape_of((n, units * size, width), BF) for n in (16, 8)]
    return pl.pallas_call(
        lambda *refs: ffn_bwd_kernel(near_first, halves, head, *refs),
        grid=(units,),
        in_specs=[
            SCALARS,
            *[ANYWHERE] * (2 * halves),
            *[whole_block(*item.shape) for item in given],
            whole_block(length, width),
            whole_block(length, 128),
            column,
            column,
            whole_block(length, width),
            whole_block(length, 128),
            whole_block(8, width),
            whole_block(8, width),
        ],
        out_specs=[
            ANYWHERE,
            ANYWHERE,
            ANYWHERE,
            whole_block(length, width),
            whole_block(8, width),
            pl.BlockSpec((1, 1, width), lambda g: (g, 0, 0)),
        ]
        + [whole_block(*item.shape) for item in given[2:]],
        out_shape=[chunk, half_chunk, half_chunk, shape_of((length, width), F32), shape_of((8, width), F32), shape_of((units, 1, width), F32)]
        + [shape_of(item.shape, F32) for item in given[2:]],
        scratch_shapes=[
            pltpu.VMEM((length, width), BF),
            pltpu.VMEM((length, width), BF),
            pltpu.VMEM((length, width), F32),
            pltpu.VMEM((units, 16, size, width), BF),
            pltpu.VMEM((16, units * size, width), BF),
            pltpu.VMEM(up, BF),
            pltpu.VMEM(down, BF),
            pltpu.SemaphoreType.DMA((units, 6)),
            pltpu.SemaphoreType.DMA((2, units, 4)),
        ],
        cost_estimate=NO_COST,
        name="ffn_bwd",
    )(place, *halves_view(planes[0]), *halves_view(planes[1]), *given, n2, t2, g, gp, n1, t1, gain, shift)


def attn_bwd_kernel(near_first, halves, place_ref, *refs):
    own, other = refs[:halves], refs[halves : 2 * halves]
    dr_ref, a_ref, sq_ref, sk_ref, q_ref, k_ref, v_ref, o_ref = refs[2 * halves : 2 * halves + 8]
    keep_ref, high_ref, low_ref, da_ref, sums_ref, sumo_ref = refs[2 * halves + 8 : 2 * halves + 14]
    dat, do_sc, dq, dk, dv, grads, low_w, high_w, sem, load_sem = refs[2 * halves + 14 :]
    step = pl.program_id(0)
    loads = Loads(near_first, place_ref, own, other, (low_w, high_w), load_sem)

    @pl.when(step == 0)
    def _():
        for plane, unit in ((1, 1), (0, 0), (0, 1), (1, 0)):
            loads.start(plane, unit)

    length, width = a_ref.shape
    blocks = length // BLOCK
    quads = outer = 4
    size = width // (quads * outer)
    cols = GROUP * HDIM

    @pl.when(step == 0)
    def _():
        low = dr_ref[...].astype(BF)
        dat[...] = low
        da_ref[...] = dr_ref[...]
        sumo_ref[...] = jnp.zeros_like(sumo_ref)
        sumo_ref[0:1] = colsum(low.astype(F32))

    d = dat[...]
    grad_o = dot(o_ref[...], d, 0, 0).astype(BF)

    @pl.when(step == 0)
    def _():
        loads.wait(1, 1)

    now = pl.ds(pl.multiple_of(step * cols, cols), cols)
    do_sc[...] = dot(d, high_w.at[1].reshape(width, width)[now, :], 1, 1).astype(BF)
    dk[...] = jnp.zeros_like(dk)
    dv[...] = jnp.zeros_like(dv)
    lane = lax.broadcasted_iota(jnp.int32, (BLOCK, 2 * HDIM), 1)
    tiles = [(b, pair) for b in range(blocks) for pair in range(GROUP // 2)]

    def products(b, pair):
        lo, hi = near(b, blocks)
        rows, lanes = block_of(b, pair)
        same = sk_ref[lo:hi, 0:1] == sq_ref[0:1, rows]
        query = two_heads(q_ref[rows, lanes] * SCALE, lane)
        d_out = two_heads(do_sc[rows, lanes], lane)
        scores = dot(k_ref[lo:hi, lanes], query, 1, 1)
        scores = jnp.where(jnp.concatenate([same, same], axis=1), scores, -1000000000.0)
        return query, d_out, scores, dot(v_ref[lo:hi, lanes], d_out, 1, 1)

    ahead = products(*tiles[0])
    for j, (b, pair) in enumerate(tiles):
        lo, hi = near(b, blocks)
        rows, lanes = block_of(b, pair)
        query, d_out, scores, d_probs = ahead
        if j + 1 < len(tiles):
            ahead = products(*tiles[j + 1])
        grown = jnp.exp(scores - jnp.max(scores, axis=0, keepdims=True))
        probs = grown * (1.0 / jnp.sum(grown, axis=0, keepdims=True))
        d_scores = probs * (d_probs - jnp.sum(probs * d_probs, axis=0, keepdims=True))
        d_scores = d_scores.astype(BF)
        dv[lo:hi, lanes] += dot(probs.astype(BF), d_out)
        dk[lo:hi, lanes] += dot(d_scores, query)
        d_query = dot(d_scores, k_ref[lo:hi, lanes], 0, 0)
        dq[rows, lanes] = jnp.where(lane < HDIM, d_query[:BLOCK], d_query[BLOCK:]) * SCALE
    a = a_ref[...]
    out = da_ref[...]
    lows = (dq[...].astype(BF), dk[...].astype(BF), dv[...].astype(BF))
    made = []

    @pl.when(step == 0)
    def _():
        for plane, unit in ((0, 0), (0, 1), (1, 0)):
            loads.wait(plane, unit)

    for low, (w_ref, j) in zip(lows, ((low_w, 0), (low_w, 1), (high_w, 0))):
        made.append(dot(a, low, 0, 0).astype(BF))
        out = out + dot(low, w_ref[j, :, :, :, :, :, now].reshape(width, cols), 1, 1)
    da_ref[...] = out
    sums_ref[...] = jnp.zeros_like(sums_ref)
    sums_ref[0:1] = colsum(lows[0].astype(F32))
    sums_ref[1:2] = colsum(lows[2].astype(F32))
    steps = HEADS // GROUP

    def place_of(chip, core):
        return send_index(chip // quads, chip % quads, place_ref[0], core, near_first)

    for unit in range(3):
        for chip in range(quads * outer):
            grads[unit, place_of(chip, unit // 2), :, now] = made[unit][chip * size : (chip + 1) * size]
    for j in range(steps):
        @pl.when(step == j)
        def _(j=j):
            for chip in range(quads * outer):
                start, end = max(chip * size, j * cols), min((chip + 1) * size, (j + 1) * cols)
                if start < end:
                    rows = slice(start - chip * size, end - chip * size)
                    grads[3, place_of(chip, 1), rows, :] = grad_o[start - j * cols : end - j * cols]

    def copies(section, j, units):
        out = []
        for unit in units:
            rows = slice((unit % 2) * size, (unit % 2 + 1) * size)
            lanes = pl.ds(pl.multiple_of(j * cols, cols), cols) if unit < 3 else slice(None)
            if unit // 2 == section:
                pairs = [(grads.at[unit, :, :, lanes], keep_ref.at[:, rows, lanes])]
            else:
                pairs = [
                    (grads.at[unit, :8, :, lanes], low_ref.at[:, rows, lanes]),
                    (grads.at[unit, 8:, :, lanes], high_ref.at[:, rows, lanes]),
                ]
            out += [pltpu.make_async_copy(*pair, sem.at[unit, part, j]) for part, pair in enumerate(pairs)]
        return out

    def begin(section):
        for item in copies(section, step, range(3)):
            item.start()

    by_section(place_ref[1], begin)

    @pl.when(step == steps - 1)
    def _():
        def finish(section):
            for item in copies(section, 0, (3,)):
                item.start()

            def one(j):
                for item in copies(section, j, range(3)):
                    item.wait()

            each(steps, one)
            for item in copies(section, 0, (3,)):
                item.wait()

        by_section(place_ref[1], finish)


def attn_bwd(near_first, more, place, dr, a, seg_col, seg_row, q, k, v, o, planes):
    length, width = a.shape
    outer, size = 4, width // 16
    halves = len(planes[0])
    half = (2, 2, 2, 2, 2, size, width)
    cols = GROUP * HDIM
    group = pl.BlockSpec((length, cols), lambda g: (0, g))
    chunk, half_chunk = [shape_of((n, 2 * size + more, width), BF) for n in (16, 8)]
    return pl.pallas_call(
        lambda *refs: attn_bwd_kernel(near_first, halves, *refs),
        grid=(HEADS // GROUP,),
        in_specs=[
            SCALARS,
            *[ANYWHERE] * (2 * halves),
            whole_block(length, width),
            whole_block(length, width),
            whole_block(8, length),
            whole_block(length, 128),
        ]
        + [group] * 4,
        out_specs=[
            ANYWHERE,
            ANYWHERE,
            ANYWHERE,
            whole_block(length, width),
            pl.BlockSpec((8, cols), lambda g: (0, g)),
            whole_block(8, width),
        ],
        out_shape=[chunk, half_chunk, half_chunk, shape_of((length, width), F32), shape_of((8, width), F32), shape_of((8, width), F32)],
        scratch_shapes=[pltpu.VMEM((length, width), BF), pltpu.VMEM((length, cols), BF)]
        + [pltpu.VMEM((length, cols), F32)] * 3
        + [pltpu.VMEM((4, 16, size, width), BF), pltpu.VMEM(half, BF), pltpu.VMEM(half, BF)]
        + [pltpu.SemaphoreType.DMA((4, 2, HEADS // GROUP)), pltpu.SemaphoreType.DMA((2, 2, 8))],
        cost_estimate=NO_COST,
        name="attn_bwd",
    )(place, *halves_view(planes[0]), *halves_view(planes[1]), dr, a, seg_row, seg_col, q, k, v, o)


def flip(value, mask, other=None):
    count = lax.axis_size("dp")
    masks = (mask, mask if other is None else other)
    pairs = [(s * count + i, s * count + (i ^ masks[s])) for s in range(2) for i in range(count)]
    return lax.ppermute(value, BOTH, pairs)


def swap(value):
    count = lax.axis_size("dp")
    pairs = [(s * count + i, (1 - s) * count + i) for s in range(2) for i in range(count)]
    return lax.ppermute(value, BOTH, pairs)


def across(value, source):
    count = lax.axis_size("dp")
    return lax.ppermute(value, BOTH, [(source * count + i, (1 - source) * count + i) for i in range(count)])


class Order:
    def __init__(self, mark):
        self.mark = mark

    def wait(self, *values):
        leaves, tree = jax.tree.flatten(values)
        *leaves, self.mark = lax.optimization_barrier((*leaves, self.mark))
        out = jax.tree.unflatten(tree, leaves)
        return out[0] if len(values) == 1 else out

    def now(self, *values):
        leaves, tree = jax.tree.flatten(values)
        leaves = lax.optimization_barrier((*leaves, self.mark))[:-1]
        out = jax.tree.unflatten(tree, leaves)
        return out[0] if len(values) == 1 else out


class Gather:
    def __init__(self, order, block, near_first=False):
        self.order, self.own, self.near_first = order, block[None], near_first
        self.left = list(zip(*[steps_of(lax.axis_size("dp"), core, near_first) for core in range(2)]))

    def start(self):
        self.got = flip(self.order.now(self.own), *self.left[0])

    def start_part(self, part):
        half = self.own.shape[0] // 2
        return flip(self.order.now(self.own[part * half : (part + 1) * half]), *self.left[0])

    def done(self):
        masks = self.left.pop(0)
        high = (lax.axis_index("dp") & jnp.where(lax.axis_index("section") == 0, *masks)) != 0
        own, got = self.own, self.got
        self.own = jnp.where(high, jnp.concatenate([got, own]), jnp.concatenate([own, got]))

    def spare(self, steps):
        while len(self.left) > steps:
            self.start()
            self.done()

    def wait(self):
        self.got = self.order.wait(self.got)

    def swap_own(self):
        self.other_own = swap(self.order.now(self.own))

    def swap_got(self):
        self.other_got = jax.tree.map(lambda item: swap(self.order.now(item)), self.got)

    def halves(self, place, units, size):
        pairs = tuple(
            (own,) + (got if isinstance(got, tuple) else (got,))
            for own, got in ((self.own, self.got), (self.other_own, self.other_got))
        )
        if is_small(lax.axis_size("dp")):
            return pairs
        return natural_planes(place, units, size, self.near_first, *pairs)


def natural_planes(place, units, size, near_first, own, other):
    count = lax.axis_size("dp")
    out = []
    for section, halves in ((place[1], own), (1 - place[1], other)):
        both = jnp.concatenate(halves)
        at = []
        for core in range(2):
            order = steps_of(count, core, near_first)
            chips = jnp.arange(count)
            index = sum(bit_of(chips, mask) << j for j, mask in enumerate(order))
            at.append(index ^ (bit_of(place[0], order[-1]) << (len(order) - 1)))
        whole = jnp.take(both, jnp.where(section == 0, *at), axis=0)
        rows, width = whole.shape[1:]
        if size:
            by_unit = jnp.stack([whole[:, j * size : (j + 1) * size].reshape(width, width) for j in range(units)])
            if units != 2:
                flat = whole.reshape(units, width, width)
                by_unit = jnp.where(section == 0, by_unit.reshape(flat.shape), flat)
            whole = by_unit.reshape(units, 4, 4, width // 16, width)
        out.append((whole,))
    return out


def tail_kernel(cut, place_ref, *refs):
    halves, (vec_ref, cup_ref, head_ref, pieces, sem) = refs[:4], refs[4:]

    def move(section):
        for start in (True, False):
            for plane in range(2):
                order = steps_of(16, plane, False)
                for p in range(2):
                    source = halves[p if plane == section else 2 + p].at[:, cut:, :]

                    def by_index(index):
                        chip = sum(bit_of(index, 1 << j) * order[j] for j in range(3))
                        chip = chip + order[3] * (bit_of(place_ref[0], order[3]) ^ p)
                        to = pieces.at[plane, chip >> 2, chip & 3]
                        copy = pltpu.make_async_copy(source.at[index], to, sem.at[plane, 8 * p + index])
                        copy.start() if start else copy.wait()

                    each(8, by_index)

    by_section(place_ref[1], move)
    size = vec_ref.shape[2] // 16
    wide = cup_ref.shape[1] * size
    height = head_ref.shape[0] // 32
    for plane in range(2):
        for chip in range(16):
            piece = pieces[plane, chip // 4, chip % 4].astype(F32)
            vec_ref[plane, :, chip * size : (chip + 1) * size] = piece[:8, :size]
            at = (chip % 4) * wide
            cup_ref[plane, chip // 4, :, at : at + wide] = piece[8:9, :wide]
            for k in range(height // 8):
                row = (plane * 16 + chip) * height + 8 * k
                head_ref[row : row + 8, :] = piece[:8, 384 + 128 * k : 512 + 128 * k]


def tails_of(place, cut, units, own, other):
    width = own[0].shape[2]
    return pl.pallas_call(
        lambda *refs: tail_kernel(cut, *refs),
        in_specs=[SCALARS] + [ANYWHERE] * 4,
        out_specs=[pl.BlockSpec(memory_space=pltpu.VMEM)] * 3,
        out_shape=[shape_of((2, 8, width), F32), shape_of((2, units, 1, width), F32), shape_of((width, 128), F32)],
        scratch_shapes=[pltpu.VMEM((2, 4, 4, PAD, width), BF), pltpu.SemaphoreType.DMA((2, 16))],
        cost_estimate=NO_COST,
        name="tails",
    )(place, *own, *other)


def natural_tails(place, cut, own, other):
    own, other = jax.tree.map(lambda item: item[:, cut:], (own, other))
    (mine,), (there,) = natural_planes(place, 0, 0, False, own, other)
    first = place[1] == 0
    return jnp.where(first, mine, there), jnp.where(first, there, mine)


def pack_kernel(cut, place_ref, *refs):
    sums = (refs[0:4], refs[4:8])
    head_ref, _, _, _, keep_ref, high_ref, low_ref, pieces, sem = refs[8:]
    width = pieces.shape[3]
    size = width // 16
    height = head_ref.shape[0] // 32
    pieces[...] = jnp.zeros_like(pieces)
    for plane, (attn, out, ffn, cup) in enumerate(sums):
        wide = cup.shape[0] * size
        rows = [ffn[0:1], ffn[1:2], attn[0:1], attn[1:2], out[0:1], ffn[3:4], ffn[4:5], ffn[2:3]]
        vec = jnp.concatenate(rows)
        for chip in range(16):
            pieces[plane, chip, :8, :size] = vec[:, chip * size : (chip + 1) * size].astype(BF)
            at = (chip % 4) * wide
            pieces[plane, chip, 8:9, :wide] = cup[chip // 4, :, at : at + wide].astype(BF)
            for k in range(height // 8):
                row = (plane * 16 + chip) * height + 8 * k
                pieces[plane, chip, :8, 384 + 128 * k : 512 + 128 * k] = head_ref[row : row + 8, :].astype(BF)

    def move(section):
        for plane in range(2):
            def by_chip(chip):
                at = send_index(chip >> 2, chip & 3, place_ref[0], plane, False)
                source, this = pieces.at[plane, chip], sem.at[plane, chip]
                if plane == section:
                    pltpu.make_async_copy(source, keep_ref.at[at, cut:, :], this).start()
                    return
                for part, ref in enumerate((low_ref, high_ref)):
                    @pl.when(at >> 3 == part)
                    def _():
                        pltpu.make_async_copy(source, ref.at[at & 7, cut:, :], this).start()

            each(16, by_chip)
        for plane in range(2):
            def wait(chip):
                pltpu.make_async_copy(pieces.at[plane, chip], keep_ref.at[0, cut:, :], sem.at[plane, chip]).wait()

            each(16, wait)

    by_section(place_ref[1], move)


def pack_tails(place, cut, layer0, layer1, g_head, chunk):
    return pl.pallas_call(
        lambda *refs: pack_kernel(cut, *refs),
        in_specs=[SCALARS] + [pl.BlockSpec(memory_space=pltpu.VMEM)] * 9 + [ANYWHERE] * 3,
        out_specs=[ANYWHERE] * 3,
        out_shape=[shape_of(item.shape, BF) for item in chunk],
        input_output_aliases={10: 0, 11: 1, 12: 2},
        scratch_shapes=[pltpu.VMEM((2, 16, PAD, chunk[0].shape[2]), BF), pltpu.SemaphoreType.DMA((2, 16))],
        cost_estimate=NO_COST,
        name="pack",
    )(place, *layer0, *layer1, g_head, *chunk)


def in_chips(chunk, place, units, count, core, near_first):
    chips = jnp.arange(16)
    at = sum(bit_of(chips, mask) << j for j, mask in enumerate(steps_of(16, core, near_first)))
    chunk = jnp.take(chunk, at, axis=0)
    width = chunk.shape[2]
    if units:
        natural = chunk.reshape(16, units, -1, width).transpose(1, 0, 2, 3).reshape(units, count, -1, width)
        natural = natural.transpose(1, 0, 2, 3).reshape(count, -1, width)
    else:
        natural = chunk.reshape(count, -1, width)
    return relative(natural, place, core, near_first)


def in_planes(keep, high, low_half, place, units, count, near_first):
    if is_small(count):
        return keep, high, low_half
    send = jnp.concatenate([low_half, high])
    first = place[1] == 0
    keeps, sends = [
        [in_chips(item, place, units[core], count, core, near_first) for core in range(2)] for item in (keep, send)
    ]
    return (jnp.where(first, *keeps),) + in_halves(jnp.where(first, sends[1], sends[0]))


def in_halves(send):
    half = send.shape[0] // 2
    return send[half:], send[:half]


def relative(block, place, core, near_first=False):
    order = steps_of(block.shape[0], core, near_first)
    index = jnp.arange(block.shape[0])
    chips = sum(bit_of(index, 1 << j) * mask for j, mask in enumerate(order))
    return jnp.take(block, chips ^ place[0], axis=0)


def low(value):
    return value.astype(BF)


def add_low(terms, start, count):
    return low(sum(item[start : start + count].astype(F32) for item in terms))


class Reduce:
    def __init__(self, order, chunk, near_first=False):
        keep, high, low_half = chunk
        self.order = order
        self.left = list(zip(*[steps_of(lax.axis_size("dp"), core, near_first) for core in range(2)]))
        self.keep = keep
        self.got = swap(order.now(high))
        self.there = swap(order.now(low_half))
        self.terms = None

    def wait(self):
        self.got = self.order.wait(self.got)

    def start(self):
        if self.terms is None:
            half = self.got.shape[0]
            sent = add_low([self.keep[half:], self.got], 0, half)
            self.terms = [self.keep[:half], self.there]
        else:
            self.terms.append(self.got)
            half = self.got.shape[0] // 2
            sent = add_low(self.terms, half, half)
        self.got = flip(self.order.now(sent), *self.left.pop())

    def start_upper(self):
        self.half = self.got.shape[0]
        self.part = self.half // 2
        self.masks = self.left.pop()
        sent = add_low([self.keep[self.half :], self.got], self.part, self.part)
        self.upper = flip(self.order.now(sent), *self.masks)

    def start_lower(self):
        sent = add_low([self.keep[self.half :], self.got], 0, self.part)
        self.got = flip(self.order.now(sent), *self.masks)
        self.terms = [self.keep[: self.half], self.there]

    def start_from_upper(self):
        part = self.part
        terms = [item[part : 2 * part] for item in self.terms] + [self.upper]
        self.ahead = flip(self.order.now(add_low(terms, 0, part)), *self.left.pop())

    def join(self):
        self.terms.append(self.got)
        self.got = self.ahead

    def spare(self, steps):
        while len(self.left) > steps:
            self.start()

    def finish(self):
        return sum(item[0].astype(F32) for item in self.terms + [self.got])


def shards(tokens, segment_ids, cotangent, qkv_w, out_w, up_w, down_w, gains_w, shifts_w, up_b, head_w):
    count = lax.axis_size("dp")
    section = lax.axis_index("section")
    me = lax.axis_index("dp")
    first = section == 0
    place = jnp.stack([me, section]).astype(jnp.int32)
    grad_place = place if is_small(count) else jnp.stack([jnp.zeros_like(section), section]).astype(jnp.int32)
    rows_dev, length, width = tokens.shape
    mine = rows_dev // 2
    size = width // count
    ff = up_w.shape[2]
    units = ff // width

    def cols(array, n):
        return [array[:, j * width : (j + 1) * width] for j in range(n)]

    def planes_of(low_units, high_units):
        low_plane, high_plane = jnp.concatenate(low_units), jnp.concatenate(high_units)
        got = swap(jnp.where(first, high_plane, low_plane))
        return jnp.where(first, low_plane, got), jnp.where(first, got, high_plane)

    q_u, k_u, v_u = cols(low(qkv_w[0]), 3)
    a_zero, a_one = planes_of([q_u, k_u], [v_u, low(out_w[0])])
    f_zero, f_one = planes_of(cols(low(up_w[0]), units), [low(down_w[0])])
    small = low(jnp.concatenate([gains_w.reshape(-1), shifts_w.reshape(-1), up_b.reshape(-1)]))
    small_n = small.shape[0]
    small_rows = -(-small_n // width)
    head_n = head_w.shape[0] * head_w.shape[1]
    head_rows = -(-head_n // width)
    pad_rows = -(-(small_rows + head_rows) // PAD) * PAD

    def to_rows(flat, rows):
        return jnp.pad(flat, (0, rows * width - flat.shape[0])).reshape(rows, width)

    if is_small(count):
        vec = jnp.concatenate([low(gains_w[0]), low(shifts_w[0])])
        eights = [low(head_w[8 * k : 8 * k + 8]) for k in range(3)]
        above = jnp.concatenate([jnp.pad(vec, ((0, 0), (0, 384 - size)))] + eights, axis=1)
        extra = jnp.concatenate([above, jnp.pad(low(up_b), ((0, 7), (0, width - up_b.shape[1])))])
    else:
        extra = jnp.concatenate(
            [
                to_rows(small, small_rows),
                to_rows(low(head_w).reshape(-1), head_rows),
                jnp.zeros((pad_rows - small_rows - head_rows, width), BF),
            ]
        )
    cut = 2 * size

    order = Order(place)
    a0_g = Gather(order, jnp.concatenate([a_zero, extra]))
    f0_g, a1_g, f1_g = Gather(order, f_zero), Gather(order, a_one, True), Gather(order, f_one)
    a0_g.spare(4)
    f0_g.spare(4)
    f1_g.spare(4)
    a0_g.start()
    a1_g.start()
    a0_g.got, a1_g.got = order.wait(a0_g.got, a1_g.got)
    a0_g.done()
    a0_g.start()
    f0_g.start()
    a1_g.done()
    a1_g.start()
    a0_g.got, f0_g.got, a1_g.got = order.wait(a0_g.got, f0_g.got, a1_g.got)
    a0_g.done()
    a0_g.start()
    f0_g.done()
    f0_g.start()
    a1_g.done()
    a1_g.spare(2)
    a0_g.got, f0_g.got = order.wait(a0_g.got, f0_g.got)
    a0_g.done()
    a0_g.start()
    f0_g.done()
    f0_g.start()
    a1_g.start()
    f1_g.start()
    a0_g.swap_own()
    a0_g.got, f0_g.got, a1_g.got, a0_g.other_own, f1_g.got = order.wait(
        a0_g.got, f0_g.got, a1_g.got, a0_g.other_own, f1_g.got
    )
    f0_g.done()
    f0_g.start()
    a1_g.done()
    f1_g.done()
    f1_g.start()
    a1_part = a1_g.start_part(0)
    a0_g.swap_got()
    a0_g.other_got = order.wait(a0_g.other_got)
    a0_half = a0_g.halves(place, 2, size)
    n_g = gains_w.shape[1] * size
    n_s = shifts_w.shape[1] * size
    tail_halves = (a0_g.own, a0_g.got), (a0_g.other_own, a0_g.other_got)
    if is_small(count):
        vecs, cups, head = tails_of(place, cut, units, *tail_halves)
        head = low(head)
    else:
        vecs, cups, heads = [], [], []
        for tail in natural_tails(place, cut, *tail_halves):
            flat = tail[:, :small_rows].reshape(count, -1)[:, :small_n].astype(F32)
            vec = flat[:, : n_g + n_s].reshape(count, -1, size).transpose(1, 0, 2).reshape(-1, width)
            vecs.append(vec)
            cups.append(flat[:, n_g + n_s :].reshape(units, 1, width))
            block = tail[:, small_rows : small_rows + head_rows].reshape(count, -1)[:, :head_n]
            heads.append(block.reshape(count * head_w.shape[0], head_w.shape[1]))
        head = jnp.concatenate(heads)
    gain0 = shift0 = vecs[0]
    gain1 = shift1 = vecs[1]
    cup0, cup1 = cups[0], cups[1]

    own = lax.dynamic_slice_in_dim(tokens, section * mine, mine, 0)
    seg = lax.dynamic_slice_in_dim(segment_ids, section * mine, mine, 0)
    cot = lax.dynamic_slice_in_dim(cotangent, section * mine, mine, 0)
    rows = range(mine)
    seg_col = [jnp.broadcast_to(seg[r][:, None], (length, 128)) for r in rows]
    seg_row = [jnp.broadcast_to(seg[r][None], (8, length)) for r in rows]

    a0 = order.now([own[r] for r in rows])
    kept_a0 = [attn_fwd(False, place, a0[r], seg_col[r], seg_row[r], a0_half, shift0) for r in rows]
    kept_a0, f0_g.got, f1_g.got, a1_part = order.wait(kept_a0, f0_g.got, f1_g.got, a1_part)
    f0_g.swap_own()
    f0_g.swap_got()
    a1_g.got = (a1_part, a1_g.start_part(1))
    f1_g.done()
    f1_g.start()
    f0_g.other_own, f0_g.other_got = order.wait(f0_g.other_own, f0_g.other_got)
    n1 = order.now([kept[4] for kept in kept_a0])
    f0_half = f0_g.halves(place, units, size)
    a1_g.swap_own()
    kept_f0 = [ffn_fwd(False, place, n1[r], f0_half, cup0, gain0, shift0) for r in rows]
    kept_f0, a1_g.other_own, a1_g.got, f1_g.got = order.wait(kept_f0, a1_g.other_own, a1_g.got, f1_g.got)
    a1_g.swap_got()
    f1_g.done()
    f1_g.start()
    a1_g.other_got = order.wait(a1_g.other_got)
    a1 = order.now([kept[4] for kept in kept_f0])
    a1_half = a1_g.halves(place, 2, size)
    f1_g.swap_own()
    kept_a1 = [attn_fwd(True, place, a1[r], seg_col[r], seg_row[r], a1_half, shift1) for r in rows]
    kept_a1, f1_g.other_own, f1_g.got = order.wait(kept_a1, f1_g.other_own, f1_g.got)
    f1_g.swap_got()
    n1 = [kept[4] for kept in kept_a1]
    f1_half = f1_g.halves(place, units, size)
    kept_f1 = [ffn_fwd(False, place, n1[r], f1_half, cup1, gain1, shift1) for r in rows]

    def total(items):
        out = items[0]
        for item in items[1:]:
            out = jax.tree.map(lambda x, y: (x.astype(F32) + y.astype(F32)).astype(x.dtype), out, item)
        return out

    def ffn_back(near_first, given, kept_a, kept_f, planes, gain, shift):
        outs = [
            ffn_bwd(near_first, grad_place, given[r], *kept_f[r][2:4], *kept_f[r][:2], planes, *kept_a[r][4:6], gain, shift)
            for r in rows
        ]
        *chunk, sums, cup = total([(*o[:3], o[4], o[5]) for o in outs])
        rest = (total([o[6:] for o in outs]),) if outs[0][6:] else ()
        return in_planes(*chunk, place, (units, 0), count, near_first), [o[3] for o in outs], sums, cup, *rest

    def attn_back(near_first, more, d_out, a, kept, planes):
        outs = [attn_bwd(near_first, more, grad_place, d_out[r], a[r], seg_col[r], seg_row[r], *kept[r][:4], planes) for r in rows]
        *chunk, sums, sumo = total([(*o[:3], o[4], o[5]) for o in outs])
        return in_planes(*chunk, place, (2, 2), count, near_first), [o[3] for o in outs], sums, sumo

    given = [(kept_f1[r][4], cot[r], head) for r in rows]
    chunk, d_r, sums_f1, g_cup1, (g_head,) = ffn_back(False, given, kept_a1, kept_f1, f1_half, gain1, shift1)
    f1_r = Reduce(order, chunk)
    f1_r.wait()
    f1_r.start_upper()
    d_r = order.now(d_r)
    chunk, d_a1, sums_a1, sumo_a1 = attn_back(True, 0, d_r, a1, kept_a1, a1_half)
    d_a1, f1_r.upper, f1_r.there = order.wait(d_a1, f1_r.upper, f1_r.there)
    a1_r = Reduce(order, chunk, True)
    f1_r.start_lower()
    f1_r.start_from_upper()
    a1_r.wait()
    a1_r.spare(4)
    a1_r.start_upper()
    d_y0 = order.now([low(item) for item in d_a1])
    chunk, d_r, sums_f0, g_cup0 = ffn_back(False, [(item,) for item in d_y0], kept_a0, kept_f0, f0_half, gain0, shift0)
    d_r, f1_r.got, f1_r.ahead, a1_r.upper, a1_r.there = order.wait(
        d_r, f1_r.got, f1_r.ahead, a1_r.upper, a1_r.there
    )
    f0_r = Reduce(order, chunk)
    f1_r.join()
    f1_r.start()
    a1_r.start_lower()
    f0_r.wait()
    f0_r.start()
    d_r = order.now(d_r)
    chunk, d_a0, sums_a0, sumo_a0 = attn_back(
        False, PAD if is_small(count) else 0, d_r, a0, kept_a0, a0_half
    )
    d_a0, a1_r.got, f1_r.got, f0_r.got, there = order.wait(d_a0, a1_r.got, f1_r.got, f0_r.got, f0_r.there)
    f0_r.terms[1] = there

    def small_block(sums_a, sumo, sums_f, g_cup, head_part, core):
        gains = jnp.stack([sums_f[0], sums_f[1]]).reshape(2, count, size).transpose(1, 0, 2)
        shift = jnp.stack([sums_a[0], sums_a[1], sumo[0], sums_f[3], sums_f[4], sums_f[2]])
        shift = shift.reshape(6, count, size).transpose(1, 0, 2)
        flat = jnp.concatenate(
            [gains.reshape(count, -1), shift.reshape(count, -1), g_cup.reshape(count, -1)], axis=1
        )
        flat = jnp.pad(flat, ((0, 0), (0, small_rows * width - small_n)))
        piece = jnp.pad(head_part.reshape(count, -1), ((0, 0), (0, head_rows * width - head_n)))
        block = jnp.concatenate(
            [
                flat.reshape(count, small_rows, width),
                piece.reshape(count, head_rows, width),
                jnp.zeros((count, pad_rows - small_rows - head_rows, width), F32),
            ],
            axis=1,
        )
        return relative(low(block), place, core)

    if is_small(count):
        layer0 = (sums_a0, sumo_a0, sums_f0, g_cup0)
        layer1 = (sums_a1, sumo_a1, sums_f1, g_cup1)
        chunk = pack_tails(place, cut, layer0, layer1, g_head, chunk)
    else:
        half_head = g_head.reshape(2, -1, head_w.shape[1])
        tail0 = small_block(sums_a0, sumo_a0, sums_f0, g_cup0, half_head[0], 0)
        tail1 = small_block(sums_a1, sumo_a1, sums_f1, g_cup1, half_head[1], 1)
        tails = (jnp.where(first, tail0, tail1),) + in_halves(jnp.where(first, tail1, tail0))
        chunk = [jnp.concatenate(pair, axis=1) for pair in zip(chunk, tails)]
    a0_r = Reduce(order, chunk)
    a0_r.wait()
    a0_r.start()
    f0_r.start()
    f1_r.spare(1)
    f1_r.start()
    a1_r.start_from_upper()
    d_first, d_second = jnp.stack(d_a0), jnp.stack(d_a1)
    a0_r.got, a1_r.ahead, f1_r.got = order.wait(a0_r.got, a1_r.ahead, f1_r.got)
    a0_r.start()
    a1_r.join()
    f0_r.wait()
    f0_r.start()
    a1_r.start()
    got = across(order.now(d_first), 1), across(order.now(d_second), 0)
    a0_r.got, a1_r.got = order.wait(a0_r.got, a1_r.got)
    a0_r.spare(2)
    a0_r.start()
    done_f1 = f1_r.finish()
    a1_r.start()
    f0_r.got, got, done_f1 = order.wait(f0_r.got, got, done_f1)
    f0_r.spare(1)
    f0_r.start()
    input_grads = jnp.where(first, jnp.concatenate([d_first, got[0]]), jnp.concatenate([got[1], d_second]))
    a0_r.got, a1_r.got, input_grads = order.wait(a0_r.got, a1_r.got, input_grads)
    a0_r.spare(1)
    a0_r.start()
    done_a1 = a1_r.finish()
    f0_r.got, done_a1 = order.wait(f0_r.got, done_a1)
    done_f0 = f0_r.finish()

    def unite(zero_part, one_part):
        got = swap(jnp.where(first, one_part, zero_part))
        return jnp.where(first, zero_part, got), jnp.where(first, got, one_part)

    up_plane, down_plane = unite(done_f0, done_f1)
    a0_r.got, up_plane, down_plane = order.wait(a0_r.got, up_plane, down_plane)
    done_a0 = a0_r.finish()
    low_plane, high_plane = unite(done_a0[:cut], done_a1)

    def unit(array, j):
        return array[j * size : (j + 1) * size]

    qkv_grad = jnp.concatenate([unit(low_plane, 0), unit(low_plane, 1), unit(high_plane, 0)], axis=1)
    out_grad = unit(high_plane, 1)
    up_grad = jnp.concatenate([unit(up_plane, j) for j in range(units)], axis=1)
    down_grad = down_plane
    tail = done_a0[cut:]
    if is_small(count):
        gain_grad = tail[None, :2, :size]
        shift_grad = tail[None, 2:8, :size]
        cup_grad = tail[8:9, : up_b.shape[1]]
        head_grad = jnp.concatenate([tail[:8, 384 + 128 * k : 512 + 128 * k] for k in range(3)])
    else:
        flat = tail[:small_rows].reshape(-1)[:small_n]
        gain_grad = flat[:n_g].reshape(gains_w.shape)
        shift_grad = flat[n_g : n_g + n_s].reshape(shifts_w.shape)
        cup_grad = flat[n_g + n_s :].reshape(up_b.shape)
        head_grad = tail[small_rows : small_rows + head_rows].reshape(-1)[:head_n].reshape(head_w.shape)

    return (
        qkv_grad[None],
        out_grad[None],
        up_grad[None],
        down_grad[None],
        gain_grad,
        shift_grad,
        cup_grad,
        head_grad,
        input_grads[None],
    )


def solution(mesh):
    return jax.shard_map(
        shards,
        mesh=mesh,
        in_specs=(
            P("dp", None, None),
            P("dp", None),
            P("dp", None, None),
            P("section", "dp", None),
            P("section", "dp", None),
            P("section", "dp", None),
            P("section", "dp", None),
            P("section", None, "dp"),
            P("section", None, "dp"),
            P("section", "dp"),
            P(("section", "dp"), None),
        ),
        out_specs=(
            P("section", "dp", None),
            P("section", "dp", None),
            P("section", "dp", None),
            P("section", "dp", None),
            P("section", None, "dp"),
            P("section", None, "dp"),
            P("section", "dp"),
            P(("section", "dp"), None),
            P("section", "dp", None, None),
        ),
        check_vma=False,
    )
```

```python
import jax
import jax.numpy as jnp
from jax import lax
from jax.experimental import pallas as pl
from jax.experimental.pallas import tpu as pltpu
from jax.sharding import PartitionSpec as P

HEADS = 12
HDIM = 64
GROUP = 4
BLOCK = 128
PAD = 16
norm_eps = 1e-06
BF = jnp.bfloat16
F32 = jnp.float32
BOTH = ("section", "dp")
SCALE = HDIM ** (-0.5)

ERF_SCALE = 0.425
ERF_POLY = (
    0.11985147519825406,
    0.12072713574380309,
    0.10159474513684189,
    0.12334456743816431,
    -0.0435293372534038,
    0.19486821903107854,
    -0.15132025578595443,
    0.03446332841595847,
)


def dot(left, right, over_left=1, over_right=0):
    return lax.dot_general(
        left, right, (((over_left,), (over_right,)), ((), ())), preferred_element_type=F32
    )


def shape_of(shape, dtype):
    return jax.ShapeDtypeStruct(shape, dtype)


def whole_block(*shape):
    return pl.BlockSpec(shape, lambda g: (0,) * len(shape))


def gelu_pair(u):
    bell = jnp.exp(u * u * -0.5)
    t = 1.0 / (1.0 + (ERF_SCALE * 0.7071067811865476) * jnp.abs(u))
    poly = ERF_POLY[-1]
    for item in ERF_POLY[-2::-1]:
        poly = poly * t + item
    tail = bell * (poly * t)
    cdf = jnp.where(u < 0.0, tail, 1.0 - tail)
    return u * cdf, cdf + u * bell * 0.3989422804014327


def norm_stats(v):
    center = v - jnp.mean(v, axis=-1, keepdims=True)
    t = lax.rsqrt(jnp.mean(center * center, axis=-1, keepdims=True) + norm_eps)
    return center * t, t


def norm_back(dy, n, t, gain):
    dn = dy * gain
    mean = jnp.mean(dn, axis=-1, keepdims=True)
    along = jnp.mean(dn * n, axis=-1, keepdims=True)
    return t * (dn - mean - n * along)


def colsum(v):
    return jnp.sum(v, axis=0, keepdims=True)


def near(b, blocks):
    return max(0, b - 1) * BLOCK, min(blocks, b + 2) * BLOCK


def is_small(count):
    return count == 16


def steps_of(count, core, near_first):
    outer = [4 << j for j in range((count // 4).bit_length() - 1)]
    quad = [1, 2]
    if core:
        quad = [2, 1]
        if is_small(count):
            outer = outer[::-1]
    return quad + outer if near_first else outer + quad


def bit_of(me, mask):
    return (me >> (mask.bit_length() - 1)) & 1


def send_index(chip_z, chip_q, me, core, near_first):
    index = 0
    rel = (chip_z * 4 + chip_q) ^ me
    for j, mask in enumerate(steps_of(16, core, near_first)):
        index = index + bit_of(rel, mask) * (1 << j)
    return index


def each(count, body):
    lax.fori_loop(0, count, lambda j, _: (body(j), 0)[1], 0)


CHIP_BITS = (8, 4, 2, 1)


class Loads:
    def __init__(self, near_first, place_ref, own, other, targets, sem):
        self.near_first, self.place, self.planes = near_first, place_ref, (own, other)
        self.targets, self.sem = targets, sem

    def groups(self, plane, unit):
        order = steps_of(16, plane, self.near_first)
        together = len(self.targets[plane].shape) == 6
        out = []
        for p in range(2):
            for b2 in range(2):
                fixed = {order[3]: bit_of(self.place[0], order[3]) ^ p, order[2]: b2}
                if together:
                    assert plane and not self.near_first
                    fixed.update({8: unit >> 1, 4: unit & 1})
                    bits = [(unit & 1, unit >> 1)]
                elif plane == 0:
                    bits = [()]
                else:
                    bits = [(0,), (1,)]
                for lead in bits:
                    if lead and not together:
                        fixed = {**fixed, order[1]: lead[0]}
                    chips = tuple(fixed.get(mask, slice(None)) for mask in CHIP_BITS)
                    out.append((p, b2, lead, chips if together else (unit,) + chips))
        return out

    def start(self, plane, unit):
        size = self.targets[plane].shape[-2]

        def begin(section):
            pieces = self.planes[0] if plane == section else self.planes[1]
            if len(pieces) == 1:
                source = pieces[0].reshape(*self.targets[plane].shape)
            for k, (p, b2, lead, at) in enumerate(self.groups(plane, unit)):
                if len(pieces) == 1:
                    piece = source.at[at]
                else:
                    piece = pieces[1 + b2] if p and len(pieces) == 3 else pieces[p].at[b2]
                    for bit in lead:
                        piece = piece.at[bit]
                    if len(at) == 5:
                        rows = pl.ds(pl.multiple_of(unit * size, PAD), size)
                        piece = piece.at[(slice(None),) * (len(piece.shape) - 2) + (rows,)]
                pltpu.make_async_copy(piece, self.targets[plane].at[at], self.sem.at[plane, unit, k]).start()

        by_section(self.place[1], begin)

    def wait(self, plane, unit):
        for k, (_, _, _, at) in enumerate(self.groups(plane, unit)):
            to = self.targets[plane].at[at]
            pltpu.make_async_copy(to, to, self.sem.at[plane, unit, k]).wait()


def halves_view(pieces):
    if len(pieces) == 1:
        return pieces
    return [item.reshape((2,) * (item.shape[0].bit_length() - 1) + item.shape[1:]) for item in pieces]


def block_of(b, pair):
    return slice(b * BLOCK, (b + 1) * BLOCK), slice(pair * 2 * HDIM, (pair + 1) * 2 * HDIM)


def two_heads(pair, lane):
    zero = jnp.zeros_like(pair)
    return jnp.concatenate([jnp.where(lane < HDIM, pair, zero), jnp.where(lane >= HDIM, pair, zero)])


def attn_fwd_kernel(near_first, halves, place_ref, *refs):
    own, other = refs[:halves], refs[halves : 2 * halves]
    a_ref, sq_ref, sk_ref, bias_ref, shift_ref = refs[2 * halves : 2 * halves + 5]
    q_ref, k_ref, v_ref, o_ref, n_ref, t_ref, acc, low_w, high_w, sem = refs[2 * halves + 5 :]
    step = pl.program_id(0)
    length, width = a_ref.shape
    blocks = length // BLOCK
    a = a_ref[...]
    loads = Loads(near_first, place_ref, own, other, (low_w, high_w), sem)

    @pl.when(step == 0)
    def _():
        for plane, unit in ((0, 0), (0, 1), (1, 0), (1, 1)):
            loads.start(plane, unit)
        for plane, unit in ((0, 0), (0, 1), (1, 0)):
            loads.wait(plane, unit)

    cols = GROUP * HDIM
    here = pl.ds(pl.multiple_of(step * cols, cols), cols)

    def column(ref, j):
        return ref[j, :, :, :, :, :, here].reshape(width, cols)

    q_ref[...] = (dot(a, column(low_w, 0)) + bias_ref[2:3]).astype(BF)
    k_ref[...] = dot(a, column(low_w, 1)).astype(BF)
    v_ref[...] = (dot(a, column(high_w, 0)) + bias_ref[3:4]).astype(BF)
    lane = lax.broadcasted_iota(jnp.int32, (BLOCK, 2 * HDIM), 1)
    tiles = [(b, pair) for b in range(blocks) for pair in range(GROUP // 2)]

    def scores_of(b, pair):
        lo, hi = near(b, blocks)
        rows, lanes = block_of(b, pair)
        same = sq_ref[rows, 0:1] == sk_ref[0:1, lo:hi]
        scores = dot(two_heads(q_ref[rows, lanes] * SCALE, lane), k_ref[lo:hi, lanes], 1, 1)
        return jnp.where(jnp.concatenate([same, same]), scores, -1000000000.0)

    ahead = scores_of(*tiles[0])
    for j, (b, pair) in enumerate(tiles):
        lo, hi = near(b, blocks)
        rows, lanes = block_of(b, pair)
        scores = ahead
        if j + 1 < len(tiles):
            ahead = scores_of(*tiles[j + 1])
        grown = jnp.exp(scores - jnp.max(scores, axis=-1, keepdims=True))
        scale = 1.0 / jnp.sum(grown, axis=-1, keepdims=True)
        out = dot((grown * scale).astype(BF), v_ref[lo:hi, lanes])
        o_ref[rows, lanes] = jnp.where(lane < HDIM, out[:BLOCK], out[BLOCK:]).astype(BF)
    @pl.when(step == 0)
    def _():
        loads.wait(1, 1)

    part = dot(o_ref[...], high_w.at[1].reshape(width, width)[here, :])

    @pl.when(step == 0)
    def _():
        acc[...] = a.astype(F32) + shift_ref[4:5] + part

    @pl.when(step != 0)
    def _():
        acc[...] += part

    @pl.when(step == pl.num_programs(0) - 1)
    def _():
        n, t = norm_stats(acc[...])
        n_ref[...] = n
        t_ref[...] = jnp.broadcast_to(t, t_ref.shape)


SCALARS = pl.BlockSpec(memory_space=pltpu.SMEM)
NO_COST = pl.CostEstimate(flops=0, bytes_accessed=0, transcendentals=0)


ANYWHERE = pl.BlockSpec(memory_space=pl.ANY)


def attn_fwd(near_first, place, a, seg_col, seg_row, planes, shift):
    length, width = a.shape
    cols = GROUP * HDIM
    group = pl.BlockSpec((length, cols), lambda g: (0, g))
    half = (2, 2, 2, 2, 2, width // 16, width)
    halves = len(planes[0])
    return pl.pallas_call(
        lambda *refs: attn_fwd_kernel(near_first, halves, *refs),
        grid=(HEADS // GROUP,),
        in_specs=[SCALARS]
        + [ANYWHERE] * (2 * halves)
        + [whole_block(length, width), whole_block(length, 128), whole_block(8, length)]
        + [pl.BlockSpec((8, cols), lambda g: (0, g)), whole_block(8, width)],
        out_specs=[group] * 4 + [whole_block(length, width), whole_block(length, 128)],
        out_shape=[shape_of((length, width), BF)] * 4
        + [shape_of((length, width), F32), shape_of((length, 128), F32)],
        scratch_shapes=[
            pltpu.VMEM((length, width), F32),
            pltpu.VMEM(half, BF),
            pltpu.VMEM(half, BF),
            pltpu.SemaphoreType.DMA((2, 2, 8)),
        ],
        cost_estimate=NO_COST,
        name="attn_fwd",
    )(place, *halves_view(planes[0]), *halves_view(planes[1]), a, seg_col, seg_row, shift, shift)


def ffn_fwd_kernel(near_first, halves, place_ref, *refs):
    own, other = refs[:halves], refs[halves : 2 * halves]
    n1_ref, cup_ref, gain_ref, shift_ref = refs[2 * halves : 2 * halves + 4]
    g_ref, gp_ref, n_ref, t_ref, y_ref = refs[2 * halves + 4 : 2 * halves + 9]
    h1, acc, up_w, down_w, sem = refs[2 * halves + 9 :]
    step = pl.program_id(0)
    width = n1_ref.shape[1]
    loads = Loads(near_first, place_ref, own, other, (up_w, down_w), sem)
    units = up_w.shape[0]

    @pl.when(step == 0)
    def _():
        loads.start(0, 0)
        loads.start(1, 0)

    @pl.when(step == 0)
    def _():
        hidden = n1_ref[...] * gain_ref[0:1] + shift_ref[6:7]
        h1[...] = hidden.astype(BF)
        acc[...] = hidden + shift_ref[5:6]

    loads.wait(0, step)

    @pl.when(step + 1 < units)
    def _():
        loads.start(0, step + 1)
        loads.start(1, step + 1)

    loads.wait(1, step)
    up = up_w[step].reshape(width, width)
    down = down_w[step >> 1, step & 1].reshape(width, width)
    wide = 256
    parts = h1.shape[1] // wide

    def upper(j):
        cols = slice(j * wide, (j + 1) * wide)
        return dot(h1[...], up[:, cols]) + cup_ref[0, :, cols]

    ahead = upper(0)
    total = acc[...]
    for j in range(parts):
        cols = slice(j * wide, (j + 1) * wide)
        here = ahead
        if j + 1 < parts:
            ahead = upper(j + 1)
        g, slope = gelu_pair(here)
        g = g.astype(BF)
        g_ref[:, cols] = g
        gp_ref[:, cols] = slope.astype(BF)
        total = total + dot(g, down[cols])
    acc[...] = total

    @pl.when(step == pl.num_programs(0) - 1)
    def _():
        n, t = norm_stats(acc[...])
        n_ref[...] = n
        t_ref[...] = jnp.broadcast_to(t, t_ref.shape)
        y_ref[...] = (n * gain_ref[1:2] + shift_ref[7:8]).astype(BF)


def ffn_fwd(near_first, place, n1, planes, cup, gain, shift):
    length, width = n1.shape
    units = cup.shape[0]
    column = pl.BlockSpec((length, width), lambda g: (0, g))
    up = (units, 2, 2, 2, 2, width // 16, width)
    down = (2, 2, 2, 2, units * width // 16, width)
    halves = len(planes[0])
    return pl.pallas_call(
        lambda *refs: ffn_fwd_kernel(near_first, halves, *refs),
        grid=(units,),
        in_specs=[SCALARS]
        + [ANYWHERE] * (2 * halves)
        + [
            whole_block(length, width),
            pl.BlockSpec((1, 1, width), lambda g: (g, 0, 0)),
            whole_block(8, width),
            whole_block(8, width),
        ],
        out_specs=[column, column, whole_block(length, width), whole_block(length, 128), whole_block(length, width)],
        out_shape=[shape_of((length, units * width), BF)] * 2
        + [shape_of((length, width), F32), shape_of((length, 128), F32), shape_of((length, width), BF)],
        scratch_shapes=[
            pltpu.VMEM((length, width), BF),
            pltpu.VMEM((length, width), F32),
            pltpu.VMEM(up, BF),
            pltpu.VMEM(down, BF),
            pltpu.SemaphoreType.DMA((2, units, 4)),
        ],
        cost_estimate=NO_COST,
        name="ffn_fwd",
    )(place, *halves_view(planes[0]), *halves_view(planes[1]), n1, cup, gain, shift)


def by_section(section, action):
    for plane in range(2):
        pl.when(section == plane)(lambda plane=plane: action(plane))


def ffn_bwd_kernel(near_first, halves, head, place_ref, *refs):
    own, other = refs[:halves], refs[halves : 2 * halves]
    if head:
        y_ref, cot_ref, head_ref, g_head_ref = refs[2 * halves], refs[2 * halves + 1], refs[2 * halves + 2], refs[2 * halves + 17]
        refs = refs[: 2 * halves] + (None,) + refs[2 * halves + 3 : 2 * halves + 17] + refs[2 * halves + 18 :]
    dy_ref, n2_ref, t2_ref, g_ref, gp_ref, n1_ref, t1_ref, gain_ref, shift_ref = refs[2 * halves : 2 * halves + 9]
    keep_ref, high_ref, low_ref, dr1_ref, sums_ref, cup_ref = refs[2 * halves + 9 : 2 * halves + 15]
    h1, df, acc, gup, gdown, up_w, down_w, sem, load_sem = refs[2 * halves + 15 :]
    step = pl.program_id(0)
    loads = Loads(near_first, place_ref, own, other, (up_w, down_w), load_sem)

    @pl.when(step == 0)
    def _():
        loads.start(1, 0)
        loads.start(0, 0)

    last = pl.num_programs(0) - 1
    quads = outer = 4
    width = h1.shape[1]
    size = width // (quads * outer)

    @pl.when(step == 0)
    def _():
        n2 = n2_ref[...]
        if head:
            y = y_ref[...]
            proj = dot(y, head_ref[...])
            rho = lax.rsqrt(jnp.sum(proj * proj, axis=-1, keepdims=True) + norm_eps)
            cot = cot_ref[...].astype(F32)
            along = jnp.sum(proj * cot, axis=-1, keepdims=True)
            d_proj = (rho * cot - rho * rho * rho * proj * along).astype(BF)
            g_head_ref[...] = dot(y, d_proj, 0, 0)
            dy = dot(d_proj, head_ref[...], 1, 1)
        else:
            dy = dy_ref[...].astype(F32)
        dr2 = norm_back(dy, n2, t2_ref[:, 0:1], gain_ref[1:2])
        low = dr2.astype(BF)
        df[...] = low
        acc[...] = dr2
        h1[...] = (n1_ref[...] * gain_ref[0:1] + shift_ref[6:7]).astype(BF)
        sums_ref[...] = jnp.zeros_like(sums_ref)
        sums_ref[1:2] = colsum(dy * n2)
        sums_ref[2:3] = colsum(dy)
        sums_ref[3:4] = colsum(low.astype(F32))

    loads.wait(1, step)
    loads.wait(0, step)

    @pl.when(step < last)
    def _():
        loads.start(1, step + 1)
        loads.start(0, step + 1)

    d = df[...]
    down = dot(g_ref[...], d, 0, 0).astype(BF)
    tall = width // quads
    for q in range(quads):
        gdown[send_index(step, q, place_ref[0], 1, near_first)] = down[q * tall : (q + 1) * tall]
    du = (dot(d, down_w[step >> 1, step & 1].reshape(width, width), 1, 1) * gp_ref[...].astype(F32)).astype(BF)
    cup_ref[0] = colsum(du.astype(F32))
    up = dot(h1[...], du, 0, 0).astype(BF)
    for chip in range(quads * outer):
        at = send_index(chip // quads, chip % quads, place_ref[0], 0, near_first)
        gup[step, at] = up[chip * size : (chip + 1) * size]
    acc[...] += dot(du, up_w[step].reshape(width, width), 1, 1)

    def up_copies(section, j):
        rows = pl.ds(pl.multiple_of(j * size, PAD), size)
        if section == 0:
            return [pltpu.make_async_copy(gup.at[j], keep_ref.at[:, rows, :], sem.at[j, 0])]
        return [
            pltpu.make_async_copy(gup.at[j, :8], low_ref.at[:, rows, :], sem.at[j, 0]),
            pltpu.make_async_copy(gup.at[j, 8:], high_ref.at[:, rows, :], sem.at[j, 1]),
        ]

    def down_copies(section, j, start):
        for q in range(quads):
            at = send_index(j, q, place_ref[0], 1, near_first)
            if section == 1:
                copy = pltpu.make_async_copy(gdown.at[at], keep_ref.at[at], sem.at[j, 2 + q])
                copy.start() if start else copy.wait()
            elif not start:
                pltpu.make_async_copy(gdown.at[at], low_ref.at[0], sem.at[j, 2 + q]).wait()
            else:
                for part, ref in enumerate((low_ref, high_ref)):
                    @pl.when(at >> 3 == part)
                    def _():
                        pltpu.make_async_copy(gdown.at[at], ref.at[at & 7], sem.at[j, 2 + q]).start()

    def begin(section):
        for item in up_copies(section, step):
            item.start()
        down_copies(section, step, True)

    by_section(place_ref[1], begin)

    @pl.when(step == last)
    def _():
        dh = acc[...]
        n1 = n1_ref[...]
        dr1_ref[...] = norm_back(dh, n1, t1_ref[:, 0:1], gain_ref[0:1])
        sums_ref[0:1] = colsum(dh * n1)
        sums_ref[4:5] = colsum(dh)

        def finish(section):
            def one(j):
                for item in up_copies(section, j):
                    item.wait()
                down_copies(section, j, False)

            each(gup.shape[0], one)

        by_section(place_ref[1], finish)


def ffn_bwd(near_first, place, given, n2, t2, g, gp, planes, n1, t1, gain, shift):
    length, width = n1.shape
    units = g.shape[1] // width
    outer, size = 4, width // 16
    halves = len(planes[0])
    head = len(given) == 3
    up = (units, 2, 2, 2, 2, size, width)
    down = (2, 2, 2, 2, units * size, width)
    column = pl.BlockSpec((length, width), lambda g: (0, g))
    chunk, half_chunk = [shape_of((n, units * size, width), BF) for n in (16, 8)]
    return pl.pallas_call(
        lambda *refs: ffn_bwd_kernel(near_first, halves, head, *refs),
        grid=(units,),
        in_specs=[
            SCALARS,
            *[ANYWHERE] * (2 * halves),
            *[whole_block(*item.shape) for item in given],
            whole_block(length, width),
            whole_block(length, 128),
            column,
            column,
            whole_block(length, width),
            whole_block(length, 128),
            whole_block(8, width),
            whole_block(8, width),
        ],
        out_specs=[
            ANYWHERE,
            ANYWHERE,
            ANYWHERE,
            whole_block(length, width),
            whole_block(8, width),
            pl.BlockSpec((1, 1, width), lambda g: (g, 0, 0)),
        ]
        + [whole_block(*item.shape) for item in given[2:]],
        out_shape=[chunk, half_chunk, half_chunk, shape_of((length, width), F32), shape_of((8, width), F32), shape_of((units, 1, width), F32)]
        + [shape_of(item.shape, F32) for item in given[2:]],
        scratch_shapes=[
            pltpu.VMEM((length, width), BF),
            pltpu.VMEM((length, width), BF),
            pltpu.VMEM((length, width), F32),
            pltpu.VMEM((units, 16, size, width), BF),
            pltpu.VMEM((16, units * size, width), BF),
            pltpu.VMEM(up, BF),
            pltpu.VMEM(down, BF),
            pltpu.SemaphoreType.DMA((units, 6)),
            pltpu.SemaphoreType.DMA((2, units, 4)),
        ],
        cost_estimate=NO_COST,
        name="ffn_bwd",
    )(place, *halves_view(planes[0]), *halves_view(planes[1]), *given, n2, t2, g, gp, n1, t1, gain, shift)


def attn_bwd_kernel(near_first, halves, place_ref, *refs):
    own, other = refs[:halves], refs[halves : 2 * halves]
    dr_ref, a_ref, sq_ref, sk_ref, q_ref, k_ref, v_ref, o_ref = refs[2 * halves : 2 * halves + 8]
    keep_ref, high_ref, low_ref, da_ref, sums_ref, sumo_ref = refs[2 * halves + 8 : 2 * halves + 14]
    dat, do_sc, dq, dk, dv, grads, low_w, high_w, sem, load_sem = refs[2 * halves + 14 :]
    step = pl.program_id(0)
    loads = Loads(near_first, place_ref, own, other, (low_w, high_w), load_sem)

    @pl.when(step == 0)
    def _():
        for plane, unit in ((1, 1), (0, 0), (0, 1), (1, 0)):
            loads.start(plane, unit)

    length, width = a_ref.shape
    blocks = length // BLOCK
    quads = outer = 4
    size = width // (quads * outer)
    cols = GROUP * HDIM

    @pl.when(step == 0)
    def _():
        low = dr_ref[...].astype(BF)
        dat[...] = low
        da_ref[...] = dr_ref[...]
        sumo_ref[...] = jnp.zeros_like(sumo_ref)
        sumo_ref[0:1] = colsum(low.astype(F32))

    d = dat[...]
    grad_o = dot(o_ref[...], d, 0, 0).astype(BF)

    @pl.when(step == 0)
    def _():
        loads.wait(1, 1)

    now = pl.ds(pl.multiple_of(step * cols, cols), cols)
    do_sc[...] = dot(d, high_w.at[1].reshape(width, width)[now, :], 1, 1).astype(BF)
    dk[...] = jnp.zeros_like(dk)
    dv[...] = jnp.zeros_like(dv)
    lane = lax.broadcasted_iota(jnp.int32, (BLOCK, 2 * HDIM), 1)
    tiles = [(b, pair) for b in range(blocks) for pair in range(GROUP // 2)]

    def products(b, pair):
        lo, hi = near(b, blocks)
        rows, lanes = block_of(b, pair)
        same = sk_ref[lo:hi, 0:1] == sq_ref[0:1, rows]
        query = two_heads(q_ref[rows, lanes] * SCALE, lane)
        d_out = two_heads(do_sc[rows, lanes], lane)
        scores = dot(k_ref[lo:hi, lanes], query, 1, 1)
        scores = jnp.where(jnp.concatenate([same, same], axis=1), scores, -1000000000.0)
        return query, d_out, scores, dot(v_ref[lo:hi, lanes], d_out, 1, 1)

    ahead = products(*tiles[0])
    for j, (b, pair) in enumerate(tiles):
        lo, hi = near(b, blocks)
        rows, lanes = block_of(b, pair)
        query, d_out, scores, d_probs = ahead
        if j + 1 < len(tiles):
            ahead = products(*tiles[j + 1])
        grown = jnp.exp(scores - jnp.max(scores, axis=0, keepdims=True))
        probs = grown * (1.0 / jnp.sum(grown, axis=0, keepdims=True))
        d_scores = probs * (d_probs - jnp.sum(probs * d_probs, axis=0, keepdims=True))
        d_scores = d_scores.astype(BF)
        dv[lo:hi, lanes] += dot(probs.astype(BF), d_out)
        dk[lo:hi, lanes] += dot(d_scores, query)
        d_query = dot(d_scores, k_ref[lo:hi, lanes], 0, 0)
        dq[rows, lanes] = jnp.where(lane < HDIM, d_query[:BLOCK], d_query[BLOCK:]) * SCALE
    a = a_ref[...]
    out = da_ref[...]
    lows = (dq[...].astype(BF), dk[...].astype(BF), dv[...].astype(BF))
    made = []

    @pl.when(step == 0)
    def _():
        for plane, unit in ((0, 0), (0, 1), (1, 0)):
            loads.wait(plane, unit)

    for low, (w_ref, j) in zip(lows, ((low_w, 0), (low_w, 1), (high_w, 0))):
        made.append(dot(a, low, 0, 0).astype(BF))
        out = out + dot(low, w_ref[j, :, :, :, :, :, now].reshape(width, cols), 1, 1)
    da_ref[...] = out
    sums_ref[...] = jnp.zeros_like(sums_ref)
    sums_ref[0:1] = colsum(lows[0].astype(F32))
    sums_ref[1:2] = colsum(lows[2].astype(F32))
    steps = HEADS // GROUP

    def place_of(chip, core):
        return send_index(chip // quads, chip % quads, place_ref[0], core, near_first)

    for unit in range(3):
        for chip in range(quads * outer):
            grads[unit, place_of(chip, unit // 2), :, now] = made[unit][chip * size : (chip + 1) * size]
    for j in range(steps):
        @pl.when(step == j)
        def _(j=j):
            for chip in range(quads * outer):
                start, end = max(chip * size, j * cols), min((chip + 1) * size, (j + 1) * cols)
                if start < end:
                    rows = slice(start - chip * size, end - chip * size)
                    grads[3, place_of(chip, 1), rows, :] = grad_o[start - j * cols : end - j * cols]

    def copies(section, j, units):
        out = []
        for unit in units:
            rows = slice((unit % 2) * size, (unit % 2 + 1) * size)
            lanes = pl.ds(pl.multiple_of(j * cols, cols), cols) if unit < 3 else slice(None)
            if unit // 2 == section:
                pairs = [(grads.at[unit, :, :, lanes], keep_ref.at[:, rows, lanes])]
            else:
                pairs = [
                    (grads.at[unit, :8, :, lanes], low_ref.at[:, rows, lanes]),
                    (grads.at[unit, 8:, :, lanes], high_ref.at[:, rows, lanes]),
                ]
            out += [pltpu.make_async_copy(*pair, sem.at[unit, part, j]) for part, pair in enumerate(pairs)]
        return out

    def begin(section):
        for item in copies(section, step, range(3)):
            item.start()

    by_section(place_ref[1], begin)

    @pl.when(step == steps - 1)
    def _():
        def finish(section):
            for item in copies(section, 0, (3,)):
                item.start()

            def one(j):
                for item in copies(section, j, range(3)):
                    item.wait()

            each(steps, one)
            for item in copies(section, 0, (3,)):
                item.wait()

        by_section(place_ref[1], finish)


def attn_bwd(near_first, more, place, dr, a, seg_col, seg_row, q, k, v, o, planes):
    length, width = a.shape
    outer, size = 4, width // 16
    halves = len(planes[0])
    half = (2, 2, 2, 2, 2, size, width)
    cols = GROUP * HDIM
    group = pl.BlockSpec((length, cols), lambda g: (0, g))
    chunk, half_chunk = [shape_of((n, 2 * size + more, width), BF) for n in (16, 8)]
    return pl.pallas_call(
        lambda *refs: attn_bwd_kernel(near_first, halves, *refs),
        grid=(HEADS // GROUP,),
        in_specs=[
            SCALARS,
            *[ANYWHERE] * (2 * halves),
            whole_block(length, width),
            whole_block(length, width),
            whole_block(8, length),
            whole_block(length, 128),
        ]
        + [group] * 4,
        out_specs=[
            ANYWHERE,
            ANYWHERE,
            ANYWHERE,
            whole_block(length, width),
            pl.BlockSpec((8, cols), lambda g: (0, g)),
            whole_block(8, width),
        ],
        out_shape=[chunk, half_chunk, half_chunk, shape_of((length, width), F32), shape_of((8, width), F32), shape_of((8, width), F32)],
        scratch_shapes=[pltpu.VMEM((length, width), BF), pltpu.VMEM((length, cols), BF)]
        + [pltpu.VMEM((length, cols), F32)] * 3
        + [pltpu.VMEM((4, 16, size, width), BF), pltpu.VMEM(half, BF), pltpu.VMEM(half, BF)]
        + [pltpu.SemaphoreType.DMA((4, 2, HEADS // GROUP)), pltpu.SemaphoreType.DMA((2, 2, 8))],
        cost_estimate=NO_COST,
        name="attn_bwd",
    )(place, *halves_view(planes[0]), *halves_view(planes[1]), dr, a, seg_row, seg_col, q, k, v, o)


def flip(value, mask, other=None):
    count = lax.axis_size("dp")
    masks = (mask, mask if other is None else other)
    pairs = [(s * count + i, s * count + (i ^ masks[s])) for s in range(2) for i in range(count)]
    return lax.ppermute(value, BOTH, pairs)


def swap(value):
    count = lax.axis_size("dp")
    pairs = [(s * count + i, (1 - s) * count + i) for s in range(2) for i in range(count)]
    return lax.ppermute(value, BOTH, pairs)


def across(value, source):
    count = lax.axis_size("dp")
    return lax.ppermute(value, BOTH, [(source * count + i, (1 - source) * count + i) for i in range(count)])


class Order:
    def __init__(self, mark):
        self.mark = mark

    def wait(self, *values):
        leaves, tree = jax.tree.flatten(values)
        *leaves, self.mark = lax.optimization_barrier((*leaves, self.mark))
        out = jax.tree.unflatten(tree, leaves)
        return out[0] if len(values) == 1 else out

    def now(self, *values):
        leaves, tree = jax.tree.flatten(values)
        leaves = lax.optimization_barrier((*leaves, self.mark))[:-1]
        out = jax.tree.unflatten(tree, leaves)
        return out[0] if len(values) == 1 else out


class Gather:
    def __init__(self, order, block, near_first=False):
        self.order, self.own, self.near_first = order, block[None], near_first
        self.left = list(zip(*[steps_of(lax.axis_size("dp"), core, near_first) for core in range(2)]))

    def start(self):
        self.got = flip(self.order.now(self.own), *self.left[0])

    def start_part(self, part):
        half = self.own.shape[0] // 2
        return flip(self.order.now(self.own[part * half : (part + 1) * half]), *self.left[0])

    def done(self):
        masks = self.left.pop(0)
        high = (lax.axis_index("dp") & jnp.where(lax.axis_index("section") == 0, *masks)) != 0
        own, got = self.own, self.got
        self.own = jnp.where(high, jnp.concatenate([got, own]), jnp.concatenate([own, got]))

    def spare(self, steps):
        while len(self.left) > steps:
            self.start()
            self.done()

    def wait(self):
        self.got = self.order.wait(self.got)

    def swap_own(self):
        self.other_own = swap(self.order.now(self.own))

    def swap_got(self):
        self.other_got = jax.tree.map(lambda item: swap(self.order.now(item)), self.got)

    def halves(self, place, units, size):
        pairs = tuple(
            (own,) + (got if isinstance(got, tuple) else (got,))
            for own, got in ((self.own, self.got), (self.other_own, self.other_got))
        )
        if is_small(lax.axis_size("dp")):
            return pairs
        return natural_planes(place, units, size, self.near_first, *pairs)


def natural_planes(place, units, size, near_first, own, other):
    count = lax.axis_size("dp")
    out = []
    for section, halves in ((place[1], own), (1 - place[1], other)):
        both = jnp.concatenate(halves)
        at = []
        for core in range(2):
            order = steps_of(count, core, near_first)
            chips = jnp.arange(count)
            index = sum(bit_of(chips, mask) << j for j, mask in enumerate(order))
            at.append(index ^ (bit_of(place[0], order[-1]) << (len(order) - 1)))
        whole = jnp.take(both, jnp.where(section == 0, *at), axis=0)
        rows, width = whole.shape[1:]
        if size:
            by_unit = jnp.stack([whole[:, j * size : (j + 1) * size].reshape(width, width) for j in range(units)])
            if units != 2:
                flat = whole.reshape(units, width, width)
                by_unit = jnp.where(section == 0, by_unit.reshape(flat.shape), flat)
            whole = by_unit.reshape(units, 4, 4, width // 16, width)
        out.append((whole,))
    return out


def tail_kernel(cut, place_ref, *refs):
    halves, (vec_ref, cup_ref, head_ref, pieces, sem) = refs[:4], refs[4:]

    def move(section):
        for start in (True, False):
            for plane in range(2):
                order = steps_of(16, plane, False)
                for p in range(2):
                    source = halves[p if plane == section else 2 + p].at[:, cut:, :]

                    def by_index(index):
                        chip = sum(bit_of(index, 1 << j) * order[j] for j in range(3))
                        chip = chip + order[3] * (bit_of(place_ref[0], order[3]) ^ p)
                        to = pieces.at[plane, chip >> 2, chip & 3]
                        copy = pltpu.make_async_copy(source.at[index], to, sem.at[plane, 8 * p + index])
                        copy.start() if start else copy.wait()

                    each(8, by_index)

    by_section(place_ref[1], move)
    size = vec_ref.shape[2] // 16
    wide = cup_ref.shape[1] * size
    height = head_ref.shape[0] // 32
    for plane in range(2):
        for chip in range(16):
            piece = pieces[plane, chip // 4, chip % 4].astype(F32)
            vec_ref[plane, :, chip * size : (chip + 1) * size] = piece[:8, :size]
            at = (chip % 4) * wide
            cup_ref[plane, chip // 4, :, at : at + wide] = piece[8:9, :wide]
            for k in range(height // 8):
                row = (plane * 16 + chip) * height + 8 * k
                head_ref[row : row + 8, :] = piece[:8, 384 + 128 * k : 512 + 128 * k]


def tails_of(place, cut, units, own, other):
    width = own[0].shape[2]
    return pl.pallas_call(
        lambda *refs: tail_kernel(cut, *refs),
        in_specs=[SCALARS] + [ANYWHERE] * 4,
        out_specs=[pl.BlockSpec(memory_space=pltpu.VMEM)] * 3,
        out_shape=[shape_of((2, 8, width), F32), shape_of((2, units, 1, width), F32), shape_of((width, 128), F32)],
        scratch_shapes=[pltpu.VMEM((2, 4, 4, PAD, width), BF), pltpu.SemaphoreType.DMA((2, 16))],
        cost_estimate=NO_COST,
        name="tails",
    )(place, *own, *other)


def natural_tails(place, cut, own, other):
    own, other = jax.tree.map(lambda item: item[:, cut:], (own, other))
    (mine,), (there,) = natural_planes(place, 0, 0, False, own, other)
    first = place[1] == 0
    return jnp.where(first, mine, there), jnp.where(first, there, mine)


def pack_kernel(cut, place_ref, *refs):
    sums = (refs[0:4], refs[4:8])
    head_ref, _, _, _, keep_ref, high_ref, low_ref, pieces, sem = refs[8:]
    width = pieces.shape[3]
    size = width // 16
    height = head_ref.shape[0] // 32
    pieces[...] = jnp.zeros_like(pieces)
    for plane, (attn, out, ffn, cup) in enumerate(sums):
        wide = cup.shape[0] * size
        rows = [ffn[0:1], ffn[1:2], attn[0:1], attn[1:2], out[0:1], ffn[3:4], ffn[4:5], ffn[2:3]]
        vec = jnp.concatenate(rows)
        for chip in range(16):
            pieces[plane, chip, :8, :size] = vec[:, chip * size : (chip + 1) * size].astype(BF)
            at = (chip % 4) * wide
            pieces[plane, chip, 8:9, :wide] = cup[chip // 4, :, at : at + wide].astype(BF)
            for k in range(height // 8):
                row = (plane * 16 + chip) * height + 8 * k
                pieces[plane, chip, :8, 384 + 128 * k : 512 + 128 * k] = head_ref[row : row + 8, :].astype(BF)

    def move(section):
        for plane in range(2):
            def by_chip(chip):
                at = send_index(chip >> 2, chip & 3, place_ref[0], plane, False)
                source, this = pieces.at[plane, chip], sem.at[plane, chip]
                if plane == section:
                    pltpu.make_async_copy(source, keep_ref.at[at, cut:, :], this).start()
                    return
                for part, ref in enumerate((low_ref, high_ref)):
                    @pl.when(at >> 3 == part)
                    def _():
                        pltpu.make_async_copy(source, ref.at[at & 7, cut:, :], this).start()

            each(16, by_chip)
        for plane in range(2):
            def wait(chip):
                pltpu.make_async_copy(pieces.at[plane, chip], keep_ref.at[0, cut:, :], sem.at[plane, chip]).wait()

            each(16, wait)

    by_section(place_ref[1], move)


def pack_tails(place, cut, layer0, layer1, g_head, chunk):
    return pl.pallas_call(
        lambda *refs: pack_kernel(cut, *refs),
        in_specs=[SCALARS] + [pl.BlockSpec(memory_space=pltpu.VMEM)] * 9 + [ANYWHERE] * 3,
        out_specs=[ANYWHERE] * 3,
        out_shape=[shape_of(item.shape, BF) for item in chunk],
        input_output_aliases={10: 0, 11: 1, 12: 2},
        scratch_shapes=[pltpu.VMEM((2, 16, PAD, chunk[0].shape[2]), BF), pltpu.SemaphoreType.DMA((2, 16))],
        cost_estimate=NO_COST,
        name="pack",
    )(place, *layer0, *layer1, g_head, *chunk)


def in_chips(chunk, place, units, count, core, near_first):
    chips = jnp.arange(16)
    at = sum(bit_of(chips, mask) << j for j, mask in enumerate(steps_of(16, core, near_first)))
    chunk = jnp.take(chunk, at, axis=0)
    width = chunk.shape[2]
    if units:
        natural = chunk.reshape(16, units, -1, width).transpose(1, 0, 2, 3).reshape(units, count, -1, width)
        natural = natural.transpose(1, 0, 2, 3).reshape(count, -1, width)
    else:
        natural = chunk.reshape(count, -1, width)
    return relative(natural, place, core, near_first)


def in_planes(keep, high, low_half, place, units, count, near_first):
    if is_small(count):
        return keep, high, low_half
    send = jnp.concatenate([low_half, high])
    first = place[1] == 0
    keeps, sends = [
        [in_chips(item, place, units[core], count, core, near_first) for core in range(2)] for item in (keep, send)
    ]
    return (jnp.where(first, *keeps),) + in_halves(jnp.where(first, sends[1], sends[0]))


def in_halves(send):
    half = send.shape[0] // 2
    return send[half:], send[:half]


def relative(block, place, core, near_first=False):
    order = steps_of(block.shape[0], core, near_first)
    index = jnp.arange(block.shape[0])
    chips = sum(bit_of(index, 1 << j) * mask for j, mask in enumerate(order))
    return jnp.take(block, chips ^ place[0], axis=0)


def low(value):
    return value.astype(BF)


def add_low(terms, start, count):
    return low(sum(item[start : start + count].astype(F32) for item in terms))


class Reduce:
    def __init__(self, order, chunk, near_first=False):
        keep, high, low_half = chunk
        self.order = order
        self.left = list(zip(*[steps_of(lax.axis_size("dp"), core, near_first) for core in range(2)]))
        self.keep = keep
        self.got = swap(order.now(high))
        self.there = swap(order.now(low_half))
        self.terms = None

    def wait(self):
        self.got = self.order.wait(self.got)

    def start(self):
        if self.terms is None:
            half = self.got.shape[0]
            sent = add_low([self.keep[half:], self.got], 0, half)
            self.terms = [self.keep[:half], self.there]
        else:
            self.terms.append(self.got)
            half = self.got.shape[0] // 2
            sent = add_low(self.terms, half, half)
        self.got = flip(self.order.now(sent), *self.left.pop())

    def start_upper(self):
        self.half = self.got.shape[0]
        self.part = self.half // 2
        self.masks = self.left.pop()
        sent = add_low([self.keep[self.half :], self.got], self.part, self.part)
        self.upper = flip(self.order.now(sent), *self.masks)

    def start_lower(self):
        sent = add_low([self.keep[self.half :], self.got], 0, self.part)
        self.got = flip(self.order.now(sent), *self.masks)
        self.terms = [self.keep[: self.half], self.there]

    def start_from_upper(self):
        part = self.part
        terms = [item[part : 2 * part] for item in self.terms] + [self.upper]
        self.ahead = flip(self.order.now(add_low(terms, 0, part)), *self.left.pop())

    def join(self):
        self.terms.append(self.got)
        self.got = self.ahead

    def spare(self, steps):
        while len(self.left) > steps:
            self.start()

    def finish(self):
        return sum(item[0].astype(F32) for item in self.terms + [self.got])


def shards(tokens, segment_ids, cotangent, qkv_w, out_w, up_w, down_w, gains_w, shifts_w, up_b, head_w):
    count = lax.axis_size("dp")
    section = lax.axis_index("section")
    me = lax.axis_index("dp")
    first = section == 0
    place = jnp.stack([me, section]).astype(jnp.int32)
    grad_place = place if is_small(count) else jnp.stack([jnp.zeros_like(section), section]).astype(jnp.int32)
    rows_dev, length, width = tokens.shape
    mine = rows_dev // 2
    size = width // count
    ff = up_w.shape[2]
    units = ff // width

    def cols(array, n):
        return [array[:, j * width : (j + 1) * width] for j in range(n)]

    def planes_of(low_units, high_units):
        low_plane, high_plane = jnp.concatenate(low_units), jnp.concatenate(high_units)
        got = swap(jnp.where(first, high_plane, low_plane))
        return jnp.where(first, low_plane, got), jnp.where(first, got, high_plane)

    q_u, k_u, v_u = cols(low(qkv_w[0]), 3)
    a_zero, a_one = planes_of([q_u, k_u], [v_u, low(out_w[0])])
    f_zero, f_one = planes_of(cols(low(up_w[0]), units), [low(down_w[0])])
    small = low(jnp.concatenate([gains_w.reshape(-1), shifts_w.reshape(-1), up_b.reshape(-1)]))
    small_n = small.shape[0]
    small_rows = -(-small_n // width)
    head_n = head_w.shape[0] * head_w.shape[1]
    head_rows = -(-head_n // width)
    pad_rows = -(-(small_rows + head_rows) // PAD) * PAD

    def to_rows(flat, rows):
        return jnp.pad(flat, (0, rows * width - flat.shape[0])).reshape(rows, width)

    if is_small(count):
        vec = jnp.concatenate([low(gains_w[0]), low(shifts_w[0])])
        eights = [low(head_w[8 * k : 8 * k + 8]) for k in range(3)]
        above = jnp.concatenate([jnp.pad(vec, ((0, 0), (0, 384 - size)))] + eights, axis=1)
        extra = jnp.concatenate([above, jnp.pad(low(up_b), ((0, 7), (0, width - up_b.shape[1])))])
    else:
        extra = jnp.concatenate(
            [
                to_rows(small, small_rows),
                to_rows(low(head_w).reshape(-1), head_rows),
                jnp.zeros((pad_rows - small_rows - head_rows, width), BF),
            ]
        )
    cut = 2 * size

    order = Order(place)
    a0_g = Gather(order, jnp.concatenate([a_zero, extra]))
    f0_g, a1_g, f1_g = Gather(order, f_zero), Gather(order, a_one, True), Gather(order, f_one)
    a0_g.spare(4)
    f0_g.spare(4)
    f1_g.spare(4)
    a0_g.start()
    a1_g.start()
    a0_g.got, a1_g.got = order.wait(a0_g.got, a1_g.got)
    a0_g.done()
    a0_g.start()
    f0_g.start()
    a1_g.done()
    a1_g.start()
    a0_g.got, f0_g.got, a1_g.got = order.wait(a0_g.got, f0_g.got, a1_g.got)
    a0_g.done()
    a0_g.start()
    f0_g.done()
    f0_g.start()
    a1_g.done()
    a1_g.spare(2)
    a0_g.got, f0_g.got = order.wait(a0_g.got, f0_g.got)
    a0_g.done()
    a0_g.start()
    f0_g.done()
    f0_g.start()
    a1_g.start()
    f1_g.start()
    a0_g.swap_own()
    a0_g.got, f0_g.got, a1_g.got, a0_g.other_own, f1_g.got = order.wait(
        a0_g.got, f0_g.got, a1_g.got, a0_g.other_own, f1_g.got
    )
    f0_g.done()
    f0_g.start()
    a1_g.done()
    f1_g.done()
    f1_g.start()
    a1_part = a1_g.start_part(0)
    a0_g.swap_got()
    a0_g.other_got = order.wait(a0_g.other_got)
    a0_half = a0_g.halves(place, 2, size)
    n_g = gains_w.shape[1] * size
    n_s = shifts_w.shape[1] * size
    tail_halves = (a0_g.own, a0_g.got), (a0_g.other_own, a0_g.other_got)
    if is_small(count):
        vecs, cups, head = tails_of(place, cut, units, *tail_halves)
        head = low(head)
    else:
        vecs, cups, heads = [], [], []
        for tail in natural_tails(place, cut, *tail_halves):
            flat = tail[:, :small_rows].reshape(count, -1)[:, :small_n].astype(F32)
            vec = flat[:, : n_g + n_s].reshape(count, -1, size).transpose(1, 0, 2).reshape(-1, width)
            vecs.append(vec)
            cups.append(flat[:, n_g + n_s :].reshape(units, 1, width))
            block = tail[:, small_rows : small_rows + head_rows].reshape(count, -1)[:, :head_n]
            heads.append(block.reshape(count * head_w.shape[0], head_w.shape[1]))
        head = jnp.concatenate(heads)
    gain0 = shift0 = vecs[0]
    gain1 = shift1 = vecs[1]
    cup0, cup1 = cups[0], cups[1]

    own = lax.dynamic_slice_in_dim(tokens, section * mine, mine, 0)
    seg = lax.dynamic_slice_in_dim(segment_ids, section * mine, mine, 0)
    cot = lax.dynamic_slice_in_dim(cotangent, section * mine, mine, 0)
    rows = range(mine)
    seg_col = [jnp.broadcast_to(seg[r][:, None], (length, 128)) for r in rows]
    seg_row = [jnp.broadcast_to(seg[r][None], (8, length)) for r in rows]

    a0 = order.now([own[r] for r in rows])
    kept_a0 = [attn_fwd(False, place, a0[r], seg_col[r], seg_row[r], a0_half, shift0) for r in rows]
    kept_a0, f0_g.got, f1_g.got, a1_part = order.wait(kept_a0, f0_g.got, f1_g.got, a1_part)
    f0_g.swap_own()
    f0_g.swap_got()
    a1_g.got = (a1_part, a1_g.start_part(1))
    f1_g.done()
    f1_g.start()
    f0_g.other_own, f0_g.other_got = order.wait(f0_g.other_own, f0_g.other_got)
    n1 = order.now([kept[4] for kept in kept_a0])
    f0_half = f0_g.halves(place, units, size)
    a1_g.swap_own()
    kept_f0 = [ffn_fwd(False, place, n1[r], f0_half, cup0, gain0, shift0) for r in rows]
    kept_f0, a1_g.other_own, a1_g.got, f1_g.got = order.wait(kept_f0, a1_g.other_own, a1_g.got, f1_g.got)
    a1_g.swap_got()
    f1_g.done()
    f1_g.start()
    a1_g.other_got = order.wait(a1_g.other_got)
    a1 = order.now([kept[4] for kept in kept_f0])
    a1_half = a1_g.halves(place, 2, size)
    f1_g.swap_own()
    kept_a1 = [attn_fwd(True, place, a1[r], seg_col[r], seg_row[r], a1_half, shift1) for r in rows]
    kept_a1, f1_g.other_own, f1_g.got = order.wait(kept_a1, f1_g.other_own, f1_g.got)
    f1_g.swap_got()
    n1 = [kept[4] for kept in kept_a1]
    f1_half = f1_g.halves(place, units, size)
    kept_f1 = [ffn_fwd(False, place, n1[r], f1_half, cup1, gain1, shift1) for r in rows]

    def total(items):
        out = items[0]
        for item in items[1:]:
            out = jax.tree.map(lambda x, y: (x.astype(F32) + y.astype(F32)).astype(x.dtype), out, item)
        return out

    def ffn_back(near_first, given, kept_a, kept_f, planes, gain, shift):
        outs = [
            ffn_bwd(near_first, grad_place, given[r], *kept_f[r][2:4], *kept_f[r][:2], planes, *kept_a[r][4:6], gain, shift)
            for r in rows
        ]
        *chunk, sums, cup = total([(*o[:3], o[4], o[5]) for o in outs])
        rest = (total([o[6:] for o in outs]),) if outs[0][6:] else ()
        return in_planes(*chunk, place, (units, 0), count, near_first), [o[3] for o in outs], sums, cup, *rest

    def attn_back(near_first, more, d_out, a, kept, planes):
        outs = [attn_bwd(near_first, more, grad_place, d_out[r], a[r], seg_col[r], seg_row[r], *kept[r][:4], planes) for r in rows]
        *chunk, sums, sumo = total([(*o[:3], o[4], o[5]) for o in outs])
        return in_planes(*chunk, place, (2, 2), count, near_first), [o[3] for o in outs], sums, sumo

    given = [(kept_f1[r][4], cot[r], head) for r in rows]
    chunk, d_r, sums_f1, g_cup1, (g_head,) = ffn_back(False, given, kept_a1, kept_f1, f1_half, gain1, shift1)
    f1_r = Reduce(order, chunk)
    f1_r.wait()
    f1_r.start_upper()
    d_r = order.now(d_r)
    chunk, d_a1, sums_a1, sumo_a1 = attn_back(True, 0, d_r, a1, kept_a1, a1_half)
    d_a1, f1_r.upper, f1_r.there = order.wait(d_a1, f1_r.upper, f1_r.there)
    a1_r = Reduce(order, chunk, True)
    f1_r.start_lower()
    f1_r.start_from_upper()
    a1_r.wait()
    a1_r.spare(4)
    a1_r.start_upper()
    d_y0 = order.now([low(item) for item in d_a1])
    chunk, d_r, sums_f0, g_cup0 = ffn_back(False, [(item,) for item in d_y0], kept_a0, kept_f0, f0_half, gain0, shift0)
    d_r, f1_r.got, f1_r.ahead, a1_r.upper, a1_r.there = order.wait(
        d_r, f1_r.got, f1_r.ahead, a1_r.upper, a1_r.there
    )
    f0_r = Reduce(order, chunk)
    f1_r.join()
    f1_r.start()
    a1_r.start_lower()
    f0_r.wait()
    f0_r.start()
    d_second = jnp.stack(d_a1)
    from_second = across(order.now(d_second), 0)
    d_r = order.now(d_r)
    chunk, d_a0, sums_a0, sumo_a0 = attn_back(
        False, PAD if is_small(count) else 0, d_r, a0, kept_a0, a0_half
    )
    d_a0, a1_r.got, f1_r.got, f0_r.got, there, from_second = order.wait(
        d_a0, a1_r.got, f1_r.got, f0_r.got, f0_r.there, from_second
    )
    f0_r.terms[1] = there

    def small_block(sums_a, sumo, sums_f, g_cup, head_part, core):
        gains = jnp.stack([sums_f[0], sums_f[1]]).reshape(2, count, size).transpose(1, 0, 2)
        shift = jnp.stack([sums_a[0], sums_a[1], sumo[0], sums_f[3], sums_f[4], sums_f[2]])
        shift = shift.reshape(6, count, size).transpose(1, 0, 2)
        flat = jnp.concatenate(
            [gains.reshape(count, -1), shift.reshape(count, -1), g_cup.reshape(count, -1)], axis=1
        )
        flat = jnp.pad(flat, ((0, 0), (0, small_rows * width - small_n)))
        piece = jnp.pad(head_part.reshape(count, -1), ((0, 0), (0, head_rows * width - head_n)))
        block = jnp.concatenate(
            [
                flat.reshape(count, small_rows, width),
                piece.reshape(count, head_rows, width),
                jnp.zeros((count, pad_rows - small_rows - head_rows, width), F32),
            ],
            axis=1,
        )
        return relative(low(block), place, core)

    if is_small(count):
        layer0 = (sums_a0, sumo_a0, sums_f0, g_cup0)
        layer1 = (sums_a1, sumo_a1, sums_f1, g_cup1)
        chunk = pack_tails(place, cut, layer0, layer1, g_head, chunk)
    else:
        half_head = g_head.reshape(2, -1, head_w.shape[1])
        tail0 = small_block(sums_a0, sumo_a0, sums_f0, g_cup0, half_head[0], 0)
        tail1 = small_block(sums_a1, sumo_a1, sums_f1, g_cup1, half_head[1], 1)
        tails = (jnp.where(first, tail0, tail1),) + in_halves(jnp.where(first, tail1, tail0))
        chunk = [jnp.concatenate(pair, axis=1) for pair in zip(chunk, tails)]
    a0_r = Reduce(order, chunk)
    a0_r.wait()
    a0_r.start()
    f0_r.start()
    f1_r.spare(1)
    f1_r.start()
    a1_r.start_from_upper()
    d_first = jnp.stack(d_a0)
    a0_r.got, a1_r.ahead, f1_r.got = order.wait(a0_r.got, a1_r.ahead, f1_r.got)
    a0_r.start()
    a1_r.join()
    f0_r.wait()
    f0_r.start()
    a1_r.start()
    from_first = across(order.now(d_first), 1)
    a0_r.got, a1_r.got = order.wait(a0_r.got, a1_r.got)
    a0_r.spare(2)
    a0_r.start()
    done_f1 = f1_r.finish()
    a1_r.start()
    f0_r.got, from_first, done_f1 = order.wait(f0_r.got, from_first, done_f1)
    f0_r.spare(1)
    f0_r.start()
    input_grads = jnp.where(first, jnp.concatenate([d_first, from_first]), jnp.concatenate([from_second, d_second]))
    a0_r.got, a1_r.got, input_grads = order.wait(a0_r.got, a1_r.got, input_grads)
    a0_r.spare(1)
    a0_r.start()
    done_a1 = a1_r.finish()
    f0_r.got, done_a1 = order.wait(f0_r.got, done_a1)
    done_f0 = f0_r.finish()

    def unite(zero_part, one_part):
        got = swap(jnp.where(first, one_part, zero_part))
        return jnp.where(first, zero_part, got), jnp.where(first, got, one_part)

    up_plane, down_plane = unite(done_f0, done_f1)
    a0_r.got, up_plane, down_plane = order.wait(a0_r.got, up_plane, down_plane)
    done_a0 = a0_r.finish()
    low_plane, high_plane = unite(done_a0[:cut], done_a1)

    def unit(array, j):
        return array[j * size : (j + 1) * size]

    qkv_grad = jnp.concatenate([unit(low_plane, 0), unit(low_plane, 1), unit(high_plane, 0)], axis=1)
    out_grad = unit(high_plane, 1)
    up_grad = jnp.concatenate([unit(up_plane, j) for j in range(units)], axis=1)
    down_grad = down_plane
    tail = done_a0[cut:]
    if is_small(count):
        gain_grad = tail[None, :2, :size]
        shift_grad = tail[None, 2:8, :size]
        cup_grad = tail[8:9, : up_b.shape[1]]
        head_grad = jnp.concatenate([tail[:8, 384 + 128 * k : 512 + 128 * k] for k in range(3)])
    else:
        flat = tail[:small_rows].reshape(-1)[:small_n]
        gain_grad = flat[:n_g].reshape(gains_w.shape)
        shift_grad = flat[n_g : n_g + n_s].reshape(shifts_w.shape)
        cup_grad = flat[n_g + n_s :].reshape(up_b.shape)
        head_grad = tail[small_rows : small_rows + head_rows].reshape(-1)[:head_n].reshape(head_w.shape)

    return (
        qkv_grad[None],
        out_grad[None],
        up_grad[None],
        down_grad[None],
        gain_grad,
        shift_grad,
        cup_grad,
        head_grad,
        input_grads[None],
    )


def solution(mesh):
    return jax.shard_map(
        shards,
        mesh=mesh,
        in_specs=(
            P("dp", None, None),
            P("dp", None),
            P("dp", None, None),
            P("section", "dp", None),
            P("section", "dp", None),
            P("section", "dp", None),
            P("section", "dp", None),
            P("section", None, "dp"),
            P("section", None, "dp"),
            P("section", "dp"),
            P(("section", "dp"), None),
        ),
        out_specs=(
            P("section", "dp", None),
            P("section", "dp", None),
            P("section", "dp", None),
            P("section", "dp", None),
            P("section", None, "dp"),
            P("section", None, "dp"),
            P("section", "dp"),
            P(("section", "dp"), None),
            P("section", "dp", None, None),
        ),
        check_vma=False,
    )
```

```python
import jax
import jax.numpy as jnp
from jax import lax
from jax.experimental import pallas as pl
from jax.experimental.pallas import tpu as pltpu
from jax.sharding import PartitionSpec as P

HEADS = 12
HDIM = 64
GROUP = 4
BLOCK = 128
PAD = 16
norm_eps = 1e-06
BF = jnp.bfloat16
F32 = jnp.float32
BOTH = ("section", "dp")
SCALE = HDIM ** (-0.5)

ERF_SCALE = 0.425
ERF_POLY = (
    0.11985147519825406,
    0.12072713574380309,
    0.10159474513684189,
    0.12334456743816431,
    -0.0435293372534038,
    0.19486821903107854,
    -0.15132025578595443,
    0.03446332841595847,
)


def dot(left, right, over_left=1, over_right=0):
    return lax.dot_general(
        left, right, (((over_left,), (over_right,)), ((), ())), preferred_element_type=F32
    )


def shape_of(shape, dtype):
    return jax.ShapeDtypeStruct(shape, dtype)


def whole_block(*shape):
    return pl.BlockSpec(shape, lambda g: (0,) * len(shape))


def gelu_pair(u):
    bell = jnp.exp(u * u * -0.5)
    t = 1.0 / (1.0 + (ERF_SCALE * 0.7071067811865476) * jnp.abs(u))
    poly = ERF_POLY[-1]
    for item in ERF_POLY[-2::-1]:
        poly = poly * t + item
    tail = bell * (poly * t)
    cdf = jnp.where(u < 0.0, tail, 1.0 - tail)
    return u * cdf, cdf + u * bell * 0.3989422804014327


def norm_stats(v):
    center = v - jnp.mean(v, axis=-1, keepdims=True)
    t = lax.rsqrt(jnp.mean(center * center, axis=-1, keepdims=True) + norm_eps)
    return center * t, t


def norm_back(dy, n, t, gain):
    dn = dy * gain
    mean = jnp.mean(dn, axis=-1, keepdims=True)
    along = jnp.mean(dn * n, axis=-1, keepdims=True)
    return t * (dn - mean - n * along)


def colsum(v):
    return jnp.sum(v, axis=0, keepdims=True)


def near(b, blocks):
    return max(0, b - 1) * BLOCK, min(blocks, b + 2) * BLOCK


def is_small(count):
    return count == 16


def steps_of(count, core, near_first):
    outer = [4 << j for j in range((count // 4).bit_length() - 1)]
    quad = [1, 2]
    if core:
        quad = [2, 1]
        if is_small(count):
            outer = outer[::-1]
    return quad + outer if near_first else outer + quad


def bit_of(me, mask):
    return (me >> (mask.bit_length() - 1)) & 1


def send_index(chip_z, chip_q, me, core, near_first):
    index = 0
    rel = (chip_z * 4 + chip_q) ^ me
    for j, mask in enumerate(steps_of(16, core, near_first)):
        index = index + bit_of(rel, mask) * (1 << j)
    return index


def each(count, body):
    lax.fori_loop(0, count, lambda j, _: (body(j), 0)[1], 0)


CHIP_BITS = (8, 4, 2, 1)


class Loads:
    def __init__(self, near_first, place_ref, own, other, targets, sem):
        self.near_first, self.place, self.planes = near_first, place_ref, (own, other)
        self.targets, self.sem = targets, sem

    def groups(self, plane, unit):
        order = steps_of(16, plane, self.near_first)
        together = len(self.targets[plane].shape) == 6
        out = []
        for p in range(2):
            for b2 in range(2):
                fixed = {order[3]: bit_of(self.place[0], order[3]) ^ p, order[2]: b2}
                if together:
                    assert plane and not self.near_first
                    fixed.update({8: unit >> 1, 4: unit & 1})
                    bits = [(unit & 1, unit >> 1)]
                elif plane == 0:
                    bits = [()]
                else:
                    bits = [(0,), (1,)]
                for lead in bits:
                    if lead and not together:
                        fixed = {**fixed, order[1]: lead[0]}
                    chips = tuple(fixed.get(mask, slice(None)) for mask in CHIP_BITS)
                    out.append((p, b2, lead, chips if together else (unit,) + chips))
        return out

    def start(self, plane, unit):
        size = self.targets[plane].shape[-2]

        def begin(section):
            pieces = self.planes[0] if plane == section else self.planes[1]
            if len(pieces) == 1:
                source = pieces[0].reshape(*self.targets[plane].shape)
            for k, (p, b2, lead, at) in enumerate(self.groups(plane, unit)):
                if len(pieces) == 1:
                    piece = source.at[at]
                else:
                    piece = pieces[1 + b2] if p and len(pieces) == 3 else pieces[p].at[b2]
                    for bit in lead:
                        piece = piece.at[bit]
                    if len(at) == 5:
                        rows = pl.ds(pl.multiple_of(unit * size, PAD), size)
                        piece = piece.at[(slice(None),) * (len(piece.shape) - 2) + (rows,)]
                pltpu.make_async_copy(piece, self.targets[plane].at[at], self.sem.at[plane, unit, k]).start()

        by_section(self.place[1], begin)

    def wait(self, plane, unit):
        for k, (_, _, _, at) in enumerate(self.groups(plane, unit)):
            to = self.targets[plane].at[at]
            pltpu.make_async_copy(to, to, self.sem.at[plane, unit, k]).wait()


def halves_view(pieces):
    if len(pieces) == 1:
        return pieces
    return [item.reshape((2,) * (item.shape[0].bit_length() - 1) + item.shape[1:]) for item in pieces]


def block_of(b, pair):
    return slice(b * BLOCK, (b + 1) * BLOCK), slice(pair * 2 * HDIM, (pair + 1) * 2 * HDIM)


def two_heads(pair, lane):
    zero = jnp.zeros_like(pair)
    return jnp.concatenate([jnp.where(lane < HDIM, pair, zero), jnp.where(lane >= HDIM, pair, zero)])


def attn_fwd_kernel(near_first, halves, place_ref, *refs):
    own, other = refs[:halves], refs[halves : 2 * halves]
    a_ref, sq_ref, sk_ref, bias_ref, shift_ref = refs[2 * halves : 2 * halves + 5]
    q_ref, k_ref, v_ref, o_ref, n_ref, t_ref, acc, low_w, high_w, sem = refs[2 * halves + 5 :]
    step = pl.program_id(0)
    length, width = a_ref.shape
    blocks = length // BLOCK
    a = a_ref[...]
    loads = Loads(near_first, place_ref, own, other, (low_w, high_w), sem)

    @pl.when(step == 0)
    def _():
        for plane, unit in ((0, 0), (0, 1), (1, 0), (1, 1)):
            loads.start(plane, unit)
        for plane, unit in ((0, 0), (0, 1), (1, 0)):
            loads.wait(plane, unit)

    cols = GROUP * HDIM
    here = pl.ds(pl.multiple_of(step * cols, cols), cols)

    def column(ref, j):
        return ref[j, :, :, :, :, :, here].reshape(width, cols)

    q_ref[...] = (dot(a, column(low_w, 0)) + bias_ref[2:3]).astype(BF)
    k_ref[...] = dot(a, column(low_w, 1)).astype(BF)
    v_ref[...] = (dot(a, column(high_w, 0)) + bias_ref[3:4]).astype(BF)
    lane = lax.broadcasted_iota(jnp.int32, (BLOCK, 2 * HDIM), 1)
    tiles = [(b, pair) for b in range(blocks) for pair in range(GROUP // 2)]

    def scores_of(b, pair):
        lo, hi = near(b, blocks)
        rows, lanes = block_of(b, pair)
        same = sq_ref[rows, 0:1] == sk_ref[0:1, lo:hi]
        scores = dot(two_heads(q_ref[rows, lanes] * SCALE, lane), k_ref[lo:hi, lanes], 1, 1)
        return jnp.where(jnp.concatenate([same, same]), scores, -1000000000.0)

    ahead = scores_of(*tiles[0])
    for j, (b, pair) in enumerate(tiles):
        lo, hi = near(b, blocks)
        rows, lanes = block_of(b, pair)
        scores = ahead
        if j + 1 < len(tiles):
            ahead = scores_of(*tiles[j + 1])
        grown = jnp.exp(scores - jnp.max(scores, axis=-1, keepdims=True))
        scale = 1.0 / jnp.sum(grown, axis=-1, keepdims=True)
        out = dot((grown * scale).astype(BF), v_ref[lo:hi, lanes])
        o_ref[rows, lanes] = jnp.where(lane < HDIM, out[:BLOCK], out[BLOCK:]).astype(BF)
    @pl.when(step == 0)
    def _():
        loads.wait(1, 1)

    part = dot(o_ref[...], high_w.at[1].reshape(width, width)[here, :])

    @pl.when(step == 0)
    def _():
        acc[...] = a.astype(F32) + shift_ref[4:5] + part

    @pl.when(step != 0)
    def _():
        acc[...] += part

    @pl.when(step == pl.num_programs(0) - 1)
    def _():
        n, t = norm_stats(acc[...])
        n_ref[...] = n
        t_ref[...] = jnp.broadcast_to(t, t_ref.shape)


SCALARS = pl.BlockSpec(memory_space=pltpu.SMEM)
NO_COST = pl.CostEstimate(flops=0, bytes_accessed=0, transcendentals=0)


ANYWHERE = pl.BlockSpec(memory_space=pl.ANY)


def attn_fwd(near_first, place, a, seg_col, seg_row, planes, shift):
    length, width = a.shape
    cols = GROUP * HDIM
    group = pl.BlockSpec((length, cols), lambda g: (0, g))
    half = (2, 2, 2, 2, 2, width // 16, width)
    halves = len(planes[0])
    return pl.pallas_call(
        lambda *refs: attn_fwd_kernel(near_first, halves, *refs),
        grid=(HEADS // GROUP,),
        in_specs=[SCALARS]
        + [ANYWHERE] * (2 * halves)
        + [whole_block(length, width), whole_block(length, 128), whole_block(8, length)]
        + [pl.BlockSpec((8, cols), lambda g: (0, g)), whole_block(8, width)],
        out_specs=[group] * 4 + [whole_block(length, width), whole_block(length, 128)],
        out_shape=[shape_of((length, width), BF)] * 4
        + [shape_of((length, width), F32), shape_of((length, 128), F32)],
        scratch_shapes=[
            pltpu.VMEM((length, width), F32),
            pltpu.VMEM(half, BF),
            pltpu.VMEM(half, BF),
            pltpu.SemaphoreType.DMA((2, 2, 8)),
        ],
        cost_estimate=NO_COST,
        name="attn_fwd",
    )(place, *halves_view(planes[0]), *halves_view(planes[1]), a, seg_col, seg_row, shift, shift)


def ffn_fwd_kernel(near_first, halves, place_ref, *refs):
    own, other = refs[:halves], refs[halves : 2 * halves]
    n1_ref, cup_ref, gain_ref, shift_ref = refs[2 * halves : 2 * halves + 4]
    g_ref, gp_ref, n_ref, t_ref, y_ref = refs[2 * halves + 4 : 2 * halves + 9]
    h1, acc, up_w, down_w, sem = refs[2 * halves + 9 :]
    step = pl.program_id(0)
    width = n1_ref.shape[1]
    loads = Loads(near_first, place_ref, own, other, (up_w, down_w), sem)
    units = up_w.shape[0]

    @pl.when(step == 0)
    def _():
        loads.start(0, 0)
        loads.start(1, 0)

    @pl.when(step == 0)
    def _():
        hidden = n1_ref[...] * gain_ref[0:1] + shift_ref[6:7]
        h1[...] = hidden.astype(BF)
        acc[...] = hidden + shift_ref[5:6]

    loads.wait(0, step)

    @pl.when(step + 1 < units)
    def _():
        loads.start(0, step + 1)
        loads.start(1, step + 1)

    loads.wait(1, step)
    up = up_w[step].reshape(width, width)
    down = down_w[step >> 1, step & 1].reshape(width, width)
    wide = 256
    parts = h1.shape[1] // wide

    def upper(j):
        cols = slice(j * wide, (j + 1) * wide)
        return dot(h1[...], up[:, cols]) + cup_ref[0, :, cols]

    ahead = upper(0)
    total = acc[...]
    for j in range(parts):
        cols = slice(j * wide, (j + 1) * wide)
        here = ahead
        if j + 1 < parts:
            ahead = upper(j + 1)
        g, slope = gelu_pair(here)
        g = g.astype(BF)
        g_ref[:, cols] = g
        gp_ref[:, cols] = slope.astype(BF)
        total = total + dot(g, down[cols])
    acc[...] = total

    @pl.when(step == pl.num_programs(0) - 1)
    def _():
        n, t = norm_stats(acc[...])
        n_ref[...] = n.astype(BF)
        t_ref[...] = jnp.broadcast_to(t, t_ref.shape)
        y_ref[...] = (n * gain_ref[1:2] + shift_ref[7:8]).astype(BF)


def ffn_fwd(near_first, place, n1, planes, cup, gain, shift):
    length, width = n1.shape
    units = cup.shape[0]
    column = pl.BlockSpec((length, width), lambda g: (0, g))
    up = (units, 2, 2, 2, 2, width // 16, width)
    down = (2, 2, 2, 2, units * width // 16, width)
    halves = len(planes[0])
    return pl.pallas_call(
        lambda *refs: ffn_fwd_kernel(near_first, halves, *refs),
        grid=(units,),
        in_specs=[SCALARS]
        + [ANYWHERE] * (2 * halves)
        + [
            whole_block(length, width),
            pl.BlockSpec((1, 1, width), lambda g: (g, 0, 0)),
            whole_block(8, width),
            whole_block(8, width),
        ],
        out_specs=[column, column, whole_block(length, width), whole_block(length, 128), whole_block(length, width)],
        out_shape=[shape_of((length, units * width), BF)] * 2
        + [shape_of((length, width), BF), shape_of((length, 128), F32), shape_of((length, width), BF)],
        scratch_shapes=[
            pltpu.VMEM((length, width), BF),
            pltpu.VMEM((length, width), F32),
            pltpu.VMEM(up, BF),
            pltpu.VMEM(down, BF),
            pltpu.SemaphoreType.DMA((2, units, 4)),
        ],
        cost_estimate=NO_COST,
        name="ffn_fwd",
    )(place, *halves_view(planes[0]), *halves_view(planes[1]), n1, cup, gain, shift)


def by_section(section, action):
    for plane in range(2):
        pl.when(section == plane)(lambda plane=plane: action(plane))


def ffn_bwd_kernel(near_first, halves, head, place_ref, *refs):
    own, other = refs[:halves], refs[halves : 2 * halves]
    if head:
        y_ref, cot_ref, head_ref, g_head_ref = refs[2 * halves], refs[2 * halves + 1], refs[2 * halves + 2], refs[2 * halves + 17]
        refs = refs[: 2 * halves] + (None,) + refs[2 * halves + 3 : 2 * halves + 17] + refs[2 * halves + 18 :]
    dy_ref, n2_ref, t2_ref, g_ref, gp_ref, n1_ref, t1_ref, gain_ref, shift_ref = refs[2 * halves : 2 * halves + 9]
    keep_ref, high_ref, low_ref, dr1_ref, sums_ref, cup_ref = refs[2 * halves + 9 : 2 * halves + 15]
    h1, df, acc, gup, gdown, up_w, down_w, sem, load_sem = refs[2 * halves + 15 :]
    step = pl.program_id(0)
    loads = Loads(near_first, place_ref, own, other, (up_w, down_w), load_sem)

    @pl.when(step == 0)
    def _():
        loads.start(1, 0)
        loads.start(0, 0)

    last = pl.num_programs(0) - 1
    quads = outer = 4
    width = h1.shape[1]
    size = width // (quads * outer)

    @pl.when(step == 0)
    def _():
        n2 = n2_ref[...].astype(F32)
        if head:
            y = y_ref[...]
            proj = dot(y, head_ref[...])
            rho = lax.rsqrt(jnp.sum(proj * proj, axis=-1, keepdims=True) + norm_eps)
            cot = cot_ref[...].astype(F32)
            along = jnp.sum(proj * cot, axis=-1, keepdims=True)
            d_proj = (rho * cot - rho * rho * rho * proj * along).astype(BF)
            g_head_ref[...] = dot(y, d_proj, 0, 0)
            dy = dot(d_proj, head_ref[...], 1, 1)
        else:
            dy = dy_ref[...].astype(F32)
        dr2 = norm_back(dy, n2, t2_ref[:, 0:1], gain_ref[1:2])
        low = dr2.astype(BF)
        df[...] = low
        acc[...] = dr2
        h1[...] = (n1_ref[...] * gain_ref[0:1] + shift_ref[6:7]).astype(BF)
        sums_ref[...] = jnp.zeros_like(sums_ref)
        sums_ref[1:2] = colsum(dy * n2)
        sums_ref[2:3] = colsum(dy)
        sums_ref[3:4] = colsum(low.astype(F32))

    loads.wait(1, step)
    loads.wait(0, step)

    @pl.when(step < last)
    def _():
        loads.start(1, step + 1)
        loads.start(0, step + 1)

    d = df[...]
    down = dot(g_ref[...], d, 0, 0).astype(BF)
    tall = width // quads
    for q in range(quads):
        gdown[send_index(step, q, place_ref[0], 1, near_first)] = down[q * tall : (q + 1) * tall]
    du = (dot(d, down_w[step >> 1, step & 1].reshape(width, width), 1, 1) * gp_ref[...].astype(F32)).astype(BF)
    cup_ref[0] = colsum(du.astype(F32))
    up = dot(h1[...], du, 0, 0).astype(BF)
    for chip in range(quads * outer):
        at = send_index(chip // quads, chip % quads, place_ref[0], 0, near_first)
        gup[step, at] = up[chip * size : (chip + 1) * size]
    acc[...] += dot(du, up_w[step].reshape(width, width), 1, 1)

    def up_copies(section, j):
        rows = pl.ds(pl.multiple_of(j * size, PAD), size)
        if section == 0:
            return [pltpu.make_async_copy(gup.at[j], keep_ref.at[:, rows, :], sem.at[j, 0])]
        return [
            pltpu.make_async_copy(gup.at[j, :8], low_ref.at[:, rows, :], sem.at[j, 0]),
            pltpu.make_async_copy(gup.at[j, 8:], high_ref.at[:, rows, :], sem.at[j, 1]),
        ]

    def down_copies(section, j, start):
        for q in range(quads):
            at = send_index(j, q, place_ref[0], 1, near_first)
            if section == 1:
                copy = pltpu.make_async_copy(gdown.at[at], keep_ref.at[at], sem.at[j, 2 + q])
                copy.start() if start else copy.wait()
            elif not start:
                pltpu.make_async_copy(gdown.at[at], low_ref.at[0], sem.at[j, 2 + q]).wait()
            else:
                for part, ref in enumerate((low_ref, high_ref)):
                    @pl.when(at >> 3 == part)
                    def _():
                        pltpu.make_async_copy(gdown.at[at], ref.at[at & 7], sem.at[j, 2 + q]).start()

    def begin(section):
        for item in up_copies(section, step):
            item.start()
        down_copies(section, step, True)

    by_section(place_ref[1], begin)

    @pl.when(step == last)
    def _():
        dh = acc[...]
        n1 = n1_ref[...]
        dr1_ref[...] = norm_back(dh, n1, t1_ref[:, 0:1], gain_ref[0:1])
        sums_ref[0:1] = colsum(dh * n1)
        sums_ref[4:5] = colsum(dh)

        def finish(section):
            def one(j):
                for item in up_copies(section, j):
                    item.wait()
                down_copies(section, j, False)

            each(gup.shape[0], one)

        by_section(place_ref[1], finish)


def ffn_bwd(near_first, place, given, n2, t2, g, gp, planes, n1, t1, gain, shift):
    length, width = n1.shape
    units = g.shape[1] // width
    outer, size = 4, width // 16
    halves = len(planes[0])
    head = len(given) == 3
    up = (units, 2, 2, 2, 2, size, width)
    down = (2, 2, 2, 2, units * size, width)
    column = pl.BlockSpec((length, width), lambda g: (0, g))
    chunk, half_chunk = [shape_of((n, units * size, width), BF) for n in (16, 8)]
    return pl.pallas_call(
        lambda *refs: ffn_bwd_kernel(near_first, halves, head, *refs),
        grid=(units,),
        in_specs=[
            SCALARS,
            *[ANYWHERE] * (2 * halves),
            *[whole_block(*item.shape) for item in given],
            whole_block(length, width),
            whole_block(length, 128),
            column,
            column,
            whole_block(length, width),
            whole_block(length, 128),
            whole_block(8, width),
            whole_block(8, width),
        ],
        out_specs=[
            ANYWHERE,
            ANYWHERE,
            ANYWHERE,
            whole_block(length, width),
            whole_block(8, width),
            pl.BlockSpec((1, 1, width), lambda g: (g, 0, 0)),
        ]
        + [whole_block(*item.shape) for item in given[2:]],
        out_shape=[chunk, half_chunk, half_chunk, shape_of((length, width), F32), shape_of((8, width), F32), shape_of((units, 1, width), F32)]
        + [shape_of(item.shape, F32) for item in given[2:]],
        scratch_shapes=[
            pltpu.VMEM((length, width), BF),
            pltpu.VMEM((length, width), BF),
            pltpu.VMEM((length, width), F32),
            pltpu.VMEM((units, 16, size, width), BF),
            pltpu.VMEM((16, units * size, width), BF),
            pltpu.VMEM(up, BF),
            pltpu.VMEM(down, BF),
            pltpu.SemaphoreType.DMA((units, 6)),
            pltpu.SemaphoreType.DMA((2, units, 4)),
        ],
        cost_estimate=NO_COST,
        name="ffn_bwd",
    )(place, *halves_view(planes[0]), *halves_view(planes[1]), *given, n2, t2, g, gp, n1, t1, gain, shift)


def attn_bwd_kernel(near_first, halves, place_ref, *refs):
    own, other = refs[:halves], refs[halves : 2 * halves]
    dr_ref, a_ref, sq_ref, sk_ref, q_ref, k_ref, v_ref, o_ref = refs[2 * halves : 2 * halves + 8]
    keep_ref, high_ref, low_ref, da_ref, sums_ref, sumo_ref = refs[2 * halves + 8 : 2 * halves + 14]
    dat, do_sc, dq, dk, dv, grads, low_w, high_w, sem, load_sem = refs[2 * halves + 14 :]
    step = pl.program_id(0)
    loads = Loads(near_first, place_ref, own, other, (low_w, high_w), load_sem)

    @pl.when(step == 0)
    def _():
        for plane, unit in ((1, 1), (0, 0), (0, 1), (1, 0)):
            loads.start(plane, unit)

    length, width = a_ref.shape
    blocks = length // BLOCK
    quads = outer = 4
    size = width // (quads * outer)
    cols = GROUP * HDIM

    @pl.when(step == 0)
    def _():
        low = dr_ref[...].astype(BF)
        dat[...] = low
        da_ref[...] = dr_ref[...]
        sumo_ref[...] = jnp.zeros_like(sumo_ref)
        sumo_ref[0:1] = colsum(low.astype(F32))

    d = dat[...]
    grad_o = dot(o_ref[...], d, 0, 0).astype(BF)

    @pl.when(step == 0)
    def _():
        loads.wait(1, 1)

    now = pl.ds(pl.multiple_of(step * cols, cols), cols)
    do_sc[...] = dot(d, high_w.at[1].reshape(width, width)[now, :], 1, 1).astype(BF)
    dk[...] = jnp.zeros_like(dk)
    dv[...] = jnp.zeros_like(dv)
    lane = lax.broadcasted_iota(jnp.int32, (BLOCK, 2 * HDIM), 1)
    tiles = [(b, pair) for b in range(blocks) for pair in range(GROUP // 2)]

    def products(b, pair):
        lo, hi = near(b, blocks)
        rows, lanes = block_of(b, pair)
        same = sk_ref[lo:hi, 0:1] == sq_ref[0:1, rows]
        query = two_heads(q_ref[rows, lanes] * SCALE, lane)
        d_out = two_heads(do_sc[rows, lanes], lane)
        scores = dot(k_ref[lo:hi, lanes], query, 1, 1)
        scores = jnp.where(jnp.concatenate([same, same], axis=1), scores, -1000000000.0)
        return query, d_out, scores, dot(v_ref[lo:hi, lanes], d_out, 1, 1)

    ahead = products(*tiles[0])
    for j, (b, pair) in enumerate(tiles):
        lo, hi = near(b, blocks)
        rows, lanes = block_of(b, pair)
        query, d_out, scores, d_probs = ahead
        if j + 1 < len(tiles):
            ahead = products(*tiles[j + 1])
        grown = jnp.exp(scores - jnp.max(scores, axis=0, keepdims=True))
        probs = grown * (1.0 / jnp.sum(grown, axis=0, keepdims=True))
        d_scores = probs * (d_probs - jnp.sum(probs * d_probs, axis=0, keepdims=True))
        d_scores = d_scores.astype(BF)
        dv[lo:hi, lanes] += dot(probs.astype(BF), d_out)
        dk[lo:hi, lanes] += dot(d_scores, query)
        d_query = dot(d_scores, k_ref[lo:hi, lanes], 0, 0)
        dq[rows, lanes] = jnp.where(lane < HDIM, d_query[:BLOCK], d_query[BLOCK:]) * SCALE
    a = a_ref[...]
    out = da_ref[...]
    lows = (dq[...].astype(BF), dk[...].astype(BF), dv[...].astype(BF))
    made = []

    @pl.when(step == 0)
    def _():
        for plane, unit in ((0, 0), (0, 1), (1, 0)):
            loads.wait(plane, unit)

    for low, (w_ref, j) in zip(lows, ((low_w, 0), (low_w, 1), (high_w, 0))):
        made.append(dot(a, low, 0, 0).astype(BF))
        out = out + dot(low, w_ref[j, :, :, :, :, :, now].reshape(width, cols), 1, 1)
    da_ref[...] = out
    sums_ref[...] = jnp.zeros_like(sums_ref)
    sums_ref[0:1] = colsum(lows[0].astype(F32))
    sums_ref[1:2] = colsum(lows[2].astype(F32))
    steps = HEADS // GROUP

    def place_of(chip, core):
        return send_index(chip // quads, chip % quads, place_ref[0], core, near_first)

    for unit in range(3):
        for chip in range(quads * outer):
            grads[unit, place_of(chip, unit // 2), :, now] = made[unit][chip * size : (chip + 1) * size]
    for j in range(steps):
        @pl.when(step == j)
        def _(j=j):
            for chip in range(quads * outer):
                start, end = max(chip * size, j * cols), min((chip + 1) * size, (j + 1) * cols)
                if start < end:
                    rows = slice(start - chip * size, end - chip * size)
                    grads[3, place_of(chip, 1), rows, :] = grad_o[start - j * cols : end - j * cols]

    def copies(section, j, units):
        out = []
        for unit in units:
            rows = slice((unit % 2) * size, (unit % 2 + 1) * size)
            lanes = pl.ds(pl.multiple_of(j * cols, cols), cols) if unit < 3 else slice(None)
            if unit // 2 == section:
                pairs = [(grads.at[unit, :, :, lanes], keep_ref.at[:, rows, lanes])]
            else:
                pairs = [
                    (grads.at[unit, :8, :, lanes], low_ref.at[:, rows, lanes]),
                    (grads.at[unit, 8:, :, lanes], high_ref.at[:, rows, lanes]),
                ]
            out += [pltpu.make_async_copy(*pair, sem.at[unit, part, j]) for part, pair in enumerate(pairs)]
        return out

    def begin(section):
        for item in copies(section, step, range(3)):
            item.start()

    by_section(place_ref[1], begin)

    @pl.when(step == steps - 1)
    def _():
        def finish(section):
            for item in copies(section, 0, (3,)):
                item.start()

            def one(j):
                for item in copies(section, j, range(3)):
                    item.wait()

            each(steps, one)
            for item in copies(section, 0, (3,)):
                item.wait()

        by_section(place_ref[1], finish)


def attn_bwd(near_first, more, place, dr, a, seg_col, seg_row, q, k, v, o, planes):
    length, width = a.shape
    outer, size = 4, width // 16
    halves = len(planes[0])
    half = (2, 2, 2, 2, 2, size, width)
    cols = GROUP * HDIM
    group = pl.BlockSpec((length, cols), lambda g: (0, g))
    chunk, half_chunk = [shape_of((n, 2 * size + more, width), BF) for n in (16, 8)]
    return pl.pallas_call(
        lambda *refs: attn_bwd_kernel(near_first, halves, *refs),
        grid=(HEADS // GROUP,),
        in_specs=[
            SCALARS,
            *[ANYWHERE] * (2 * halves),
            whole_block(length, width),
            whole_block(length, width),
            whole_block(8, length),
            whole_block(length, 128),
        ]
        + [group] * 4,
        out_specs=[
            ANYWHERE,
            ANYWHERE,
            ANYWHERE,
            whole_block(length, width),
            pl.BlockSpec((8, cols), lambda g: (0, g)),
            whole_block(8, width),
        ],
        out_shape=[chunk, half_chunk, half_chunk, shape_of((length, width), F32), shape_of((8, width), F32), shape_of((8, width), F32)],
        scratch_shapes=[pltpu.VMEM((length, width), BF), pltpu.VMEM((length, cols), BF)]
        + [pltpu.VMEM((length, cols), F32)] * 3
        + [pltpu.VMEM((4, 16, size, width), BF), pltpu.VMEM(half, BF), pltpu.VMEM(half, BF)]
        + [pltpu.SemaphoreType.DMA((4, 2, HEADS // GROUP)), pltpu.SemaphoreType.DMA((2, 2, 8))],
        cost_estimate=NO_COST,
        name="attn_bwd",
    )(place, *halves_view(planes[0]), *halves_view(planes[1]), dr, a, seg_row, seg_col, q, k, v, o)


def flip(value, mask, other=None):
    count = lax.axis_size("dp")
    masks = (mask, mask if other is None else other)
    pairs = [(s * count + i, s * count + (i ^ masks[s])) for s in range(2) for i in range(count)]
    return lax.ppermute(value, BOTH, pairs)


def swap(value):
    count = lax.axis_size("dp")
    pairs = [(s * count + i, (1 - s) * count + i) for s in range(2) for i in range(count)]
    return lax.ppermute(value, BOTH, pairs)


def across(value, source):
    count = lax.axis_size("dp")
    return lax.ppermute(value, BOTH, [(source * count + i, (1 - source) * count + i) for i in range(count)])


class Order:
    def __init__(self, mark):
        self.mark = mark

    def wait(self, *values):
        leaves, tree = jax.tree.flatten(values)
        *leaves, self.mark = lax.optimization_barrier((*leaves, self.mark))
        out = jax.tree.unflatten(tree, leaves)
        return out[0] if len(values) == 1 else out

    def now(self, *values):
        leaves, tree = jax.tree.flatten(values)
        leaves = lax.optimization_barrier((*leaves, self.mark))[:-1]
        out = jax.tree.unflatten(tree, leaves)
        return out[0] if len(values) == 1 else out


class Gather:
    def __init__(self, order, block, near_first=False):
        self.order, self.own, self.near_first = order, block[None], near_first
        self.left = list(zip(*[steps_of(lax.axis_size("dp"), core, near_first) for core in range(2)]))

    def start(self):
        self.got = flip(self.order.now(self.own), *self.left[0])

    def start_part(self, part):
        half = self.own.shape[0] // 2
        return flip(self.order.now(self.own[part * half : (part + 1) * half]), *self.left[0])

    def done(self):
        masks = self.left.pop(0)
        high = (lax.axis_index("dp") & jnp.where(lax.axis_index("section") == 0, *masks)) != 0
        own, got = self.own, self.got
        self.own = jnp.where(high, jnp.concatenate([got, own]), jnp.concatenate([own, got]))

    def spare(self, steps):
        while len(self.left) > steps:
            self.start()
            self.done()

    def wait(self):
        self.got = self.order.wait(self.got)

    def swap_own(self):
        self.other_own = swap(self.order.now(self.own))

    def swap_got(self):
        self.other_got = jax.tree.map(lambda item: swap(self.order.now(item)), self.got)

    def halves(self, place, units, size):
        pairs = tuple(
            (own,) + (got if isinstance(got, tuple) else (got,))
            for own, got in ((self.own, self.got), (self.other_own, self.other_got))
        )
        if is_small(lax.axis_size("dp")):
            return pairs
        return natural_planes(place, units, size, self.near_first, *pairs)


def natural_planes(place, units, size, near_first, own, other):
    count = lax.axis_size("dp")
    out = []
    for section, halves in ((place[1], own), (1 - place[1], other)):
        both = jnp.concatenate(halves)
        at = []
        for core in range(2):
            order = steps_of(count, core, near_first)
            chips = jnp.arange(count)
            index = sum(bit_of(chips, mask) << j for j, mask in enumerate(order))
            at.append(index ^ (bit_of(place[0], order[-1]) << (len(order) - 1)))
        whole = jnp.take(both, jnp.where(section == 0, *at), axis=0)
        rows, width = whole.shape[1:]
        if size:
            by_unit = jnp.stack([whole[:, j * size : (j + 1) * size].reshape(width, width) for j in range(units)])
            if units != 2:
                flat = whole.reshape(units, width, width)
                by_unit = jnp.where(section == 0, by_unit.reshape(flat.shape), flat)
            whole = by_unit.reshape(units, 4, 4, width // 16, width)
        out.append((whole,))
    return out


def tail_kernel(cut, place_ref, *refs):
    halves, (vec_ref, cup_ref, head_ref, pieces, sem) = refs[:4], refs[4:]

    def move(section):
        for start in (True, False):
            for plane in range(2):
                order = steps_of(16, plane, False)
                for p in range(2):
                    source = halves[p if plane == section else 2 + p].at[:, cut:, :]

                    def by_index(index):
                        chip = sum(bit_of(index, 1 << j) * order[j] for j in range(3))
                        chip = chip + order[3] * (bit_of(place_ref[0], order[3]) ^ p)
                        to = pieces.at[plane, chip >> 2, chip & 3]
                        copy = pltpu.make_async_copy(source.at[index], to, sem.at[plane, 8 * p + index])
                        copy.start() if start else copy.wait()

                    each(8, by_index)

    by_section(place_ref[1], move)
    size = vec_ref.shape[2] // 16
    wide = cup_ref.shape[1] * size
    height = head_ref.shape[0] // 32
    for plane in range(2):
        for chip in range(16):
            piece = pieces[plane, chip // 4, chip % 4].astype(F32)
            vec_ref[plane, :, chip * size : (chip + 1) * size] = piece[:8, :size]
            at = (chip % 4) * wide
            cup_ref[plane, chip // 4, :, at : at + wide] = piece[8:9, :wide]
            for k in range(height // 8):
                row = (plane * 16 + chip) * height + 8 * k
                head_ref[row : row + 8, :] = piece[:8, 384 + 128 * k : 512 + 128 * k]


def tails_of(place, cut, units, own, other):
    width = own[0].shape[2]
    return pl.pallas_call(
        lambda *refs: tail_kernel(cut, *refs),
        in_specs=[SCALARS] + [ANYWHERE] * 4,
        out_specs=[pl.BlockSpec(memory_space=pltpu.VMEM)] * 3,
        out_shape=[shape_of((2, 8, width), F32), shape_of((2, units, 1, width), F32), shape_of((width, 128), F32)],
        scratch_shapes=[pltpu.VMEM((2, 4, 4, PAD, width), BF), pltpu.SemaphoreType.DMA((2, 16))],
        cost_estimate=NO_COST,
        name="tails",
    )(place, *own, *other)


def natural_tails(place, cut, own, other):
    own, other = jax.tree.map(lambda item: item[:, cut:], (own, other))
    (mine,), (there,) = natural_planes(place, 0, 0, False, own, other)
    first = place[1] == 0
    return jnp.where(first, mine, there), jnp.where(first, there, mine)


def pack_kernel(cut, place_ref, *refs):
    sums = (refs[0:4], refs[4:8])
    head_ref, _, _, _, keep_ref, high_ref, low_ref, pieces, sem = refs[8:]
    width = pieces.shape[3]
    size = width // 16
    height = head_ref.shape[0] // 32
    pieces[...] = jnp.zeros_like(pieces)
    for plane, (attn, out, ffn, cup) in enumerate(sums):
        wide = cup.shape[0] * size
        rows = [ffn[0:1], ffn[1:2], attn[0:1], attn[1:2], out[0:1], ffn[3:4], ffn[4:5], ffn[2:3]]
        vec = jnp.concatenate(rows)
        for chip in range(16):
            pieces[plane, chip, :8, :size] = vec[:, chip * size : (chip + 1) * size].astype(BF)
            at = (chip % 4) * wide
            pieces[plane, chip, 8:9, :wide] = cup[chip // 4, :, at : at + wide].astype(BF)
            for k in range(height // 8):
                row = (plane * 16 + chip) * height + 8 * k
                pieces[plane, chip, :8, 384 + 128 * k : 512 + 128 * k] = head_ref[row : row + 8, :].astype(BF)

    def move(section):
        for plane in range(2):
            def by_chip(chip):
                at = send_index(chip >> 2, chip & 3, place_ref[0], plane, False)
                source, this = pieces.at[plane, chip], sem.at[plane, chip]
                if plane == section:
                    pltpu.make_async_copy(source, keep_ref.at[at, cut:, :], this).start()
                    return
                for part, ref in enumerate((low_ref, high_ref)):
                    @pl.when(at >> 3 == part)
                    def _():
                        pltpu.make_async_copy(source, ref.at[at & 7, cut:, :], this).start()

            each(16, by_chip)
        for plane in range(2):
            def wait(chip):
                pltpu.make_async_copy(pieces.at[plane, chip], keep_ref.at[0, cut:, :], sem.at[plane, chip]).wait()

            each(16, wait)

    by_section(place_ref[1], move)


def pack_tails(place, cut, layer0, layer1, g_head, chunk):
    return pl.pallas_call(
        lambda *refs: pack_kernel(cut, *refs),
        in_specs=[SCALARS] + [pl.BlockSpec(memory_space=pltpu.VMEM)] * 9 + [ANYWHERE] * 3,
        out_specs=[ANYWHERE] * 3,
        out_shape=[shape_of(item.shape, BF) for item in chunk],
        input_output_aliases={10: 0, 11: 1, 12: 2},
        scratch_shapes=[pltpu.VMEM((2, 16, PAD, chunk[0].shape[2]), BF), pltpu.SemaphoreType.DMA((2, 16))],
        cost_estimate=NO_COST,
        name="pack",
    )(place, *layer0, *layer1, g_head, *chunk)


def in_chips(chunk, place, units, count, core, near_first):
    chips = jnp.arange(16)
    at = sum(bit_of(chips, mask) << j for j, mask in enumerate(steps_of(16, core, near_first)))
    chunk = jnp.take(chunk, at, axis=0)
    width = chunk.shape[2]
    if units:
        natural = chunk.reshape(16, units, -1, width).transpose(1, 0, 2, 3).reshape(units, count, -1, width)
        natural = natural.transpose(1, 0, 2, 3).reshape(count, -1, width)
    else:
        natural = chunk.reshape(count, -1, width)
    return relative(natural, place, core, near_first)


def in_planes(keep, high, low_half, place, units, count, near_first):
    if is_small(count):
        return keep, high, low_half
    send = jnp.concatenate([low_half, high])
    first = place[1] == 0
    keeps, sends = [
        [in_chips(item, place, units[core], count, core, near_first) for core in range(2)] for item in (keep, send)
    ]
    return (jnp.where(first, *keeps),) + in_halves(jnp.where(first, sends[1], sends[0]))


def in_halves(send):
    half = send.shape[0] // 2
    return send[half:], send[:half]


def relative(block, place, core, near_first=False):
    order = steps_of(block.shape[0], core, near_first)
    index = jnp.arange(block.shape[0])
    chips = sum(bit_of(index, 1 << j) * mask for j, mask in enumerate(order))
    return jnp.take(block, chips ^ place[0], axis=0)


def low(value):
    return value.astype(BF)


def add_low(terms, start, count):
    return low(sum(item[start : start + count].astype(F32) for item in terms))


class Reduce:
    def __init__(self, order, chunk, near_first=False):
        keep, high, low_half = chunk
        self.order = order
        self.left = list(zip(*[steps_of(lax.axis_size("dp"), core, near_first) for core in range(2)]))
        self.keep = keep
        self.got = swap(order.now(high))
        self.there = swap(order.now(low_half))
        self.terms = None

    def wait(self):
        self.got = self.order.wait(self.got)

    def start(self):
        if self.terms is None:
            half = self.got.shape[0]
            sent = add_low([self.keep[half:], self.got], 0, half)
            self.terms = [self.keep[:half], self.there]
        else:
            self.terms.append(self.got)
            half = self.got.shape[0] // 2
            sent = add_low(self.terms, half, half)
        self.got = flip(self.order.now(sent), *self.left.pop())

    def start_upper(self):
        self.half = self.got.shape[0]
        self.part = self.half // 2
        self.masks = self.left.pop()
        sent = add_low([self.keep[self.half :], self.got], self.part, self.part)
        self.upper = flip(self.order.now(sent), *self.masks)

    def start_lower(self):
        sent = add_low([self.keep[self.half :], self.got], 0, self.part)
        self.got = flip(self.order.now(sent), *self.masks)
        self.terms = [self.keep[: self.half], self.there]

    def start_from_upper(self):
        part = self.part
        terms = [item[part : 2 * part] for item in self.terms] + [self.upper]
        self.ahead = flip(self.order.now(add_low(terms, 0, part)), *self.left.pop())

    def join(self):
        self.terms.append(self.got)
        self.got = self.ahead

    def spare(self, steps):
        while len(self.left) > steps:
            self.start()

    def finish(self):
        return sum(item[0].astype(F32) for item in self.terms + [self.got])


def shards(tokens, segment_ids, cotangent, qkv_w, out_w, up_w, down_w, gains_w, shifts_w, up_b, head_w):
    count = lax.axis_size("dp")
    section = lax.axis_index("section")
    me = lax.axis_index("dp")
    first = section == 0
    place = jnp.stack([me, section]).astype(jnp.int32)
    grad_place = place if is_small(count) else jnp.stack([jnp.zeros_like(section), section]).astype(jnp.int32)
    rows_dev, length, width = tokens.shape
    mine = rows_dev // 2
    size = width // count
    ff = up_w.shape[2]
    units = ff // width

    def cols(array, n):
        return [array[:, j * width : (j + 1) * width] for j in range(n)]

    def planes_of(low_units, high_units):
        low_plane, high_plane = jnp.concatenate(low_units), jnp.concatenate(high_units)
        got = swap(jnp.where(first, high_plane, low_plane))
        return jnp.where(first, low_plane, got), jnp.where(first, got, high_plane)

    q_u, k_u, v_u = cols(low(qkv_w[0]), 3)
    a_zero, a_one = planes_of([q_u, k_u], [v_u, low(out_w[0])])
    f_zero, f_one = planes_of(cols(low(up_w[0]), units), [low(down_w[0])])
    small = low(jnp.concatenate([gains_w.reshape(-1), shifts_w.reshape(-1), up_b.reshape(-1)]))
    small_n = small.shape[0]
    small_rows = -(-small_n // width)
    head_n = head_w.shape[0] * head_w.shape[1]
    head_rows = -(-head_n // width)
    pad_rows = -(-(small_rows + head_rows) // PAD) * PAD

    def to_rows(flat, rows):
        return jnp.pad(flat, (0, rows * width - flat.shape[0])).reshape(rows, width)

    if is_small(count):
        vec = jnp.concatenate([low(gains_w[0]), low(shifts_w[0])])
        eights = [low(head_w[8 * k : 8 * k + 8]) for k in range(3)]
        above = jnp.concatenate([jnp.pad(vec, ((0, 0), (0, 384 - size)))] + eights, axis=1)
        extra = jnp.concatenate([above, jnp.pad(low(up_b), ((0, 7), (0, width - up_b.shape[1])))])
    else:
        extra = jnp.concatenate(
            [
                to_rows(small, small_rows),
                to_rows(low(head_w).reshape(-1), head_rows),
                jnp.zeros((pad_rows - small_rows - head_rows, width), BF),
            ]
        )
    cut = 2 * size

    order = Order(place)
    a0_g = Gather(order, jnp.concatenate([a_zero, extra]))
    f0_g, a1_g, f1_g = Gather(order, f_zero), Gather(order, a_one, True), Gather(order, f_one)
    a0_g.spare(4)
    f0_g.spare(4)
    f1_g.spare(4)
    a0_g.start()
    a1_g.start()
    a0_g.got, a1_g.got = order.wait(a0_g.got, a1_g.got)
    a0_g.done()
    a0_g.start()
    f0_g.start()
    a1_g.done()
    a1_g.start()
    a0_g.got, f0_g.got, a1_g.got = order.wait(a0_g.got, f0_g.got, a1_g.got)
    a0_g.done()
    a0_g.start()
    f0_g.done()
    f0_g.start()
    a1_g.done()
    a1_g.spare(2)
    a0_g.got, f0_g.got = order.wait(a0_g.got, f0_g.got)
    a0_g.done()
    a0_g.start()
    f0_g.done()
    f0_g.start()
    a1_g.start()
    f1_g.start()
    a0_g.swap_own()
    a0_g.got, f0_g.got, a1_g.got, a0_g.other_own, f1_g.got = order.wait(
        a0_g.got, f0_g.got, a1_g.got, a0_g.other_own, f1_g.got
    )
    f0_g.done()
    f0_g.start()
    a1_g.done()
    f1_g.done()
    f1_g.start()
    a1_part = a1_g.start_part(0)
    a0_g.swap_got()
    a0_g.other_got = order.wait(a0_g.other_got)
    a0_half = a0_g.halves(place, 2, size)
    n_g = gains_w.shape[1] * size
    n_s = shifts_w.shape[1] * size
    tail_halves = (a0_g.own, a0_g.got), (a0_g.other_own, a0_g.other_got)
    if is_small(count):
        vecs, cups, head = tails_of(place, cut, units, *tail_halves)
        head = low(head)
    else:
        vecs, cups, heads = [], [], []
        for tail in natural_tails(place, cut, *tail_halves):
            flat = tail[:, :small_rows].reshape(count, -1)[:, :small_n].astype(F32)
            vec = flat[:, : n_g + n_s].reshape(count, -1, size).transpose(1, 0, 2).reshape(-1, width)
            vecs.append(vec)
            cups.append(flat[:, n_g + n_s :].reshape(units, 1, width))
            block = tail[:, small_rows : small_rows + head_rows].reshape(count, -1)[:, :head_n]
            heads.append(block.reshape(count * head_w.shape[0], head_w.shape[1]))
        head = jnp.concatenate(heads)
    gain0 = shift0 = vecs[0]
    gain1 = shift1 = vecs[1]
    cup0, cup1 = cups[0], cups[1]

    own = lax.dynamic_slice_in_dim(tokens, section * mine, mine, 0)
    seg = lax.dynamic_slice_in_dim(segment_ids, section * mine, mine, 0)
    cot = lax.dynamic_slice_in_dim(cotangent, section * mine, mine, 0)
    rows = range(mine)
    seg_col = [jnp.broadcast_to(seg[r][:, None], (length, 128)) for r in rows]
    seg_row = [jnp.broadcast_to(seg[r][None], (8, length)) for r in rows]

    a0 = order.now([own[r] for r in rows])
    kept_a0 = [attn_fwd(False, place, a0[r], seg_col[r], seg_row[r], a0_half, shift0) for r in rows]
    kept_a0, f0_g.got, f1_g.got, a1_part = order.wait(kept_a0, f0_g.got, f1_g.got, a1_part)
    f0_g.swap_own()
    f0_g.swap_got()
    a1_g.got = (a1_part, a1_g.start_part(1))
    f1_g.done()
    f1_g.start()
    f0_g.other_own, f0_g.other_got = order.wait(f0_g.other_own, f0_g.other_got)
    n1 = order.now([kept[4] for kept in kept_a0])
    f0_half = f0_g.halves(place, units, size)
    a1_g.swap_own()
    kept_f0 = [ffn_fwd(False, place, n1[r], f0_half, cup0, gain0, shift0) for r in rows]
    kept_f0, a1_g.other_own, a1_g.got, f1_g.got = order.wait(kept_f0, a1_g.other_own, a1_g.got, f1_g.got)
    a1_g.swap_got()
    f1_g.done()
    f1_g.start()
    a1_g.other_got = order.wait(a1_g.other_got)
    a1 = order.now([kept[4] for kept in kept_f0])
    a1_half = a1_g.halves(place, 2, size)
    f1_g.swap_own()
    kept_a1 = [attn_fwd(True, place, a1[r], seg_col[r], seg_row[r], a1_half, shift1) for r in rows]
    kept_a1, f1_g.other_own, f1_g.got = order.wait(kept_a1, f1_g.other_own, f1_g.got)
    f1_g.swap_got()
    n1 = [kept[4] for kept in kept_a1]
    f1_half = f1_g.halves(place, units, size)
    kept_f1 = [ffn_fwd(False, place, n1[r], f1_half, cup1, gain1, shift1) for r in rows]

    def total(items):
        out = items[0]
        for item in items[1:]:
            out = jax.tree.map(lambda x, y: (x.astype(F32) + y.astype(F32)).astype(x.dtype), out, item)
        return out

    def ffn_back(near_first, given, kept_a, kept_f, planes, gain, shift):
        outs = [
            ffn_bwd(near_first, grad_place, given[r], *kept_f[r][2:4], *kept_f[r][:2], planes, *kept_a[r][4:6], gain, shift)
            for r in rows
        ]
        *chunk, sums, cup = total([(*o[:3], o[4], o[5]) for o in outs])
        rest = (total([o[6:] for o in outs]),) if outs[0][6:] else ()
        return in_planes(*chunk, place, (units, 0), count, near_first), [o[3] for o in outs], sums, cup, *rest

    def attn_back(near_first, more, d_out, a, kept, planes):
        outs = [attn_bwd(near_first, more, grad_place, d_out[r], a[r], seg_col[r], seg_row[r], *kept[r][:4], planes) for r in rows]
        *chunk, sums, sumo = total([(*o[:3], o[4], o[5]) for o in outs])
        return in_planes(*chunk, place, (2, 2), count, near_first), [o[3] for o in outs], sums, sumo

    given = [(kept_f1[r][4], cot[r], head) for r in rows]
    chunk, d_r, sums_f1, g_cup1, (g_head,) = ffn_back(False, given, kept_a1, kept_f1, f1_half, gain1, shift1)
    f1_r = Reduce(order, chunk)
    f1_r.wait()
    f1_r.start_upper()
    d_r = order.now(d_r)
    chunk, d_a1, sums_a1, sumo_a1 = attn_back(True, 0, d_r, a1, kept_a1, a1_half)
    d_a1, f1_r.upper, f1_r.there = order.wait(d_a1, f1_r.upper, f1_r.there)
    a1_r = Reduce(order, chunk, True)
    f1_r.start_lower()
    f1_r.start_from_upper()
    a1_r.wait()
    a1_r.spare(4)
    a1_r.start_upper()
    d_y0 = order.now([low(item) for item in d_a1])
    chunk, d_r, sums_f0, g_cup0 = ffn_back(False, [(item,) for item in d_y0], kept_a0, kept_f0, f0_half, gain0, shift0)
    d_r, f1_r.got, f1_r.ahead, a1_r.upper, a1_r.there = order.wait(
        d_r, f1_r.got, f1_r.ahead, a1_r.upper, a1_r.there
    )
    f0_r = Reduce(order, chunk)
    f1_r.join()
    f1_r.start()
    a1_r.start_lower()
    f0_r.wait()
    f0_r.start()
    d_second = jnp.stack(d_a1)
    from_second = across(order.now(d_second), 0)
    d_r = order.now(d_r)
    chunk, d_a0, sums_a0, sumo_a0 = attn_back(
        False, PAD if is_small(count) else 0, d_r, a0, kept_a0, a0_half
    )
    d_a0, a1_r.got, f1_r.got, f0_r.got, there, from_second = order.wait(
        d_a0, a1_r.got, f1_r.got, f0_r.got, f0_r.there, from_second
    )
    f0_r.terms[1] = there

    def small_block(sums_a, sumo, sums_f, g_cup, head_part, core):
        gains = jnp.stack([sums_f[0], sums_f[1]]).reshape(2, count, size).transpose(1, 0, 2)
        shift = jnp.stack([sums_a[0], sums_a[1], sumo[0], sums_f[3], sums_f[4], sums_f[2]])
        shift = shift.reshape(6, count, size).transpose(1, 0, 2)
        flat = jnp.concatenate(
            [gains.reshape(count, -1), shift.reshape(count, -1), g_cup.reshape(count, -1)], axis=1
        )
        flat = jnp.pad(flat, ((0, 0), (0, small_rows * width - small_n)))
        piece = jnp.pad(head_part.reshape(count, -1), ((0, 0), (0, head_rows * width - head_n)))
        block = jnp.concatenate(
            [
                flat.reshape(count, small_rows, width),
                piece.reshape(count, head_rows, width),
                jnp.zeros((count, pad_rows - small_rows - head_rows, width), F32),
            ],
            axis=1,
        )
        return relative(low(block), place, core)

    if is_small(count):
        layer0 = (sums_a0, sumo_a0, sums_f0, g_cup0)
        layer1 = (sums_a1, sumo_a1, sums_f1, g_cup1)
        chunk = pack_tails(place, cut, layer0, layer1, g_head, chunk)
    else:
        half_head = g_head.reshape(2, -1, head_w.shape[1])
        tail0 = small_block(sums_a0, sumo_a0, sums_f0, g_cup0, half_head[0], 0)
        tail1 = small_block(sums_a1, sumo_a1, sums_f1, g_cup1, half_head[1], 1)
        tails = (jnp.where(first, tail0, tail1),) + in_halves(jnp.where(first, tail1, tail0))
        chunk = [jnp.concatenate(pair, axis=1) for pair in zip(chunk, tails)]
    a0_r = Reduce(order, chunk)
    a0_r.wait()
    a0_r.start()
    f0_r.start()
    f1_r.spare(1)
    f1_r.start()
    a1_r.start_from_upper()
    d_first = jnp.stack(d_a0)
    a0_r.got, a1_r.ahead, f1_r.got = order.wait(a0_r.got, a1_r.ahead, f1_r.got)
    a0_r.start()
    a1_r.join()
    f0_r.wait()
    f0_r.start()
    a1_r.start()
    from_first = across(order.now(d_first), 1)
    a0_r.got, a1_r.got = order.wait(a0_r.got, a1_r.got)
    a0_r.spare(2)
    a0_r.start()
    done_f1 = f1_r.finish()
    a1_r.start()
    f0_r.got, from_first, done_f1 = order.wait(f0_r.got, from_first, done_f1)
    f0_r.spare(1)
    f0_r.start()
    input_grads = jnp.where(first, jnp.concatenate([d_first, from_first]), jnp.concatenate([from_second, d_second]))
    a0_r.got, a1_r.got, input_grads = order.wait(a0_r.got, a1_r.got, input_grads)
    a0_r.spare(1)
    a0_r.start()
    done_a1 = a1_r.finish()
    f0_r.got, done_a1 = order.wait(f0_r.got, done_a1)
    done_f0 = f0_r.finish()

    def unite(zero_part, one_part):
        got = swap(jnp.where(first, one_part, zero_part))
        return jnp.where(first, zero_part, got), jnp.where(first, got, one_part)

    up_plane, down_plane = unite(done_f0, done_f1)
    a0_r.got, up_plane, down_plane = order.wait(a0_r.got, up_plane, down_plane)
    done_a0 = a0_r.finish()
    low_plane, high_plane = unite(done_a0[:cut], done_a1)

    def unit(array, j):
        return array[j * size : (j + 1) * size]

    qkv_grad = jnp.concatenate([unit(low_plane, 0), unit(low_plane, 1), unit(high_plane, 0)], axis=1)
    out_grad = unit(high_plane, 1)
    up_grad = jnp.concatenate([unit(up_plane, j) for j in range(units)], axis=1)
    down_grad = down_plane
    tail = done_a0[cut:]
    if is_small(count):
        gain_grad = tail[None, :2, :size]
        shift_grad = tail[None, 2:8, :size]
        cup_grad = tail[8:9, : up_b.shape[1]]
        head_grad = jnp.concatenate([tail[:8, 384 + 128 * k : 512 + 128 * k] for k in range(3)])
    else:
        flat = tail[:small_rows].reshape(-1)[:small_n]
        gain_grad = flat[:n_g].reshape(gains_w.shape)
        shift_grad = flat[n_g : n_g + n_s].reshape(shifts_w.shape)
        cup_grad = flat[n_g + n_s :].reshape(up_b.shape)
        head_grad = tail[small_rows : small_rows + head_rows].reshape(-1)[:head_n].reshape(head_w.shape)

    return (
        qkv_grad[None],
        out_grad[None],
        up_grad[None],
        down_grad[None],
        gain_grad,
        shift_grad,
        cup_grad,
        head_grad,
        input_grads[None],
    )


def solution(mesh):
    return jax.shard_map(
        shards,
        mesh=mesh,
        in_specs=(
            P("dp", None, None),
            P("dp", None),
            P("dp", None, None),
            P("section", "dp", None),
            P("section", "dp", None),
            P("section", "dp", None),
            P("section", "dp", None),
            P("section", None, "dp"),
            P("section", None, "dp"),
            P("section", "dp"),
            P(("section", "dp"), None),
        ),
        out_specs=(
            P("section", "dp", None),
            P("section", "dp", None),
            P("section", "dp", None),
            P("section", "dp", None),
            P("section", None, "dp"),
            P("section", None, "dp"),
            P("section", "dp"),
            P(("section", "dp"), None),
            P("section", "dp", None, None),
        ),
        check_vma=False,
    )
```
